256 devices in a mesh: node: 16 (over z_lo, y), rep: 16 (over x, z_hi, core).
Axes of the slice: x: 4, y: 4, z: 8 (z_hi: 2, z_lo: 4; z = z_hi * 4 + z_lo), core: 2. Of those that a mesh axis runs over, the one named last changes fastest.
Arguments:
- tokens: bfloat16 [32768, 8192], P(('node', 'rep')), may hold values from -24 to 24
- norm_gain: float32 [8192], replicated, may hold values from 0.5 to 1.5
- key_cotangent: bfloat16 [32768, 512], P(('node', 'rep')), may hold values from -6 to 6
- secondary: bfloat16 [8192, 512], P('node'), may hold values from -0.0625 to 0.0625
- master: float32 [8192, 512], P(('node', 'rep')), may hold values from -0.0625 to 0.0625
- moment_first: float32 [4096, 1024], P(('node', 'rep')), may hold values from -0.03314563 to 0.03314563
- moment_second: float32 [4096, 1024], P(('node', 'rep')), may hold values from 7.6293945e-06 to 0.00012207031
- signs: int32 [1024], replicated, may hold values from 0 to 1
Outputs:
- keys: bfloat16 [32768, 512], P(('node', 'rep'))
- token_grad: bfloat16 [32768, 8192], P(('node', 'rep'))
- new_master: float32 [8192, 512], P(('node', 'rep'))
- new_first: float32 [4096, 1024], P(('node', 'rep'))
- new_second: float32 [4096, 1024], P(('node', 'rep'))
- new_secondary: bfloat16 [8192, 512], P('node')
The draws below stay inside these ranges and needn't reach their ends.
All inputs are finite; a program needn't handle non-finite values.
Results may differ from the reference program's by a relative error of at most 0.0049.
Values may be sent and summed in bfloat16 or wider, within the bound.
No kernel may reach another device: no remote copies, remote signals or barrier semaphores. Data moves between devices by JAX's collectives and lax.ppermute only.
A program may use at most 128 MiB of HBM per device.

```python
import math
import jax
import jax.numpy as jnp
from jax import lax

D = 8192
KV = 512
TOK_DEV = 128
PAIR_GAP = 16
TOKENS = 32768
N_NODE = 16
N_REP = 16


def with_ends(entries, own_key, low, high):
    longest = entries.shape.index(max(entries.shape))
    spots = []
    for shift in (0, 1):
        where = [jax.random.randint(jax.random.fold_in(own_key, axis), (), 0, length) for axis, length in enumerate(entries.shape)]
        where[longest] = (where[longest] + shift) % entries.shape[longest]
        spots.append(tuple(where))
    return entries.at[spots[0]].set(low).at[spots[1]].set(high)


def strengthened(drawn, key, source, target, blocks, factor):
    def block_of(dim):
        return (jnp.arange(drawn.shape[dim]) // (drawn.shape[dim] // blocks)).reshape((-1,) + (1,) * (drawn.ndim - 1 - dim))

    near = jax.random.permutation(key, blocks)[block_of(target)]
    second = (block_of(target) + blocks // 2) % blocks
    return jnp.where((block_of(source) == near) | (block_of(source) == second), factor * drawn, drawn)


def block_scale(key, dims, split, low, largest):
    gain = 1.0
    for axis_at, blocks in split:
        draws = jax.random.uniform(jax.random.fold_in(jax.random.fold_in(key, 6), axis_at), (blocks,), jnp.float32, low / len(split), largest / len(split))
        gain = gain * jnp.repeat(jnp.exp(draws), dims[axis_at] // blocks).reshape((-1,) + (1,) * (len(dims) - 1 - axis_at))
    return gain


def normal_values(own_key, dims, deviation, limit, pieces=(), kind=jnp.bfloat16):
    drawn = deviation * jax.random.normal(own_key, dims, jnp.float32)
    if pieces:
        drawn = drawn * block_scale(own_key, dims, pieces, -0.22, 0.18)
    return jnp.clip(drawn, -limit, limit).astype(kind)


def heavy_noise(key, shape, deviation, bound, shards, heavy, kind=jnp.bfloat16):
    array = deviation * jax.random.normal(key, shape, jnp.float32)
    if shards:
        array = array * block_scale(key, shape, shards, -0.22, 0.18)
    return jnp.clip(strengthened(array, jax.random.fold_in(key, 3), *heavy), -bound, bound).astype(kind)


def setup_inputs(seed: int = 0) -> dict:
    key_of = jax.random.split(jax.random.key(seed), 9)
    tokens = heavy_noise(key_of[0], (TOKENS, D), 1.0, 24.0, ((0, 256),), (0, 1, 256, 6.0))
    norm_gain = jnp.clip(1.0 + 0.1 * jax.random.normal(key_of[1], (D,), jnp.float32), 0.5, 1.5)
    key_cotangent = normal_values(key_of[2], (TOKENS, KV), 1.0, 6.0, ((0, 256),))
    secondary = normal_values(key_of[3], (D, KV), D ** -0.5, 0.0625, ((0, 16),))
    master = normal_values(key_of[4], (D, KV), D ** -0.5, 0.0625, ((0, 256),), jnp.float32)
    moment_first = normal_values(key_of[5], (D // 2, 2 * KV), (1.0 / (TOK_DEV * N_NODE * N_REP) ** 0.5), 0.03314563, ((0, 256),), jnp.float32)
    moment_second = jnp.clip(jnp.exp(math.log(0.00012207031) - 2.7725887 * jax.random.uniform(key_of[6], (D // 2, 2 * KV), jnp.float32) ** block_scale(key_of[6], (D // 2, 2 * KV), ((0, 256),), -0.2, 0.2)), 7.62939453125e-06, 0.00012207031)
    signs = with_ends(jax.random.randint(key_of[7], (2 * KV,), 0, 2), jax.random.fold_in(key_of[7], 1), 0, 1).astype(jnp.int32)
    return dict(tokens=tokens, norm_gain=norm_gain, key_cotangent=key_cotangent, secondary=secondary, master=master, moment_first=moment_first, moment_second=moment_second, signs=signs)


norm_eps = 1e-05
adam_eps = 1e-08
beta_first = 0.9
beta_second = 0.95
adam_steps = 10
learn_rate = 0.002
weight_decay = 0.1

def sylvester(extent):
    position = jnp.arange(extent, dtype=jnp.int32)
    parity = jnp.zeros((extent, extent), jnp.int32)
    for bit_place in range(extent.bit_length() - 1):
        parity = parity + (position[:, None] >> bit_place & 1) * (position[None, :] >> bit_place & 1)
    return (1 - 2 * (parity % 2)).astype(jnp.float32)

def reference(tokens, norm_gain, key_cotangent, secondary, master, moment_first, moment_second, signs):
    devices = N_NODE * N_REP
    had_table = sylvester(KV)
    sign_rows = (1 - 2 * signs).astype(jnp.float32).reshape(2, KV)
    rot_scale = 1.0 / (math.sqrt(2 * KV) * TOK_DEV * devices)
    token_blocks = tokens.reshape(devices, TOK_DEV, D)
    cot_blocks = key_cotangent.reshape(devices, TOK_DEV, KV)

    def device_step(running, block):
        activations, cotangent = block
        floats = activations.astype(jnp.float32)
        inverse = lax.rsqrt(lax.optimization_barrier(jnp.mean(floats * floats, axis=-1, keepdims=True)) + norm_eps)
        normed = floats * inverse
        hidden = (normed * norm_gain).astype(jnp.bfloat16)
        keys = jnp.dot(hidden, secondary, preferred_element_type=jnp.float32).astype(jnp.bfloat16)
        hidden_grad = jnp.dot(cotangent, secondary.T, preferred_element_type=jnp.float32)
        scaled = hidden_grad * norm_gain
        token_grad = (inverse * (scaled - normed * lax.optimization_barrier(jnp.mean(scaled * normed, axis=-1, keepdims=True)))).astype(jnp.bfloat16)
        flipped = cotangent.astype(jnp.float32)[:, None, :] * sign_rows
        rotated = (jnp.einsum('tak,kl->tal', flipped, had_table, precision=lax.Precision.HIGHEST) * rot_scale).astype(jnp.bfloat16)
        grouped = hidden.reshape(TOK_DEV, D // (2 * PAIR_GAP), 2, PAIR_GAP).astype(jnp.float32)
        halves = jnp.einsum('tgaj,tak->agjk', grouped, rotated.astype(jnp.float32), precision=lax.Precision.HIGHEST)
        term = jnp.concatenate([halves[0] + halves[1], halves[0] - halves[1]], axis=-1).reshape(D // 2, 2 * KV)
        coded_term = lax.optimization_barrier(term.astype(jnp.bfloat16)).astype(jnp.float32)
        return (running + coded_term, (keys, token_grad))
    start_sum = jnp.zeros((D // 2, 2 * KV), jnp.float32)
    coded, (all_keys, all_grads) = lax.scan(device_step, start_sum, (token_blocks, cot_blocks))
    new_first = beta_first * moment_first + (1.0 - beta_first) * coded
    new_second = beta_second * moment_second + (1.0 - beta_second) * coded * coded
    first_hat = new_first / (1.0 - beta_first ** adam_steps)
    second_hat = new_second / (1.0 - beta_second ** adam_steps)
    ratio = first_hat / (jnp.sqrt(second_hat) + adam_eps)
    lower = ratio[:, :KV]
    upper = ratio[:, KV:]
    norm_root = math.sqrt(2 * KV)
    row_even = jnp.dot(lower + upper, had_table, precision=lax.Precision.HIGHEST) / norm_root * sign_rows[0]
    row_odd = jnp.dot(lower - upper, had_table, precision=lax.Precision.HIGHEST) / norm_root * sign_rows[1]
    stacked = jnp.stack([row_even, row_odd], axis=1)
    update = stacked.reshape(D // (2 * PAIR_GAP), PAIR_GAP, 2, KV).transpose(0, 2, 1, 3).reshape(D, KV)
    new_master = master - learn_rate * (update + weight_decay * master)
    keys_out = all_keys.reshape(devices * TOK_DEV, KV)
    grads_out = all_grads.reshape(devices * TOK_DEV, D)
    return (keys_out, grads_out, new_master, new_first, new_second, new_master.astype(jnp.bfloat16))
```

```python
import functools
import math

import jax
import jax.numpy as jnp
from jax import lax
from jax.experimental import pallas as pl
from jax.experimental.pallas import tpu as pltpu
from jax.sharding import Mesh
from jax.sharding import PartitionSpec as P

PAIR_GAP = 16
norm_eps = 1e-05
adam_eps = 1e-08
beta_first = 0.9
beta_second = 0.95
adam_steps = 10
learn_rate = 0.002
weight_decay = 0.1

AXES = ("zl", "y", "x", "zh", "c")
SIZES = (4, 4, 4, 2, 2)
ZL, Y, X, ZH, C = SIZES
ROWS = 32
VMEM = pl.BlockSpec(memory_space=pltpu.VMEM)
BF16 = jnp.bfloat16
F32 = jnp.float32


def shape(dims, kind):
    return jax.ShapeDtypeStruct(dims, kind)


def kernel_call(body, outs, flops, nbytes, n_in):
    return pl.pallas_call(
        body,
        out_shape=outs,
        in_specs=[VMEM] * n_in,
        out_specs=jax.tree.map(lambda _: VMEM, outs),
        cost_estimate=pl.CostEstimate(flops=flops, bytes_accessed=nbytes, transcendentals=0),
        compiler_params=pltpu.CompilerParams(vmem_limit_bytes=56 << 20),
    )


def norm_kernel(tok_ref, gain_ref, cot_ref, send_ref, inv_ref):
    rows, width = tok_ref.shape
    step = X * ZH * C * ROWS
    acc = jnp.zeros((rows, step), F32)
    for k in range(width // step):
        t = tok_ref[:, k * step : (k + 1) * step].astype(F32)
        acc = acc + t * t
    inv = lax.rsqrt(jnp.sum(acc, axis=-1, keepdims=True) / width + norm_eps)
    inv = jnp.broadcast_to(inv, inv_ref.shape)
    inv_ref[...] = inv
    part = ZH * C * ROWS
    for n in range(ZL * Y):
        for x in range(X):
            cols = slice(n * step + x * part, n * step + (x + 1) * part)
            normed = tok_ref[:, cols].astype(F32) * inv
            send_ref[x, :, n * part : (n + 1) * part] = (normed * gain_ref[:, cols]).astype(BF16)
    for x in range(X):
        send_ref[x, :, ZL * Y * part :] = cot_ref[...]


def grad_kernel(recv_ref, own_ref, sib_ref):
    c = lax.axis_index("c")
    part = ZH * C * ROWS
    cols = ZL * Y * part
    cot = recv_ref[:, cols:]
    for zl in range(ZL):
        block = recv_ref[:, zl * Y * part : (zl + 1) * Y * part]
        grad = lax.dot_general(block, cot, (((0,), (0,)), ((), ())), preferred_element_type=F32)
        for y in range(Y):
            for zh in range(ZH):
                at = y * part + zh * C * ROWS
                first, second = grad[at : at + ROWS], grad[at + ROWS : at + 2 * ROWS]
                to = ((y * ZL + zl) * ZH + zh) * ROWS
                own_ref[to : to + ROWS, :] = jnp.where(c == 0, first, second)
                sib_ref[to : to + ROWS, :] = jnp.where(c == 0, second, first).astype(BF16)


def out_kernel(tok_ref, gain_ref, cot_ref, inv_ref, *refs):
    w_refs, (keys_ref, tg_ref) = refs[:-2], refs[-2:]
    c, zl = lax.axis_index("c"), lax.axis_index("zl")
    rows, width = tok_ref.shape
    step = width // (ZL * Y)
    half = step // 2
    inv = jnp.concatenate([inv_ref[...]] * (half // inv_ref.shape[1]), axis=1)
    cot = cot_ref[...]

    def places():
        for s, off in enumerate((0, 1, 3, 2)):
            for h in range(2):
                for y in range(Y):
                    node = lax.rem(zl + off, ZL) * Y + y
                    core = c if h == 0 else 1 - c
                    at = pl.multiple_of(node * step + core * half, half)
                    yield pl.ds(at, half), w_refs[2 * s + h], slice(y * half, (y + 1) * half)

    keys = jnp.zeros(keys_ref.shape, F32)
    for cols, w_ref, wrows in places():
        normed = tok_ref[:, cols].astype(F32) * inv
        hidden = (normed * gain_ref[:, cols]).astype(BF16)
        keys = keys + jnp.dot(hidden, w_ref[wrows, :], preferred_element_type=F32)
    keys_ref[...] = keys.astype(BF16)
    mean = jnp.sum(cot.astype(F32) * keys, axis=-1, keepdims=True) / width
    for cols, w_ref, wrows in places():
        hidden_grad = lax.dot_general(
            cot, w_ref[wrows, :], (((1,), (1,)), ((), ())), preferred_element_type=F32
        )
        normed = tok_ref[:, cols].astype(F32) * inv
        tg_ref[:, cols] = (inv * (hidden_grad * gain_ref[:, cols] - normed * mean)).astype(BF16)


def hadamard(value, extent=128):
    rows, width = value.shape
    i = lax.broadcasted_iota(jnp.int32, (extent, extent), 0)
    j = lax.broadcasted_iota(jnp.int32, (extent, extent), 1)
    both = i & j
    both = both ^ (both >> 4)
    both = both ^ (both >> 2)
    both = both ^ (both >> 1)
    table = (1 - 2 * (both & 1)).astype(F32).astype(BF16)
    parts = []
    for k in range(width // extent):
        rest = value[:, k * extent : (k + 1) * extent]
        for _ in range(3):
            top = rest.astype(BF16)
            parts.append(top)
            rest = rest - top.astype(F32)
    out = jnp.dot(jnp.concatenate(parts, axis=0), table, preferred_element_type=F32)
    p = []
    for k in range(width // extent):
        at = 3 * k * rows
        p.append((out[at + 2 * rows : at + 3 * rows] + out[at + rows : at + 2 * rows]) + out[at : at + rows])
    s, t, u, v = p[0] + p[1], p[0] - p[1], p[2] + p[3], p[2] - p[3]
    return jnp.concatenate([s + u, t + v, s - u, t - v], axis=1)


def adam_kernel(tokens_all, recv_ref, first_ref, second_ref, master_ref, signs_ref, nm_ref, nf_ref, ns_ref, new_ref):
    total = jnp.sum(recv_ref[...].astype(F32), axis=0)
    half = total.shape[1]
    root = math.sqrt(2 * half)
    sign = (1 - 2 * signs_ref[...]).astype(F32)
    sign0, sign1 = sign[:, :half], sign[:, half:]
    gap = PAIR_GAP
    spun = hadamard(jnp.concatenate([total[:gap] * sign0, total[gap:] * sign1], axis=0)) * (1.0 / (root * tokens_all))
    q0, q1 = spun[:gap], spun[gap:]
    coded = jnp.concatenate([q0 + q1, q0 - q1], axis=1)
    new_first = beta_first * first_ref[...] + (1.0 - beta_first) * coded
    new_second = beta_second * second_ref[...] + (1.0 - beta_second) * coded * coded
    nf_ref[...] = new_first
    ns_ref[...] = new_second
    first_hat = new_first / (1.0 - beta_first**adam_steps)
    second_hat = new_second / (1.0 - beta_second**adam_steps)
    ratio = first_hat / (jnp.sqrt(second_hat) + adam_eps)
    lower, upper = ratio[:, :half], ratio[:, half:]
    back = hadamard(jnp.concatenate([lower + upper, lower - upper], axis=0)) / root
    update = jnp.concatenate([back[:gap] * sign0, back[gap:] * sign1], axis=0)
    master = master_ref[...]
    new_master = master - learn_rate * (update + weight_decay * master)
    nm_ref[...] = new_master
    new_ref[...] = new_master.astype(BF16)


def ring(n, s):
    return [(i, (i + s) % n) for i in range(n)]


def along_z(shift):
    pairs = []
    for zl in range(ZL):
        for zh in range(ZH):
            for c in range(C):
                z = (zh * ZL + zl + shift(c)) % (ZH * ZL)
                pairs.append(((zl * ZH + zh) * C + c, ((z % ZL) * ZH + z // ZL) * C + c))
    return pairs


def to_all(value, axes, n):
    copies = jnp.broadcast_to(value, (n, *value.shape))
    return lax.all_to_all(copies, axes, 0, 0, tiled=True)


def shards(tokens, norm_gain, key_cotangent, secondary, master, moment_first, moment_second, signs):
    tok_rows, width = tokens.shape
    keys_w = key_cotangent.shape[1]
    c = lax.axis_index("c")
    gain = norm_gain.reshape(1, width)
    node_rows = secondary.shape[0]

    half = lax.dynamic_slice_in_dim(secondary, c * (node_rows // 2), node_rows // 2, 0)
    column = to_all(half, "y", Y).reshape(Y * node_rows // 2, keys_w)
    z_axes = ("zl", "zh", "c")
    from_up = lax.ppermute(column, z_axes, along_z(lambda c: -1))
    from_down = lax.ppermute(column, z_axes, along_z(lambda c: 1))
    from_far = lax.ppermute(column, z_axes, along_z(lambda c: 2 - 4 * c))
    weights = []
    for block in (column, from_up, from_down, from_far):
        weights += [block, lax.ppermute(block, "c", ring(C, 1))]

    part = width // X
    send, inv = kernel_call(
        norm_kernel,
        (shape((X, tok_rows, part + keys_w), BF16), shape((tok_rows, 128), F32)),
        tok_rows * width * 6,
        5 << 20,
        3,
    )(tokens, gain, key_cotangent)
    recv = lax.all_to_all(send, "x", 0, 0, tiled=True).reshape(X * tok_rows, part + keys_w)
    own, sib = kernel_call(
        grad_kernel,
        (shape((part // 2, keys_w), F32), shape((part // 2, keys_w), BF16)),
        2 * X * tok_rows * part * keys_w,
        6 << 20,
        1,
    )(recv)
    sib = lax.ppermute(sib, "c", ring(C, 1))
    summed = (own + sib.astype(F32)).astype(BF16)
    blocks = lax.all_to_all(summed.reshape(Y, -1, keys_w), "y", 0, 0, tiled=True)
    summed = jnp.sum(blocks.astype(F32), axis=0).astype(BF16)
    blocks = lax.all_to_all(summed.reshape(ZL * ZH, ROWS, keys_w), ("zl", "zh"), 0, 0, tiled=True)
    new_master, new_first, new_second, new_rows = kernel_call(
        functools.partial(adam_kernel, tok_rows * math.prod(SIZES)),
        (
            shape(master.shape, F32),
            shape(moment_first.shape, F32),
            shape(moment_second.shape, F32),
            shape(master.shape, BF16),
        ),
        1 << 25,
        1 << 20,
        5,
    )(blocks, moment_first, moment_second, master, signs.reshape(1, -1))

    mine = to_all(new_rows, ("x", "zh"), X * ZH)
    other = lax.ppermute(mine, "c", ring(C, 1))
    even = jnp.where(c == 0, mine, other)
    odd = jnp.where(c == 0, other, mine)
    new_secondary = jnp.stack([even, odd], axis=1).reshape(node_rows, keys_w)

    keys, token_grad = kernel_call(
        out_kernel,
        (shape((tok_rows, keys_w), BF16), shape(tokens.shape, BF16)),
        4 * tok_rows * width * keys_w,
        14 << 20,
        4 + len(weights),
    )(tokens, gain, key_cotangent, inv, *weights)
    return (keys, token_grad, new_master, new_first, new_second, new_secondary)


def solution(mesh):
    fine = Mesh(mesh.devices.reshape(SIZES), AXES)
    split = P(AXES, None)
    return jax.shard_map(
        shards,
        mesh=fine,
        in_specs=(split, P(), split, P(("zl", "y"), None), split, split, split, P()),
        out_specs=(split, split, split, split, split, P(("zl", "y"), None)),
        check_vma=False,
    )
```

```python
import functools
import math

import jax
import jax.numpy as jnp
from jax import lax
from jax.experimental import pallas as pl
from jax.experimental.pallas import tpu as pltpu
from jax.sharding import Mesh
from jax.sharding import PartitionSpec as P

PAIR_GAP = 16
norm_eps = 1e-05
adam_eps = 1e-08
beta_first = 0.9
beta_second = 0.95
adam_steps = 10
learn_rate = 0.002
weight_decay = 0.1

AXES = ("zl", "y", "x", "zh", "c")
SIZES = (4, 4, 4, 2, 2)
ZL, Y, X, ZH, C = SIZES
ROWS = 32
VMEM = pl.BlockSpec(memory_space=pltpu.VMEM)
BF16 = jnp.bfloat16
F32 = jnp.float32


def shape(dims, kind):
    return jax.ShapeDtypeStruct(dims, kind)


def kernel_call(body, outs, flops, nbytes, n_in):
    return pl.pallas_call(
        body,
        out_shape=outs,
        in_specs=[VMEM] * n_in,
        out_specs=jax.tree.map(lambda _: VMEM, outs),
        cost_estimate=pl.CostEstimate(flops=flops, bytes_accessed=nbytes, transcendentals=0),
        compiler_params=pltpu.CompilerParams(vmem_limit_bytes=56 << 20),
    )


def norm_kernel(tok_ref, gain_ref, cot_ref, send_ref, inv_ref):
    rows, width = tok_ref.shape
    step = X * ZH * C * ROWS
    acc = jnp.zeros((rows, step), F32)
    for k in range(width // step):
        t = tok_ref[:, k * step : (k + 1) * step].astype(F32)
        acc = acc + t * t
    inv = lax.rsqrt(jnp.sum(acc, axis=-1, keepdims=True) / width + norm_eps)
    inv = jnp.broadcast_to(inv, inv_ref.shape)
    inv_ref[...] = inv
    part = ZH * C * ROWS
    for n in range(ZL * Y):
        for x in range(X):
            cols = slice(n * step + x * part, n * step + (x + 1) * part)
            normed = tok_ref[:, cols].astype(F32) * inv
            send_ref[x, :, n * part : (n + 1) * part] = (normed * gain_ref[:, cols]).astype(BF16)
    for x in range(X):
        send_ref[x, :, ZL * Y * part :] = cot_ref[...]


def grad_kernel(recv_ref, own_ref, sib_ref):
    c = lax.axis_index("c")
    part = ZH * C * ROWS
    cols = ZL * Y * part
    cot = recv_ref[:, cols:]
    for zl in range(ZL):
        block = recv_ref[:, zl * Y * part : (zl + 1) * Y * part]
        grad = lax.dot_general(block, cot, (((0,), (0,)), ((), ())), preferred_element_type=F32)
        for y in range(Y):
            for zh in range(ZH):
                at = y * part + zh * C * ROWS
                first, second = grad[at : at + ROWS], grad[at + ROWS : at + 2 * ROWS]
                to = ((y * ZL + zl) * ZH + zh) * ROWS
                own_ref[to : to + ROWS, :] = jnp.where(c == 0, first, second)
                sib_ref[to : to + ROWS, :] = jnp.where(c == 0, second, first).astype(BF16)


def out_kernel(tok_ref, gain_ref, cot_ref, inv_ref, *refs):
    w_refs, (keys_ref, tg_ref) = refs[:-2], refs[-2:]
    c, zl, y = (lax.axis_index(name) for name in ("c", "zl", "y"))
    rows, width = tok_ref.shape
    step = width // (ZL * Y)
    half = step // 2
    inv = jnp.concatenate([inv_ref[...]] * (half // inv_ref.shape[1]), axis=1)
    cot = cot_ref[...]

    def places():
        for s, off in enumerate((0, 1, 3, 2)):
            for h in range(2):
                for k in range(Y):
                    node = lax.rem(zl + off, ZL) * Y + lax.rem(y + k, Y)
                    core = c if h == 0 else 1 - c
                    at = pl.multiple_of(node * step + core * half, half)
                    yield pl.ds(at, half), w_refs[2 * s + h], slice(k * half, (k + 1) * half)

    keys = jnp.zeros(keys_ref.shape, F32)
    for cols, w_ref, wrows in places():
        normed = tok_ref[:, cols].astype(F32) * inv
        hidden = (normed * gain_ref[:, cols]).astype(BF16)
        keys = keys + jnp.dot(hidden, w_ref[wrows, :], preferred_element_type=F32)
    keys_ref[...] = keys.astype(BF16)
    mean = jnp.sum(cot.astype(F32) * keys, axis=-1, keepdims=True) / width
    for cols, w_ref, wrows in places():
        hidden_grad = lax.dot_general(
            cot, w_ref[wrows, :], (((1,), (1,)), ((), ())), preferred_element_type=F32
        )
        normed = tok_ref[:, cols].astype(F32) * inv
        tg_ref[:, cols] = (inv * (hidden_grad * gain_ref[:, cols] - normed * mean)).astype(BF16)


def hadamard(value, extent=128):
    rows, width = value.shape
    i = lax.broadcasted_iota(jnp.int32, (extent, extent), 0)
    j = lax.broadcasted_iota(jnp.int32, (extent, extent), 1)
    both = i & j
    both = both ^ (both >> 4)
    both = both ^ (both >> 2)
    both = both ^ (both >> 1)
    table = (1 - 2 * (both & 1)).astype(F32).astype(BF16)
    parts = []
    for k in range(width // extent):
        rest = value[:, k * extent : (k + 1) * extent]
        for _ in range(3):
            top = rest.astype(BF16)
            parts.append(top)
            rest = rest - top.astype(F32)
    out = jnp.dot(jnp.concatenate(parts, axis=0), table, preferred_element_type=F32)
    p = []
    for k in range(width // extent):
        at = 3 * k * rows
        p.append((out[at + 2 * rows : at + 3 * rows] + out[at + rows : at + 2 * rows]) + out[at : at + rows])
    s, t, u, v = p[0] + p[1], p[0] - p[1], p[2] + p[3], p[2] - p[3]
    return jnp.concatenate([s + u, t + v, s - u, t - v], axis=1)


def adam_kernel(tokens_all, recv_ref, first_ref, second_ref, master_ref, signs_ref, nm_ref, nf_ref, ns_ref, new_ref):
    total = jnp.sum(recv_ref[...].astype(F32), axis=0)
    half = total.shape[1]
    root = math.sqrt(2 * half)
    sign = (1 - 2 * signs_ref[...]).astype(F32)
    sign0, sign1 = sign[:, :half], sign[:, half:]
    gap = PAIR_GAP
    spun = hadamard(jnp.concatenate([total[:gap] * sign0, total[gap:] * sign1], axis=0)) * (1.0 / (root * tokens_all))
    q0, q1 = spun[:gap], spun[gap:]
    coded = jnp.concatenate([q0 + q1, q0 - q1], axis=1)
    new_first = beta_first * first_ref[...] + (1.0 - beta_first) * coded
    new_second = beta_second * second_ref[...] + (1.0 - beta_second) * coded * coded
    nf_ref[...] = new_first
    ns_ref[...] = new_second
    first_hat = new_first / (1.0 - beta_first**adam_steps)
    second_hat = new_second / (1.0 - beta_second**adam_steps)
    ratio = first_hat / (jnp.sqrt(second_hat) + adam_eps)
    lower, upper = ratio[:, :half], ratio[:, half:]
    back = hadamard(jnp.concatenate([lower + upper, lower - upper], axis=0)) / root
    update = jnp.concatenate([back[:gap] * sign0, back[gap:] * sign1], axis=0)
    master = master_ref[...]
    new_master = master - learn_rate * (update + weight_decay * master)
    nm_ref[...] = new_master
    new_ref[...] = new_master.astype(BF16)


def ring(n, s):
    return [(i, (i + s) % n) for i in range(n)]


def along_z(shift):
    pairs = []
    for zl in range(ZL):
        for zh in range(ZH):
            for c in range(C):
                z = (zh * ZL + zl + shift(c)) % (ZH * ZL)
                pairs.append(((zl * ZH + zh) * C + c, ((z % ZL) * ZH + z // ZL) * C + c))
    return pairs


def to_all(value, axes, n):
    copies = jnp.broadcast_to(value, (n, *value.shape))
    return lax.all_to_all(copies, axes, 0, 0, tiled=True)


def shards(tokens, norm_gain, key_cotangent, secondary, master, moment_first, moment_second, signs):
    tok_rows, width = tokens.shape
    keys_w = key_cotangent.shape[1]
    c = lax.axis_index("c")
    gain = norm_gain.reshape(1, width)
    node_rows = secondary.shape[0]

    half = lax.dynamic_slice_in_dim(secondary, c * (node_rows // 2), node_rows // 2, 0)
    column = [half] + [lax.ppermute(half, "y", ring(Y, -k)) for k in range(1, Y)]
    column = jnp.concatenate(column, axis=0)
    z_axes = ("zl", "zh", "c")
    from_up = lax.ppermute(column, z_axes, along_z(lambda c: -1))
    from_down = lax.ppermute(column, z_axes, along_z(lambda c: 1))

    part = width // X
    send, inv = kernel_call(
        norm_kernel,
        (shape((X, tok_rows, part + keys_w), BF16), shape((tok_rows, 128), F32)),
        tok_rows * width * 6,
        5 << 20,
        3,
    )(tokens, gain, key_cotangent)
    recv = lax.all_to_all(send, "x", 0, 0, tiled=True).reshape(X * tok_rows, part + keys_w)
    recv, _ = lax.optimization_barrier((recv, column))
    own, sib = kernel_call(
        grad_kernel,
        (shape((part // 2, keys_w), F32), shape((part // 2, keys_w), BF16)),
        0,
        1 << 20,
        1,
    )(recv)
    sib, column, from_up, from_down = lax.optimization_barrier((sib, column, from_up, from_down))
    sib = lax.ppermute(sib, "c", ring(C, 1))
    summed = (own + sib.astype(F32)).astype(BF16)
    summed, column, from_up, from_down = lax.optimization_barrier((summed, column, from_up, from_down))
    from_far = lax.ppermute(column, z_axes, along_z(lambda c: 2 - 4 * c))
    weights = []
    for block in (column, from_up, from_down):
        weights += [block, lax.ppermute(block, "c", ring(C, 1))]
    blocks = lax.all_to_all(summed.reshape(Y, -1, keys_w), "y", 0, 0, tiled=True)
    summed = jnp.sum(blocks.astype(F32), axis=0).astype(BF16)
    blocks = lax.all_to_all(summed.reshape(ZL * ZH, ROWS, keys_w), ("zl", "zh"), 0, 0, tiled=True)
    blocks, from_far = lax.optimization_barrier((blocks, from_far))
    weights += [from_far, lax.ppermute(from_far, "c", ring(C, 1))]
    new_master, new_first, new_second, new_rows = kernel_call(
        functools.partial(adam_kernel, tok_rows * math.prod(SIZES)),
        (
            shape(master.shape, F32),
            shape(moment_first.shape, F32),
            shape(moment_second.shape, F32),
            shape(master.shape, BF16),
        ),
        1 << 25,
        1 << 20,
        5,
    )(blocks, moment_first, moment_second, master, signs.reshape(1, -1))
    new_rows, inv = lax.optimization_barrier((new_rows, inv))

    mine = to_all(new_rows, ("x", "zh"), X * ZH)
    keys, token_grad = kernel_call(
        out_kernel,
        (shape((tok_rows, keys_w), BF16), shape(tokens.shape, BF16)),
        4 * tok_rows * width * keys_w,
        14 << 20,
        4 + len(weights),
    )(tokens, gain, key_cotangent, inv, *weights)
    mine, keys, token_grad = lax.optimization_barrier((mine, keys, token_grad))
    other = lax.ppermute(mine, "c", ring(C, 1))
    even = jnp.where(c == 0, mine, other)
    odd = jnp.where(c == 0, other, mine)
    new_secondary = jnp.stack([even, odd], axis=1).reshape(node_rows, keys_w)
    return (keys, token_grad, new_master, new_first, new_second, new_secondary)


def solution(mesh):
    fine = Mesh(mesh.devices.reshape(SIZES), AXES)
    split = P(AXES, None)
    return jax.shard_map(
        shards,
        mesh=fine,
        in_specs=(split, P(), split, P(("zl", "y"), None), split, split, split, P()),
        out_specs=(split, split, split, split, split, P(("zl", "y"), None)),
        check_vma=False,
    )
```

```python
import functools
import math

import jax
import jax.numpy as jnp
from jax import lax
from jax.experimental import pallas as pl
from jax.experimental.pallas import tpu as pltpu
from jax.sharding import Mesh
from jax.sharding import PartitionSpec as P

PAIR_GAP = 16
norm_eps = 1e-05
adam_eps = 1e-08
beta_first = 0.9
beta_second = 0.95
adam_steps = 10
learn_rate = 0.002
weight_decay = 0.1

AXES = ("zl", "y", "x", "zh", "c")
SIZES = (4, 4, 4, 2, 2)
ZL, Y, X, ZH, C = SIZES
ROWS = 32
VMEM = pl.BlockSpec(memory_space=pltpu.VMEM)
BF16 = jnp.bfloat16
F32 = jnp.float32


def shape(dims, kind):
    return jax.ShapeDtypeStruct(dims, kind)


def kernel_call(body, outs, flops, nbytes, n_in, limit=24 << 20):
    return pl.pallas_call(
        body,
        out_shape=outs,
        in_specs=[VMEM] * n_in,
        out_specs=jax.tree.map(lambda _: VMEM, outs),
        cost_estimate=pl.CostEstimate(flops=flops, bytes_accessed=nbytes, transcendentals=0),
        compiler_params=pltpu.CompilerParams(vmem_limit_bytes=limit),
    )


def norm_kernel(tok_ref, gain_ref, cot_ref, send_ref, inv_ref):
    rows, width = tok_ref.shape
    step = X * ZH * C * ROWS
    acc = jnp.zeros((rows, step), F32)
    for k in range(width // step):
        t = tok_ref[:, k * step : (k + 1) * step].astype(F32)
        acc = acc + t * t
    inv = lax.rsqrt(jnp.sum(acc, axis=-1, keepdims=True) / width + norm_eps)
    inv = jnp.broadcast_to(inv, inv_ref.shape)
    inv_ref[...] = inv
    part = ZH * C * ROWS
    for n in range(ZL * Y):
        for x in range(X):
            cols = slice(n * step + x * part, n * step + (x + 1) * part)
            normed = tok_ref[:, cols].astype(F32) * inv
            send_ref[x, :, n * part : (n + 1) * part] = (normed * gain_ref[:, cols]).astype(BF16)
    for x in range(X):
        send_ref[x, :, ZL * Y * part :] = cot_ref[...]


def grad_kernel(recv_ref, own_ref, sib_a_ref, sib_b_ref):
    c = lax.axis_index("c")
    part = ZH * C * ROWS
    cols = ZL * Y * part
    cot = recv_ref[:, cols:]
    for zl in range(ZL):
        block = recv_ref[:, zl * Y * part : (zl + 1) * Y * part]
        grad = lax.dot_general(block, cot, (((0,), (0,)), ((), ())), preferred_element_type=F32)
        for y in range(Y):
            for zh in range(ZH):
                at = y * part + zh * C * ROWS
                first, second = grad[at : at + ROWS], grad[at + ROWS : at + 2 * ROWS]
                to = ((y * ZL + zl) * ZH + zh) * ROWS
                own_ref[to : to + ROWS, :] = jnp.where(c == 0, first, second).astype(BF16)
                sib_ref, to = (sib_a_ref, to) if y < Y // 2 else (sib_b_ref, to - Y // 2 * ZL * ZH * ROWS)
                sib_ref[to : to + ROWS, :] = jnp.where(c == 0, second, first).astype(BF16)


def out_kernel(tok_ref, gain_ref, cot_ref, inv_ref, *refs):
    w_refs, (keys_ref, tg_ref) = refs[:-2], refs[-2:]
    c, zl, y = (lax.axis_index(name) for name in ("c", "zl", "y"))
    rows, width = tok_ref.shape
    step = width // (ZL * Y)
    half = step // 2
    inv = jnp.concatenate([inv_ref[...]] * (half // inv_ref.shape[1]), axis=1)
    cot = cot_ref[...]

    def places():
        for s, off in enumerate((0, 1, 3, 2)):
            for h in range(2):
                for k in range(Y):
                    node = lax.rem(zl + off, ZL) * Y + lax.rem(y + k, Y)
                    core = c if h == 0 else 1 - c
                    at = pl.multiple_of(node * step + core * half, half)
                    yield pl.ds(at, half), w_refs[2 * s + h], slice(k * half, (k + 1) * half)

    keys = jnp.zeros(keys_ref.shape, F32)
    for cols, w_ref, wrows in places():
        normed = tok_ref[:, cols].astype(F32) * inv
        hidden = (normed * gain_ref[:, cols]).astype(BF16)
        keys = keys + jnp.dot(hidden, w_ref[wrows, :], preferred_element_type=F32)
    keys_ref[...] = keys.astype(BF16)
    mean = jnp.sum(cot.astype(F32) * keys, axis=-1, keepdims=True) / width
    for cols, w_ref, wrows in places():
        hidden_grad = lax.dot_general(
            cot, w_ref[wrows, :], (((1,), (1,)), ((), ())), preferred_element_type=F32
        )
        normed = tok_ref[:, cols].astype(F32) * inv
        tg_ref[:, cols] = (inv * (hidden_grad * gain_ref[:, cols] - normed * mean)).astype(BF16)


def hadamard(value, extent=128):
    rows, width = value.shape
    i = lax.broadcasted_iota(jnp.int32, (extent, extent), 0)
    j = lax.broadcasted_iota(jnp.int32, (extent, extent), 1)
    both = i & j
    both = both ^ (both >> 4)
    both = both ^ (both >> 2)
    both = both ^ (both >> 1)
    table = (1 - 2 * (both & 1)).astype(F32).astype(BF16)
    parts = []
    for k in range(width // extent):
        rest = value[:, k * extent : (k + 1) * extent]
        for _ in range(3):
            top = rest.astype(BF16)
            parts.append(top)
            rest = rest - top.astype(F32)
    out = jnp.dot(jnp.concatenate(parts, axis=0), table, preferred_element_type=F32)
    p = []
    for k in range(width // extent):
        at = 3 * k * rows
        p.append((out[at + 2 * rows : at + 3 * rows] + out[at + rows : at + 2 * rows]) + out[at : at + rows])
    s, t, u, v = p[0] + p[1], p[0] - p[1], p[2] + p[3], p[2] - p[3]
    return jnp.concatenate([s + u, t + v, s - u, t - v], axis=1)


def adam_kernel(tokens_all, recv_ref, first_ref, second_ref, master_ref, signs_ref, nm_ref, nf_ref, ns_ref, new_ref):
    total = jnp.sum(recv_ref[...].astype(F32), axis=0)
    half = total.shape[1]
    root = math.sqrt(2 * half)
    sign = (1 - 2 * signs_ref[...]).astype(F32)
    sign0, sign1 = sign[:, :half], sign[:, half:]
    gap = PAIR_GAP
    spun = hadamard(jnp.concatenate([total[:gap] * sign0, total[gap:] * sign1], axis=0)) * (1.0 / (root * tokens_all))
    q0, q1 = spun[:gap], spun[gap:]
    coded = jnp.concatenate([q0 + q1, q0 - q1], axis=1)
    new_first = beta_first * first_ref[...] + (1.0 - beta_first) * coded
    new_second = beta_second * second_ref[...] + (1.0 - beta_second) * coded * coded
    nf_ref[...] = new_first
    ns_ref[...] = new_second
    first_hat = new_first / (1.0 - beta_first**adam_steps)
    second_hat = new_second / (1.0 - beta_second**adam_steps)
    ratio = first_hat / (jnp.sqrt(second_hat) + adam_eps)
    lower, upper = ratio[:, :half], ratio[:, half:]
    back = hadamard(jnp.concatenate([lower + upper, lower - upper], axis=0)) / root
    update = jnp.concatenate([back[:gap] * sign0, back[gap:] * sign1], axis=0)
    master = master_ref[...]
    new_master = master - learn_rate * (update + weight_decay * master)
    nm_ref[...] = new_master
    new_ref[...] = jnp.broadcast_to(new_master.astype(BF16), new_ref.shape)


def ring(n, s):
    return [(i, (i + s) % n) for i in range(n)]


def along_z(shift):
    pairs = []
    for zl in range(ZL):
        for zh in range(ZH):
            for c in range(C):
                z = (zh * ZL + zl + shift(c)) % (ZH * ZL)
                pairs.append(((zl * ZH + zh) * C + c, ((z % ZL) * ZH + z // ZL) * C + c))
    return pairs


def shards(tokens, norm_gain, key_cotangent, secondary, master, moment_first, moment_second, signs):
    tok_rows, width = tokens.shape
    keys_w = key_cotangent.shape[1]
    c = lax.axis_index("c")
    gain = norm_gain.reshape(1, width)
    node_rows = secondary.shape[0]

    half = lax.dynamic_slice_in_dim(secondary, c * (node_rows // 2), node_rows // 2, 0)
    column = [half] + [lax.ppermute(half, "y", ring(Y, -k)) for k in range(1, Y)]
    column = jnp.concatenate(column, axis=0)
    z_axes = ("zl", "zh", "c")
    from_up = lax.ppermute(column, z_axes, along_z(lambda c: -1))
    from_down = lax.ppermute(column, z_axes, along_z(lambda c: 1))

    part = width // X
    step = 32
    by_rows = lambda cols: pl.BlockSpec((step, cols), lambda i: (i, 0))
    send, inv = pl.pallas_call(
        norm_kernel,
        out_shape=(shape((X, tok_rows, part + keys_w), BF16), shape((tok_rows, 128), F32)),
        grid=(tok_rows // step,),
        in_specs=[by_rows(width), pl.BlockSpec((1, width), lambda i: (0, 0)), by_rows(keys_w)],
        out_specs=(pl.BlockSpec((X, step, part + keys_w), lambda i: (0, i, 0)), by_rows(128)),
        cost_estimate=pl.CostEstimate(flops=tok_rows * width * 6, bytes_accessed=5 << 20, transcendentals=0),
        compiler_params=pltpu.CompilerParams(vmem_limit_bytes=56 << 20),
    )(tokens, gain, key_cotangent)
    recv = lax.all_to_all(send, "x", 0, 0, tiled=True).reshape(X * tok_rows, part + keys_w)
    recv, _ = lax.optimization_barrier((recv, column))
    own, *sib = kernel_call(
        grad_kernel,
        (shape((part // 2, keys_w), BF16),) + (shape((part // 4, keys_w), BF16),) * 2,
        0,
        1 << 20,
        1,
    )(recv)
    sib = [lax.ppermute(piece, "c", ring(C, 1)) for piece in sib]
    summed = (own.astype(F32) + jnp.concatenate(sib, axis=0).astype(F32)).astype(BF16)
    summed, column, from_up, from_down = lax.optimization_barrier((summed, column, from_up, from_down))
    from_far = jnp.where(c == 0, from_up, from_down)
    from_far = lax.ppermute(from_far, z_axes, along_z(lambda c: 2 * c - 1))
    weights = []
    for block in (column, from_up, from_down):
        weights += [block, lax.ppermute(block, "c", ring(C, 1))]
    blocks = lax.all_to_all(summed.reshape(Y, -1, keys_w), "y", 0, 0, tiled=True)
    blocks, from_far = lax.optimization_barrier((blocks, from_far))
    weights += [from_far, lax.ppermute(from_far, "c", ring(C, 1))]
    summed = jnp.sum(blocks.astype(F32), axis=0).astype(BF16)
    blocks = lax.all_to_all(summed.reshape(ZL * ZH, ROWS, keys_w), ("zl", "zh"), 0, 0, tiled=True)
    keys, token_grad = kernel_call(
        out_kernel,
        (shape((tok_rows, keys_w), BF16), shape(tokens.shape, BF16)),
        4 * tok_rows * width * keys_w,
        14 << 20,
        4 + len(weights),
    )(tokens, gain, key_cotangent, inv, *weights)
    blocks, keys, token_grad = lax.optimization_barrier((blocks, keys, token_grad))
    new_master, new_first, new_second, new_rows = kernel_call(
        functools.partial(adam_kernel, tok_rows * math.prod(SIZES)),
        (
            shape(master.shape, F32),
            shape(moment_first.shape, F32),
            shape(moment_second.shape, F32),
            shape((X * ZH, *master.shape), BF16),
        ),
        1 << 25,
        1 << 20,
        5,
    )(blocks, moment_first, moment_second, master, signs.reshape(1, -1))

    mine = lax.all_to_all(new_rows, ("x", "zh"), 0, 0, tiled=True)
    other = lax.ppermute(mine, "c", ring(C, 1))
    even = jnp.where(c == 0, mine, other)
    odd = jnp.where(c == 0, other, mine)
    new_secondary = jnp.stack([even, odd], axis=1).reshape(node_rows, keys_w)
    return (keys, token_grad, new_master, new_first, new_second, new_secondary)


def solution(mesh):
    fine = Mesh(mesh.devices.reshape(SIZES), AXES)
    split = P(AXES, None)
    return jax.shard_map(
        shards,
        mesh=fine,
        in_specs=(split, P(), split, P(("zl", "y"), None), split, split, split, P()),
        out_specs=(split, split, split, split, split, P(("zl", "y"), None)),
        check_vma=False,
    )
```

```python
import functools
import math

import jax
import jax.numpy as jnp
from jax import lax
from jax.experimental import pallas as pl
from jax.experimental.pallas import tpu as pltpu
from jax.sharding import Mesh
from jax.sharding import PartitionSpec as P

PAIR_GAP = 16
norm_eps = 1e-05
adam_eps = 1e-08
beta_first = 0.9
beta_second = 0.95
adam_steps = 10
learn_rate = 0.002
weight_decay = 0.1

AXES = ("zl", "y", "x", "zh", "c")
SIZES = (4, 4, 4, 2, 2)
ZL, Y, X, ZH, C = SIZES
ROWS = 32
VMEM = pl.BlockSpec(memory_space=pltpu.VMEM)
BF16 = jnp.bfloat16
F32 = jnp.float32


def shape(dims, kind):
    return jax.ShapeDtypeStruct(dims, kind)


def kernel_call(body, outs, flops, nbytes, n_in, limit=24 << 20):
    return pl.pallas_call(
        body,
        out_shape=outs,
        in_specs=[VMEM] * n_in,
        out_specs=jax.tree.map(lambda _: VMEM, outs),
        cost_estimate=pl.CostEstimate(flops=flops, bytes_accessed=nbytes, transcendentals=0),
        compiler_params=pltpu.CompilerParams(vmem_limit_bytes=limit),
    )


def norm_kernel(tok_ref, gain_ref, cot_ref, send_ref, inv_ref):
    c = lax.axis_index("c")
    rows, width = tok_ref.shape
    step = X * ZH * C * ROWS
    acc = jnp.zeros((rows, step), F32)
    for k in range(width // step):
        t = tok_ref[:, k * step : (k + 1) * step].astype(F32)
        acc = acc + t * t
    inv = lax.rsqrt(jnp.sum(acc, axis=-1, keepdims=True) / width + norm_eps)
    inv = jnp.broadcast_to(inv, inv_ref.shape)
    inv_ref[...] = inv
    part = ZH * C * ROWS
    stride_p, stride_q = jnp.where(c == 0, part, step), jnp.where(c == 0, step, part)
    for zl in range(ZL):
        for p in range(X):
            for q in range(Y):
                at = pl.multiple_of(zl * Y * step + p * stride_p + q * stride_q, part)
                cols = pl.ds(at, part)
                normed = tok_ref[:, cols].astype(F32) * inv
                to = (zl * Y + q) * part
                send_ref[p, :, to : to + part] = (normed * gain_ref[:, cols]).astype(BF16)
    for p in range(X):
        send_ref[p, :, ZL * Y * part :] = cot_ref[...]


def grad_kernel(recv_ref, send_ref):
    part = ZH * C * ROWS
    cols = ZL * Y * part
    cot = recv_ref[:, cols:]
    for zl in range(ZL):
        block = recv_ref[:, zl * Y * part : (zl + 1) * Y * part]
        grad = lax.dot_general(block, cot, (((0,), (0,)), ((), ())), preferred_element_type=F32)
        grad = grad.astype(BF16)
        for q in range(Y):
            for zh in range(ZH):
                for c in range(C):
                    at = q * part + (zh * C + c) * ROWS
                    to = ((c * ZL + zl) * ZH + zh) * ROWS
                    send_ref[q, to : to + ROWS, :] = grad[at : at + ROWS]


def sum_kernel(recv_ref, own_ref, sib_ref):
    c = lax.axis_index("c")
    rows = own_ref.shape[0]
    for ref, core in ((sib_ref, 1 - c), (own_ref, c)):
        part = recv_ref[:, pl.ds(pl.multiple_of(core * rows, rows), rows), :].astype(F32)
        ref[...] = jnp.sum(part, axis=0).astype(ref.dtype)


def out_kernel(tok_ref, gain_ref, cot_ref, inv_ref, *refs):
    w_refs, (keys_ref, tg_ref) = refs[:-2], refs[-2:]
    c, zl, y = (lax.axis_index(name) for name in ("c", "zl", "y"))
    rows, width = tok_ref.shape
    step = width // (ZL * Y)
    half = step // 2
    inv = jnp.concatenate([inv_ref[...]] * (half // inv_ref.shape[1]), axis=1)
    cot = cot_ref[...]

    def places():
        for s, off in enumerate((0, 1, 3, 2)):
            for h in range(2):
                for k in range(Y):
                    node = lax.rem(zl + off, ZL) * Y + lax.rem(y + k, Y)
                    core = c if h == 0 else 1 - c
                    at = pl.multiple_of(node * step + core * half, half)
                    yield pl.ds(at, half), w_refs[2 * s + h], slice(k * half, (k + 1) * half)

    keys = jnp.zeros(keys_ref.shape, F32)
    for cols, w_ref, wrows in places():
        normed = tok_ref[:, cols].astype(F32) * inv
        hidden = (normed * gain_ref[:, cols]).astype(BF16)
        keys = keys + jnp.dot(hidden, w_ref[wrows, :], preferred_element_type=F32)
    keys_ref[...] = keys.astype(BF16)
    mean = jnp.sum(cot.astype(F32) * keys, axis=-1, keepdims=True) / width
    for cols, w_ref, wrows in places():
        hidden_grad = lax.dot_general(
            cot, w_ref[wrows, :], (((1,), (1,)), ((), ())), preferred_element_type=F32
        )
        normed = tok_ref[:, cols].astype(F32) * inv
        tg_ref[:, cols] = (inv * (hidden_grad * gain_ref[:, cols] - normed * mean)).astype(BF16)


def hadamard(value, extent=128):
    rows, width = value.shape
    i = lax.broadcasted_iota(jnp.int32, (extent, extent), 0)
    j = lax.broadcasted_iota(jnp.int32, (extent, extent), 1)
    both = i & j
    both = both ^ (both >> 4)
    both = both ^ (both >> 2)
    both = both ^ (both >> 1)
    table = (1 - 2 * (both & 1)).astype(F32).astype(BF16)
    parts = []
    for k in range(width // extent):
        rest = value[:, k * extent : (k + 1) * extent]
        for _ in range(3):
            top = rest.astype(BF16)
            parts.append(top)
            rest = rest - top.astype(F32)
    out = jnp.dot(jnp.concatenate(parts, axis=0), table, preferred_element_type=F32)
    p = []
    for k in range(width // extent):
        at = 3 * k * rows
        p.append((out[at + 2 * rows : at + 3 * rows] + out[at + rows : at + 2 * rows]) + out[at : at + rows])
    s, t, u, v = p[0] + p[1], p[0] - p[1], p[2] + p[3], p[2] - p[3]
    return jnp.concatenate([s + u, t + v, s - u, t - v], axis=1)


def adam_kernel(tokens_all, recv_ref, first_ref, second_ref, master_ref, signs_ref, nm_ref, nf_ref, ns_ref, new_ref):
    total = jnp.sum(recv_ref[...].astype(F32), axis=0)
    half = total.shape[1]
    root = math.sqrt(2 * half)
    sign = (1 - 2 * signs_ref[...]).astype(F32)
    sign0, sign1 = sign[:, :half], sign[:, half:]
    gap = PAIR_GAP
    spun = hadamard(jnp.concatenate([total[:gap] * sign0, total[gap:] * sign1], axis=0)) * (1.0 / (root * tokens_all))
    q0, q1 = spun[:gap], spun[gap:]
    coded = jnp.concatenate([q0 + q1, q0 - q1], axis=1)
    new_first = beta_first * first_ref[...] + (1.0 - beta_first) * coded
    new_second = beta_second * second_ref[...] + (1.0 - beta_second) * coded * coded
    nf_ref[...] = new_first
    ns_ref[...] = new_second
    first_hat = new_first / (1.0 - beta_first**adam_steps)
    second_hat = new_second / (1.0 - beta_second**adam_steps)
    ratio = first_hat / (jnp.sqrt(second_hat) + adam_eps)
    lower, upper = ratio[:, :half], ratio[:, half:]
    back = hadamard(jnp.concatenate([lower + upper, lower - upper], axis=0)) / root
    update = jnp.concatenate([back[:gap] * sign0, back[gap:] * sign1], axis=0)
    master = master_ref[...]
    new_master = master - learn_rate * (update + weight_decay * master)
    nm_ref[...] = new_master
    new_ref[...] = jnp.broadcast_to(new_master.astype(BF16), new_ref.shape)


def ring(n, s):
    return [(i, (i + s) % n) for i in range(n)]


def along_z(shift):
    pairs = []
    for zl in range(ZL):
        for zh in range(ZH):
            for c in range(C):
                z = (zh * ZL + zl + shift(c)) % (ZH * ZL)
                pairs.append(((zl * ZH + zh) * C + c, ((z % ZL) * ZH + z // ZL) * C + c))
    return pairs


def mixed(value, first):
    groups = []
    for c in range(C):
        for i in range(X):
            lines = [((i, j) if (c == 0) == first else (j, i)) for j in range(Y)]
            groups.append([(y * X + x) * C + c for y, x in lines])
    return lax.all_to_all(value, ("y", "x", "c"), 0, 0, axis_index_groups=groups, tiled=True)


def shards(tokens, norm_gain, key_cotangent, secondary, master, moment_first, moment_second, signs):
    tok_rows, width = tokens.shape
    keys_w = key_cotangent.shape[1]
    c = lax.axis_index("c")
    gain = norm_gain.reshape(1, width)
    node_rows = secondary.shape[0]

    half = lax.dynamic_slice_in_dim(secondary, c * (node_rows // 2), node_rows // 2, 0)
    column = [half] + [lax.ppermute(half, "y", ring(Y, -k)) for k in range(1, Y)]
    column = jnp.concatenate(column, axis=0)
    z_axes = ("zl", "zh", "c")

    part = width // X
    step = 32
    by_rows = lambda cols: pl.BlockSpec((step, cols), lambda i: (i, 0))
    send, inv = pl.pallas_call(
        norm_kernel,
        out_shape=(shape((X, tok_rows, part + keys_w), BF16), shape((tok_rows, 128), F32)),
        grid=(tok_rows // step,),
        in_specs=[by_rows(width), pl.BlockSpec((1, width), lambda i: (0, 0)), by_rows(keys_w)],
        out_specs=(pl.BlockSpec((X, step, part + keys_w), lambda i: (0, i, 0)), by_rows(128)),
        cost_estimate=pl.CostEstimate(flops=tok_rows * width * 6, bytes_accessed=5 << 20, transcendentals=0),
        compiler_params=pltpu.CompilerParams(vmem_limit_bytes=56 << 20),
    )(tokens, gain, key_cotangent)
    recv = mixed(send, True).reshape(X * tok_rows, part + keys_w)
    from_up = lax.ppermute(column, z_axes, along_z(lambda c: -1))
    from_down = lax.ppermute(column, z_axes, along_z(lambda c: 1))
    weights = []
    for block in (column, from_up, from_down):
        weights += [block, lax.ppermute(block, "c", ring(C, 1))]
    send = kernel_call(
        grad_kernel,
        shape((Y, part // Y, keys_w), BF16),
        0,
        1 << 20,
        1,
        40 << 20,
    )(recv)
    blocks = mixed(send, False)
    own, sib = kernel_call(
        sum_kernel,
        (shape((part // Y // C, keys_w), F32), shape((part // Y // C, keys_w), BF16)),
        0,
        1 << 20,
        1,
    )(blocks)
    sib = lax.ppermute(sib, "c", ring(C, 1))
    summed = (own + sib.astype(F32)).astype(BF16)
    summed, *weights = lax.optimization_barrier((summed, *weights))
    from_far = jnp.where(c == 0, weights[2], weights[4])
    from_far = lax.ppermute(from_far, z_axes, along_z(lambda c: 2 * c - 1))
    blocks = lax.all_to_all(summed.reshape(ZL * ZH, ROWS, keys_w), ("zl", "zh"), 0, 0, tiled=True)
    blocks, from_far = lax.optimization_barrier((blocks, from_far))
    weights += [from_far, lax.ppermute(from_far, "c", ring(C, 1))]
    new_master, new_first, new_second, new_rows = kernel_call(
        functools.partial(adam_kernel, tok_rows * math.prod(SIZES)),
        (
            shape(master.shape, F32),
            shape(moment_first.shape, F32),
            shape(moment_second.shape, F32),
            shape((X * ZH, *master.shape), BF16),
        ),
        1 << 25,
        1 << 20,
        5,
    )(blocks, moment_first, moment_second, master, signs.reshape(1, -1))

    mine = lax.all_to_all(new_rows, ("x", "zh"), 0, 0, tiled=True)
    keys, token_grad = kernel_call(
        out_kernel,
        (shape((tok_rows, keys_w), BF16), shape(tokens.shape, BF16)),
        4 * tok_rows * width * keys_w,
        14 << 20,
        4 + len(weights),
    )(tokens, gain, key_cotangent, inv, *weights)
    mine, keys, token_grad = lax.optimization_barrier((mine, keys, token_grad))
    other = lax.ppermute(mine, "c", ring(C, 1))
    even = jnp.where(c == 0, mine, other)
    odd = jnp.where(c == 0, other, mine)
    new_secondary = jnp.stack([even, odd], axis=1).reshape(node_rows, keys_w)
    return (keys, token_grad, new_master, new_first, new_second, new_secondary)


def solution(mesh):
    fine = Mesh(mesh.devices.reshape(SIZES), AXES)
    split = P(AXES, None)
    return jax.shard_map(
        shards,
        mesh=fine,
        in_specs=(split, P(), split, P(("zl", "y"), None), split, split, split, P()),
        out_specs=(split, split, split, split, split, P(("zl", "y"), None)),
        check_vma=False,
    )
```

```python
import functools
import math

import jax
import jax.numpy as jnp
from jax import lax
from jax.experimental import pallas as pl
from jax.experimental.pallas import tpu as pltpu
from jax.sharding import Mesh
from jax.sharding import PartitionSpec as P

PAIR_GAP = 16
norm_eps = 1e-05
adam_eps = 1e-08
beta_first = 0.9
beta_second = 0.95
adam_steps = 10
learn_rate = 0.002
weight_decay = 0.1

AXES = ("zl", "y", "x", "zh", "c")
SIZES = (4, 4, 4, 2, 2)
ZL, Y, X, ZH, C = SIZES
ROWS = 32
VMEM = pl.BlockSpec(memory_space=pltpu.VMEM)
BF16 = jnp.bfloat16
F32 = jnp.float32


def shape(dims, kind):
    return jax.ShapeDtypeStruct(dims, kind)


def kernel_call(body, outs, flops, nbytes, n_in, limit=24 << 20):
    return pl.pallas_call(
        body,
        out_shape=outs,
        in_specs=[VMEM] * n_in,
        out_specs=jax.tree.map(lambda _: VMEM, outs),
        cost_estimate=pl.CostEstimate(flops=flops, bytes_accessed=nbytes, transcendentals=0),
        compiler_params=pltpu.CompilerParams(vmem_limit_bytes=limit),
    )


def norm_kernel(tok_ref, gain_ref, cot_ref, send_ref, inv_ref):
    c = lax.axis_index("c")
    rows, width = tok_ref.shape
    step = X * ZH * C * ROWS
    acc = jnp.zeros((rows, step), F32)
    for k in range(width // step):
        t = tok_ref[:, k * step : (k + 1) * step].astype(F32)
        acc = acc + t * t
    inv = lax.rsqrt(jnp.sum(acc, axis=-1, keepdims=True) / width + norm_eps)
    inv = jnp.broadcast_to(inv, inv_ref.shape)
    inv_ref[...] = inv
    part = ZH * C * ROWS
    stride_p, stride_q = jnp.where(c == 0, part, step), jnp.where(c == 0, step, part)
    for zl in range(ZL):
        for p in range(X):
            for q in range(Y):
                at = pl.multiple_of(zl * Y * step + p * stride_p + q * stride_q, part)
                cols = pl.ds(at, part)
                normed = tok_ref[:, cols].astype(F32) * inv
                to = (zl * Y + q) * part
                send_ref[p, :, to : to + part] = (normed * gain_ref[:, cols]).astype(BF16)
    for p in range(X):
        send_ref[p, :, ZL * Y * part :] = cot_ref[...]


def grad_kernel(recv_ref, send_ref):
    part = ZH * C * ROWS
    cols = ZL * Y * part
    cot = recv_ref[:, cols:]
    for zl in range(ZL):
        block = recv_ref[:, zl * Y * part : (zl + 1) * Y * part]
        grad = lax.dot_general(block, cot, (((0,), (0,)), ((), ())), preferred_element_type=F32)
        grad = grad.astype(BF16)
        for q in range(Y):
            for zh in range(ZH):
                for c in range(C):
                    at = q * part + (zh * C + c) * ROWS
                    to = ((c * ZL + zl) * ZH + zh) * ROWS
                    send_ref[q, to : to + ROWS, :] = grad[at : at + ROWS]


def sum_kernel(recv_ref, own_ref, sib_ref):
    c = lax.axis_index("c")
    rows = own_ref.shape[0]
    for ref, core in ((sib_ref, 1 - c), (own_ref, c)):
        part = recv_ref[:, pl.ds(pl.multiple_of(core * rows, rows), rows), :].astype(F32)
        ref[...] = jnp.sum(part, axis=0).astype(ref.dtype)


def out_kernel(tok_ref, gain_ref, cot_ref, inv_ref, *refs):
    w_refs, (keys_ref, tg_ref) = refs[:-2], refs[-2:]
    c, zl, y = (lax.axis_index(name) for name in ("c", "zl", "y"))
    rows, width = tok_ref.shape
    step = width // (ZL * Y)
    half = step // 2
    inv = jnp.concatenate([inv_ref[...]] * (half // inv_ref.shape[1]), axis=1)
    cot = cot_ref[...]

    def places():
        for s, off in enumerate((0, 1, 3, 2)):
            for h in range(2):
                for k in range(Y):
                    core = c if h == 0 else 1 - c
                    on_zl, on_y = jnp.where(core == 0, off, k), jnp.where(core == 0, k, off)
                    node = lax.rem(zl + on_zl, ZL) * Y + lax.rem(y + on_y, Y)
                    at = pl.multiple_of(node * step + core * half, half)
                    yield pl.ds(at, half), w_refs[2 * s + h], slice(k * half, (k + 1) * half)

    keys = jnp.zeros(keys_ref.shape, F32)
    for cols, w_ref, wrows in places():
        normed = tok_ref[:, cols].astype(F32) * inv
        hidden = (normed * gain_ref[:, cols]).astype(BF16)
        keys = keys + jnp.dot(hidden, w_ref[wrows, :], preferred_element_type=F32)
    keys_ref[...] = keys.astype(BF16)
    mean = jnp.sum(cot.astype(F32) * keys, axis=-1, keepdims=True) / width
    for cols, w_ref, wrows in places():
        hidden_grad = lax.dot_general(
            cot, w_ref[wrows, :], (((1,), (1,)), ((), ())), preferred_element_type=F32
        )
        normed = tok_ref[:, cols].astype(F32) * inv
        tg_ref[:, cols] = (inv * (hidden_grad * gain_ref[:, cols] - normed * mean)).astype(BF16)


def hadamard(value, extent=128):
    rows, width = value.shape
    i = lax.broadcasted_iota(jnp.int32, (extent, extent), 0)
    j = lax.broadcasted_iota(jnp.int32, (extent, extent), 1)
    both = i & j
    both = both ^ (both >> 4)
    both = both ^ (both >> 2)
    both = both ^ (both >> 1)
    table = (1 - 2 * (both & 1)).astype(F32).astype(BF16)
    parts = []
    for k in range(width // extent):
        rest = value[:, k * extent : (k + 1) * extent]
        for _ in range(3):
            top = rest.astype(BF16)
            parts.append(top)
            rest = rest - top.astype(F32)
    out = jnp.dot(jnp.concatenate(parts, axis=0), table, preferred_element_type=F32)
    p = []
    for k in range(width // extent):
        at = 3 * k * rows
        p.append((out[at + 2 * rows : at + 3 * rows] + out[at + rows : at + 2 * rows]) + out[at : at + rows])
    s, t, u, v = p[0] + p[1], p[0] - p[1], p[2] + p[3], p[2] - p[3]
    return jnp.concatenate([s + u, t + v, s - u, t - v], axis=1)


def adam_kernel(tokens_all, recv_ref, first_ref, second_ref, master_ref, signs_ref, nm_ref, nf_ref, ns_ref, new_ref):
    total = jnp.sum(recv_ref[...].astype(F32), axis=0)
    half = total.shape[1]
    root = math.sqrt(2 * half)
    sign = (1 - 2 * signs_ref[...]).astype(F32)
    sign0, sign1 = sign[:, :half], sign[:, half:]
    gap = PAIR_GAP
    spun = hadamard(jnp.concatenate([total[:gap] * sign0, total[gap:] * sign1], axis=0)) * (1.0 / (root * tokens_all))
    q0, q1 = spun[:gap], spun[gap:]
    coded = jnp.concatenate([q0 + q1, q0 - q1], axis=1)
    new_first = beta_first * first_ref[...] + (1.0 - beta_first) * coded
    new_second = beta_second * second_ref[...] + (1.0 - beta_second) * coded * coded
    nf_ref[...] = new_first
    ns_ref[...] = new_second
    first_hat = new_first / (1.0 - beta_first**adam_steps)
    second_hat = new_second / (1.0 - beta_second**adam_steps)
    ratio = first_hat / (jnp.sqrt(second_hat) + adam_eps)
    lower, upper = ratio[:, :half], ratio[:, half:]
    back = hadamard(jnp.concatenate([lower + upper, lower - upper], axis=0)) / root
    update = jnp.concatenate([back[:gap] * sign0, back[gap:] * sign1], axis=0)
    master = master_ref[...]
    new_master = master - learn_rate * (update + weight_decay * master)
    nm_ref[...] = new_master
    new_ref[...] = jnp.broadcast_to(new_master.astype(BF16), new_ref.shape)


def ring(n, s):
    return [(i, (i + s) % n) for i in range(n)]


GATHER = ("zl", "y", "zh", "c")


def moved(on_z, shift):
    pairs = []
    for i in range(ZL * Y * ZH * C):
        zl, y, zh, c = i // (Y * ZH * C), i // (ZH * C) % Y, i // C % ZH, i % C
        if on_z(c):
            z = (zh * ZL + zl + shift(zl, True)) % (ZH * ZL)
            zl, zh = z % ZL, z // ZL
        else:
            y = (y + shift(y, False)) % Y
        pairs.append((i, ((zl * Y + y) * ZH + zh) * C + c))
    return pairs


def first_step(value, k):
    shift = lambda place, on_z: {1: -1, 2: 2 - 4 * (place % 2) if on_z else -2, 3: 1}[k]
    return lax.ppermute(value, GATHER, moved(lambda c: c == 1, shift))


def second_step(value, shift):
    return lax.ppermute(value, GATHER, moved(lambda c: c == 0, shift))


def mixed(value, first):
    groups = []
    for c in range(C):
        for i in range(X):
            lines = [((i, j) if (c == 0) == first else (j, i)) for j in range(Y)]
            groups.append([(y * X + x) * C + c for y, x in lines])
    return lax.all_to_all(value, ("y", "x", "c"), 0, 0, axis_index_groups=groups, tiled=True)


def shards(tokens, norm_gain, key_cotangent, secondary, master, moment_first, moment_second, signs):
    tok_rows, width = tokens.shape
    keys_w = key_cotangent.shape[1]
    c = lax.axis_index("c")
    gain = norm_gain.reshape(1, width)
    node_rows = secondary.shape[0]

    half = lax.dynamic_slice_in_dim(secondary, c * (node_rows // 2), node_rows // 2, 0)
    column = jnp.concatenate([half] + [first_step(half, k) for k in range(1, Y)], axis=0)

    part = width // X
    step = 32
    by_rows = lambda cols: pl.BlockSpec((step, cols), lambda i: (i, 0))
    send, inv = pl.pallas_call(
        norm_kernel,
        out_shape=(shape((X, tok_rows, part + keys_w), BF16), shape((tok_rows, 128), F32)),
        grid=(tok_rows // step,),
        in_specs=[by_rows(width), pl.BlockSpec((1, width), lambda i: (0, 0)), by_rows(keys_w)],
        out_specs=(pl.BlockSpec((X, step, part + keys_w), lambda i: (0, i, 0)), by_rows(128)),
        cost_estimate=pl.CostEstimate(flops=tok_rows * width * 6, bytes_accessed=5 << 20, transcendentals=0),
        compiler_params=pltpu.CompilerParams(vmem_limit_bytes=56 << 20),
    )(tokens, gain, key_cotangent)
    recv = mixed(send, True).reshape(X * tok_rows, part + keys_w)
    from_up = second_step(column, lambda place, on_z: -1)
    from_down = second_step(column, lambda place, on_z: 1)
    weights = []
    for block in (column, from_up, from_down):
        weights += [block, lax.ppermute(block, "c", ring(C, 1))]
    send = kernel_call(
        grad_kernel,
        shape((Y, part // Y, keys_w), BF16),
        0,
        1 << 20,
        1,
        40 << 20,
    )(recv)
    blocks = mixed(send, False)
    own, sib = kernel_call(
        sum_kernel,
        (shape((part // Y // C, keys_w), F32), shape((part // Y // C, keys_w), BF16)),
        0,
        1 << 20,
        1,
    )(blocks)
    sib = lax.ppermute(sib, "c", ring(C, 1))
    summed = (own + sib.astype(F32)).astype(BF16)
    summed, *weights = lax.optimization_barrier((summed, *weights))
    odd = jnp.where(c == 0, lax.axis_index("zl"), lax.axis_index("y")) % 2 == 1
    from_far = jnp.where(odd, weights[2], weights[4])
    from_far = second_step(from_far, lambda place, on_z: 1 - 2 * (place % 2))
    blocks = lax.all_to_all(summed.reshape(ZL * ZH, ROWS, keys_w), ("zl", "zh"), 0, 0, tiled=True)
    blocks, from_far = lax.optimization_barrier((blocks, from_far))
    weights += [from_far, lax.ppermute(from_far, "c", ring(C, 1))]
    new_master, new_first, new_second, new_rows = kernel_call(
        functools.partial(adam_kernel, tok_rows * math.prod(SIZES)),
        (
            shape(master.shape, F32),
            shape(moment_first.shape, F32),
            shape(moment_second.shape, F32),
            shape((X * ZH, *master.shape), BF16),
        ),
        1 << 25,
        1 << 20,
        5,
    )(blocks, moment_first, moment_second, master, signs.reshape(1, -1))

    mine = lax.all_to_all(new_rows, ("x", "zh"), 0, 0, tiled=True)
    keys, token_grad = kernel_call(
        out_kernel,
        (shape((tok_rows, keys_w), BF16), shape(tokens.shape, BF16)),
        4 * tok_rows * width * keys_w,
        14 << 20,
        4 + len(weights),
    )(tokens, gain, key_cotangent, inv, *weights)
    mine, keys, token_grad = lax.optimization_barrier((mine, keys, token_grad))
    other = lax.ppermute(mine, "c", ring(C, 1))
    even = jnp.where(c == 0, mine, other)
    odd = jnp.where(c == 0, other, mine)
    new_secondary = jnp.stack([even, odd], axis=1).reshape(node_rows, keys_w)
    return (keys, token_grad, new_master, new_first, new_second, new_secondary)


def solution(mesh):
    fine = Mesh(mesh.devices.reshape(SIZES), AXES)
    split = P(AXES, None)
    return jax.shard_map(
        shards,
        mesh=fine,
        in_specs=(split, P(), split, P(("zl", "y"), None), split, split, split, P()),
        out_specs=(split, split, split, split, split, P(("zl", "y"), None)),
        check_vma=False,
    )
```

```python
import functools
import math

import jax
import jax.numpy as jnp
from jax import lax
from jax.experimental import pallas as pl
from jax.experimental.pallas import tpu as pltpu
from jax.sharding import Mesh
from jax.sharding import PartitionSpec as P

PAIR_GAP = 16
norm_eps = 1e-05
adam_eps = 1e-08
beta_first = 0.9
beta_second = 0.95
adam_steps = 10
learn_rate = 0.002
weight_decay = 0.1

AXES = ("zl", "y", "x", "zh", "c")
SIZES = (4, 4, 4, 2, 2)
ZL, Y, X, ZH, C = SIZES
ROWS = 32
VMEM = pl.BlockSpec(memory_space=pltpu.VMEM)
BF16 = jnp.bfloat16
F32 = jnp.float32


def shape(dims, kind):
    return jax.ShapeDtypeStruct(dims, kind)


def kernel_call(body, outs, flops, nbytes, n_in, limit=24 << 20):
    return pl.pallas_call(
        body,
        out_shape=outs,
        in_specs=[VMEM] * n_in,
        out_specs=jax.tree.map(lambda _: VMEM, outs),
        cost_estimate=pl.CostEstimate(flops=flops, bytes_accessed=nbytes, transcendentals=0),
        compiler_params=pltpu.CompilerParams(vmem_limit_bytes=limit),
    )


def norm_kernel(tok_ref, gain_ref, cot_ref, send_ref, inv_ref):
    c = lax.axis_index("c")
    rows, width = tok_ref.shape
    step = X * ZH * C * ROWS
    acc = jnp.zeros((rows, step), F32)
    for k in range(width // step):
        t = tok_ref[:, k * step : (k + 1) * step].astype(F32)
        acc = acc + t * t
    inv = lax.rsqrt(jnp.sum(acc, axis=-1, keepdims=True) / width + norm_eps)
    inv = jnp.broadcast_to(inv, inv_ref.shape)
    inv_ref[...] = inv
    part = ZH * C * ROWS
    stride_p, stride_q = jnp.where(c == 0, part, step), jnp.where(c == 0, step, part)
    for zl in range(ZL):
        for p in range(X):
            for q in range(Y):
                at = pl.multiple_of(zl * Y * step + p * stride_p + q * stride_q, part)
                cols = pl.ds(at, part)
                normed = tok_ref[:, cols].astype(F32) * inv
                to = (zl * Y + q) * part
                send_ref[p, :, to : to + part] = (normed * gain_ref[:, cols]).astype(BF16)
    for p in range(X):
        send_ref[p, :, ZL * Y * part :] = cot_ref[...]


def grad_kernel(recv_ref, send_ref):
    part = ZH * C * ROWS
    cols = ZL * Y * part
    cot = recv_ref[:, cols:]
    for zl in range(ZL):
        block = recv_ref[:, zl * Y * part : (zl + 1) * Y * part]
        grad = lax.dot_general(block, cot, (((0,), (0,)), ((), ())), preferred_element_type=F32)
        grad = grad.astype(BF16)
        for q in range(Y):
            for zh in range(ZH):
                for c in range(C):
                    at = q * part + (zh * C + c) * ROWS
                    to = ((c * ZL + zl) * ZH + zh) * ROWS
                    send_ref[q, to : to + ROWS, :] = grad[at : at + ROWS]


def sum_kernel(recv_ref, own_ref, sib_ref):
    c = lax.axis_index("c")
    rows = own_ref.shape[0]
    for ref, core in ((sib_ref, 1 - c), (own_ref, c)):
        part = recv_ref[:, pl.ds(pl.multiple_of(core * rows, rows), rows), :].astype(F32)
        ref[...] = jnp.sum(part, axis=0).astype(ref.dtype)


def places(width, refs):
    c, zl, y = (lax.axis_index(name) for name in ("c", "zl", "y"))
    step = width // (ZL * Y)
    half = step // 2
    for s, off in enumerate((0, 1, 3, 2)):
        for h in range(C):
            for k in range(Y):
                core = c if h == 0 else 1 - c
                on_zl, on_y = jnp.where(core == 0, off, k), jnp.where(core == 0, k, off)
                node = lax.rem(zl + on_zl, ZL) * Y + lax.rem(y + on_y, Y)
                at = pl.multiple_of(node * step + core * half, half)
                ref, row = (refs[2 * s + h], k) if s < 3 else (refs[2 * (s + k // 2) + h], k % 2)
                yield pl.ds(at, half), ref[row * half : (row + 1) * half, :]


def widened(ref, cols):
    return jnp.concatenate([ref[...]] * (cols // ref.shape[1]), axis=1)


def keys_kernel(tok_ref, gain_ref, cot_ref, inv_ref, *refs):
    refs, (keys_ref, mean_ref) = refs[:-2], refs[-2:]
    width = tok_ref.shape[1]
    inv = widened(inv_ref, width // (ZL * Y * C))
    keys = jnp.zeros(keys_ref.shape, F32)
    for cols, weights in places(width, refs):
        normed = tok_ref[:, cols].astype(F32) * inv
        hidden = (normed * gain_ref[:, cols]).astype(BF16)
        keys = keys + jnp.dot(hidden, weights, preferred_element_type=F32)
    keys_ref[...] = keys.astype(BF16)
    mean = jnp.sum(cot_ref[...].astype(F32) * keys, axis=-1, keepdims=True) / width
    mean_ref[...] = jnp.broadcast_to(mean, mean_ref.shape)


def token_grad_kernel(tok_ref, gain_ref, cot_ref, inv_ref, mean_ref, *refs):
    refs, (tg_ref,) = refs[:-1], refs[-1:]
    width = tok_ref.shape[1]
    inv = widened(inv_ref, width // (ZL * Y * C))
    mean = widened(mean_ref, width // (ZL * Y * C))
    cot = cot_ref[...]
    for cols, weights in places(width, refs):
        hidden_grad = lax.dot_general(cot, weights, (((1,), (1,)), ((), ())), preferred_element_type=F32)
        normed = tok_ref[:, cols].astype(F32) * inv
        tg_ref[:, cols] = (inv * (hidden_grad * gain_ref[:, cols] - normed * mean)).astype(BF16)


def hadamard(value, extent=128):
    rows, width = value.shape
    i = lax.broadcasted_iota(jnp.int32, (extent, extent), 0)
    j = lax.broadcasted_iota(jnp.int32, (extent, extent), 1)
    both = i & j
    both = both ^ (both >> 4)
    both = both ^ (both >> 2)
    both = both ^ (both >> 1)
    table = (1 - 2 * (both & 1)).astype(F32).astype(BF16)
    parts = []
    for k in range(width // extent):
        rest = value[:, k * extent : (k + 1) * extent]
        for _ in range(3):
            top = rest.astype(BF16)
            parts.append(top)
            rest = rest - top.astype(F32)
    out = jnp.dot(jnp.concatenate(parts, axis=0), table, preferred_element_type=F32)
    p = []
    for k in range(width // extent):
        at = 3 * k * rows
        p.append((out[at + 2 * rows : at + 3 * rows] + out[at + rows : at + 2 * rows]) + out[at : at + rows])
    s, t, u, v = p[0] + p[1], p[0] - p[1], p[2] + p[3], p[2] - p[3]
    return jnp.concatenate([s + u, t + v, s - u, t - v], axis=1)


def adam_kernel(tokens_all, recv_ref, first_ref, second_ref, master_ref, signs_ref, nm_ref, nf_ref, ns_ref, new_ref):
    total = jnp.sum(recv_ref[...].astype(F32), axis=0)
    half = total.shape[1]
    root = math.sqrt(2 * half)
    sign = (1 - 2 * signs_ref[...]).astype(F32)
    sign0, sign1 = sign[:, :half], sign[:, half:]
    gap = PAIR_GAP
    spun = hadamard(jnp.concatenate([total[:gap] * sign0, total[gap:] * sign1], axis=0)) * (1.0 / (root * tokens_all))
    q0, q1 = spun[:gap], spun[gap:]
    coded = jnp.concatenate([q0 + q1, q0 - q1], axis=1)
    new_first = beta_first * first_ref[...] + (1.0 - beta_first) * coded
    new_second = beta_second * second_ref[...] + (1.0 - beta_second) * coded * coded
    nf_ref[...] = new_first
    ns_ref[...] = new_second
    first_hat = new_first / (1.0 - beta_first**adam_steps)
    second_hat = new_second / (1.0 - beta_second**adam_steps)
    ratio = first_hat / (jnp.sqrt(second_hat) + adam_eps)
    lower, upper = ratio[:, :half], ratio[:, half:]
    back = hadamard(jnp.concatenate([lower + upper, lower - upper], axis=0)) / root
    update = jnp.concatenate([back[:gap] * sign0, back[gap:] * sign1], axis=0)
    master = master_ref[...]
    new_master = master - learn_rate * (update + weight_decay * master)
    nm_ref[...] = new_master
    new_ref[...] = jnp.broadcast_to(new_master.astype(BF16), new_ref.shape)


def ring(n, s):
    return [(i, (i + s) % n) for i in range(n)]


GATHER = ("zl", "y", "zh", "c")


def moved(on_z, shift):
    pairs = []
    for i in range(ZL * Y * ZH * C):
        zl, y, zh, c = i // (Y * ZH * C), i // (ZH * C) % Y, i // C % ZH, i % C
        if on_z(c):
            z = (zh * ZL + zl + shift(zl, True)) % (ZH * ZL)
            zl, zh = z % ZL, z // ZL
        else:
            y = (y + shift(y, False)) % Y
        pairs.append((i, ((zl * Y + y) * ZH + zh) * C + c))
    return pairs


def first_step(value, k):
    shift = lambda place, on_z: {1: -1, 2: 2 - 4 * (place % 2) if on_z else -2, 3: 1}[k]
    return lax.ppermute(value, GATHER, moved(lambda c: c == 1, shift))


def second_step(value, shift):
    return lax.ppermute(value, GATHER, moved(lambda c: c == 0, shift))


def mixed(value, first):
    groups = []
    for c in range(C):
        for i in range(X):
            lines = [((i, j) if (c == 0) == first else (j, i)) for j in range(Y)]
            groups.append([(y * X + x) * C + c for y, x in lines])
    return lax.all_to_all(value, ("y", "x", "c"), 0, 0, axis_index_groups=groups, tiled=True)


def shards(tokens, norm_gain, key_cotangent, secondary, master, moment_first, moment_second, signs):
    tok_rows, width = tokens.shape
    keys_w = key_cotangent.shape[1]
    c = lax.axis_index("c")
    gain = norm_gain.reshape(1, width)
    node_rows = secondary.shape[0]

    half = lax.dynamic_slice_in_dim(secondary, c * (node_rows // 2), node_rows // 2, 0)
    column = jnp.concatenate([half] + [first_step(half, k) for k in range(1, Y)], axis=0)

    part = width // X
    step = 32
    by_rows = lambda cols: pl.BlockSpec((step, cols), lambda i: (i, 0))
    send, inv = pl.pallas_call(
        norm_kernel,
        out_shape=(shape((X, tok_rows, part + keys_w), BF16), shape((tok_rows, 128), F32)),
        grid=(tok_rows // step,),
        in_specs=[by_rows(width), pl.BlockSpec((1, width), lambda i: (0, 0)), by_rows(keys_w)],
        out_specs=(pl.BlockSpec((X, step, part + keys_w), lambda i: (0, i, 0)), by_rows(128)),
        cost_estimate=pl.CostEstimate(flops=tok_rows * width * 6, bytes_accessed=5 << 20, transcendentals=0),
        compiler_params=pltpu.CompilerParams(vmem_limit_bytes=56 << 20),
    )(tokens, gain, key_cotangent)
    recv = mixed(send, True).reshape(X * tok_rows, part + keys_w)
    from_up = second_step(column, lambda place, on_z: -1)
    from_down = second_step(column, lambda place, on_z: 1)
    weights = []
    for block in (column, from_up, from_down):
        weights += [block, lax.ppermute(block, "c", ring(C, 1))]
    send = kernel_call(
        grad_kernel,
        shape((Y, part // Y, keys_w), BF16),
        0,
        1 << 20,
        1,
        40 << 20,
    )(recv)
    blocks = mixed(send, False)
    own, sib = kernel_call(
        sum_kernel,
        (shape((part // Y // C, keys_w), F32), shape((part // Y // C, keys_w), BF16)),
        0,
        1 << 20,
        1,
    )(blocks)
    from_up, from_down = weights[2], weights[4]
    rows = from_up.shape[0] // 2
    far = [
        second_step(from_up[:rows], lambda place, on_z: -1),
        second_step(from_down[rows:], lambda place, on_z: 1),
    ]
    sib, far, weights = lax.optimization_barrier((sib, far, weights))
    sib = lax.ppermute(sib, "c", ring(C, 1))
    summed = (own + sib.astype(F32)).astype(BF16)
    for block in far:
        weights += [block, lax.ppermute(block, "c", ring(C, 1))]
    blocks = lax.all_to_all(summed.reshape(ZL * ZH, ROWS, keys_w), ("zl", "zh"), 0, 0, tiled=True)
    keys, mean = kernel_call(
        keys_kernel,
        (shape((tok_rows, keys_w), BF16), shape((tok_rows, 128), F32)),
        2 * tok_rows * width * keys_w,
        11 << 20,
        4 + len(weights),
    )(tokens, gain, key_cotangent, inv, *weights)
    blocks, keys, mean = lax.optimization_barrier((blocks, keys, mean))
    new_master, new_first, new_second, new_rows = kernel_call(
        functools.partial(adam_kernel, tok_rows * math.prod(SIZES)),
        (
            shape(master.shape, F32),
            shape(moment_first.shape, F32),
            shape(moment_second.shape, F32),
            shape((X * ZH, *master.shape), BF16),
        ),
        1 << 25,
        1 << 20,
        5,
    )(blocks, moment_first, moment_second, master, signs.reshape(1, -1))

    mine = lax.all_to_all(new_rows, ("x", "zh"), 0, 0, tiled=True)
    token_grad = kernel_call(
        token_grad_kernel,
        shape(tokens.shape, BF16),
        2 * tok_rows * width * keys_w,
        13 << 20,
        5 + len(weights),
    )(tokens, gain, key_cotangent, inv, mean, *weights)
    mine, token_grad = lax.optimization_barrier((mine, token_grad))
    other = lax.ppermute(mine, "c", ring(C, 1))
    even = jnp.where(c == 0, mine, other)
    odd = jnp.where(c == 0, other, mine)
    new_secondary = jnp.stack([even, odd], axis=1).reshape(node_rows, keys_w)
    return (keys, token_grad, new_master, new_first, new_second, new_secondary)


def solution(mesh):
    fine = Mesh(mesh.devices.reshape(SIZES), AXES)
    split = P(AXES, None)
    return jax.shard_map(
        shards,
        mesh=fine,
        in_specs=(split, P(), split, P(("zl", "y"), None), split, split, split, P()),
        out_specs=(split, split, split, split, split, P(("zl", "y"), None)),
        check_vma=False,
    )
```

```python
import functools
import math

import jax
import jax.numpy as jnp
from jax import lax
from jax.experimental import pallas as pl
from jax.experimental.pallas import tpu as pltpu
from jax.sharding import Mesh
from jax.sharding import PartitionSpec as P

PAIR_GAP = 16
norm_eps = 1e-05
adam_eps = 1e-08
beta_first = 0.9
beta_second = 0.95
adam_steps = 10
learn_rate = 0.002
weight_decay = 0.1

AXES = ("zl", "y", "x", "zh", "c")
SIZES = (4, 4, 4, 2, 2)
ZL, Y, X, ZH, C = SIZES
ROWS = 32
VMEM = pl.BlockSpec(memory_space=pltpu.VMEM)
BF16 = jnp.bfloat16
F32 = jnp.float32


def shape(dims, kind):
    return jax.ShapeDtypeStruct(dims, kind)


def kernel_call(body, outs, flops, nbytes, n_in, limit=24 << 20):
    return pl.pallas_call(
        body,
        out_shape=outs,
        in_specs=[VMEM] * n_in,
        out_specs=jax.tree.map(lambda _: VMEM, outs),
        cost_estimate=pl.CostEstimate(flops=flops, bytes_accessed=nbytes, transcendentals=0),
        compiler_params=pltpu.CompilerParams(vmem_limit_bytes=limit),
    )


def norm_kernel(tok_ref, gain_ref, cot_ref, send_ref, inv_ref):
    c = lax.axis_index("c")
    rows, width = tok_ref.shape
    step = X * ZH * C * ROWS
    acc = jnp.zeros((rows, step), F32)
    for k in range(width // step):
        t = tok_ref[:, k * step : (k + 1) * step].astype(F32)
        acc = acc + t * t
    inv = lax.rsqrt(jnp.sum(acc, axis=-1, keepdims=True) / width + norm_eps)
    inv = jnp.broadcast_to(inv, inv_ref.shape)
    inv_ref[...] = inv
    part = ZH * C * ROWS
    stride_p, stride_q = jnp.where(c == 0, part, step), jnp.where(c == 0, step, part)
    for zl in range(ZL):
        for p in range(X):
            for q in range(Y):
                at = pl.multiple_of(zl * Y * step + p * stride_p + q * stride_q, part)
                cols = pl.ds(at, part)
                normed = tok_ref[:, cols].astype(F32) * inv
                to = (zl * Y + q) * part
                send_ref[p, :, to : to + part] = (normed * gain_ref[:, cols]).astype(BF16)
    for p in range(X):
        send_ref[p, :, ZL * Y * part :] = cot_ref[...]


def grad_kernel(recv_ref, send_ref):
    part = ZH * C * ROWS
    cols = ZL * Y * part
    cot = recv_ref[:, cols:]
    for zl in range(ZL):
        block = recv_ref[:, zl * Y * part : (zl + 1) * Y * part]
        grad = lax.dot_general(block, cot, (((0,), (0,)), ((), ())), preferred_element_type=F32)
        grad = grad.astype(BF16)
        for q in range(Y):
            for zh in range(ZH):
                for c in range(C):
                    at = q * part + (zh * C + c) * ROWS
                    to = ((c * ZL + zl) * ZH + zh) * ROWS
                    send_ref[q, to : to + ROWS, :] = grad[at : at + ROWS]


def sum_kernel(recv_ref, own_ref, sib_ref):
    c = lax.axis_index("c")
    rows = own_ref.shape[0]
    for ref, core in ((sib_ref, 1 - c), (own_ref, c)):
        part = recv_ref[:, pl.ds(pl.multiple_of(core * rows, rows), rows), :].astype(F32)
        ref[...] = jnp.sum(part, axis=0).astype(ref.dtype)


def places(width, refs):
    c, zl, y = (lax.axis_index(name) for name in ("c", "zl", "y"))
    step = width // (ZL * Y)
    half = step // 2
    for s, off in enumerate((0, 1, 3, 2)):
        for h in range(C):
            for k in range(Y):
                core = c if h == 0 else 1 - c
                on_zl, on_y = jnp.where(core == 0, off, k), jnp.where(core == 0, k, off)
                node = lax.rem(zl + on_zl, ZL) * Y + lax.rem(y + on_y, Y)
                at = pl.multiple_of(node * step + core * half, half)
                ref, row = (refs[2 * s + h], k) if s < 3 else (refs[2 * (s + k // 2) + h], k % 2)
                yield pl.ds(at, half), ref[row * half : (row + 1) * half, :]


def widened(ref, cols):
    return jnp.concatenate([ref[...]] * (cols // ref.shape[1]), axis=1)


def keys_kernel(tok_ref, gain_ref, cot_ref, inv_ref, *refs):
    refs, (keys_ref, mean_ref) = refs[:-2], refs[-2:]
    width = tok_ref.shape[1]
    inv = widened(inv_ref, width // (ZL * Y * C))
    keys = jnp.zeros(keys_ref.shape, F32)
    for cols, weights in places(width, refs):
        normed = tok_ref[:, cols].astype(F32) * inv
        hidden = (normed * gain_ref[:, cols]).astype(BF16)
        keys = keys + jnp.dot(hidden, weights, preferred_element_type=F32)
    keys_ref[...] = keys.astype(BF16)
    mean = jnp.sum(cot_ref[...].astype(F32) * keys, axis=-1, keepdims=True) / width
    mean_ref[...] = jnp.broadcast_to(mean, mean_ref.shape)


def token_grad_kernel(tok_ref, gain_ref, cot_ref, inv_ref, mean_ref, *refs):
    refs, (tg_ref,) = refs[:-1], refs[-1:]
    width = tok_ref.shape[1]
    inv = widened(inv_ref, width // (ZL * Y * C))
    mean = widened(mean_ref, width // (ZL * Y * C))
    cot = cot_ref[...]
    for cols, weights in places(width, refs):
        hidden_grad = lax.dot_general(cot, weights, (((1,), (1,)), ((), ())), preferred_element_type=F32)
        normed = tok_ref[:, cols].astype(F32) * inv
        tg_ref[:, cols] = (inv * (hidden_grad * gain_ref[:, cols] - normed * mean)).astype(BF16)


def hadamard(value, extent=128):
    rows, width = value.shape
    i = lax.broadcasted_iota(jnp.int32, (extent, extent), 0)
    j = lax.broadcasted_iota(jnp.int32, (extent, extent), 1)
    both = i & j
    both = both ^ (both >> 4)
    both = both ^ (both >> 2)
    both = both ^ (both >> 1)
    table = (1 - 2 * (both & 1)).astype(F32).astype(BF16)
    parts = []
    for k in range(width // extent):
        rest = value[:, k * extent : (k + 1) * extent]
        for _ in range(3):
            top = rest.astype(BF16)
            parts.append(top)
            rest = rest - top.astype(F32)
    out = jnp.dot(jnp.concatenate(parts, axis=0), table, preferred_element_type=F32)
    p = []
    for k in range(width // extent):
        at = 3 * k * rows
        p.append((out[at + 2 * rows : at + 3 * rows] + out[at + rows : at + 2 * rows]) + out[at : at + rows])
    s, t, u, v = p[0] + p[1], p[0] - p[1], p[2] + p[3], p[2] - p[3]
    return jnp.concatenate([s + u, t + v, s - u, t - v], axis=1)


def adam_kernel(tokens_all, recv_ref, first_ref, second_ref, master_ref, signs_ref, nm_ref, nf_ref, ns_ref, new_ref):
    total = jnp.sum(recv_ref[...].astype(F32), axis=0)
    half = total.shape[1]
    root = math.sqrt(2 * half)
    sign = (1 - 2 * signs_ref[...]).astype(F32)
    sign0, sign1 = sign[:, :half], sign[:, half:]
    gap = PAIR_GAP
    spun = hadamard(jnp.concatenate([total[:gap] * sign0, total[gap:] * sign1], axis=0)) * (1.0 / (root * tokens_all))
    q0, q1 = spun[:gap], spun[gap:]
    coded = jnp.concatenate([q0 + q1, q0 - q1], axis=1)
    new_first = beta_first * first_ref[...] + (1.0 - beta_first) * coded
    new_second = beta_second * second_ref[...] + (1.0 - beta_second) * coded * coded
    nf_ref[...] = new_first
    ns_ref[...] = new_second
    first_hat = new_first / (1.0 - beta_first**adam_steps)
    second_hat = new_second / (1.0 - beta_second**adam_steps)
    ratio = first_hat / (jnp.sqrt(second_hat) + adam_eps)
    lower, upper = ratio[:, :half], ratio[:, half:]
    back = hadamard(jnp.concatenate([lower + upper, lower - upper], axis=0)) / root
    update = jnp.concatenate([back[:gap] * sign0, back[gap:] * sign1], axis=0)
    master = master_ref[...]
    new_master = master - learn_rate * (update + weight_decay * master)
    nm_ref[...] = new_master
    new_ref[...] = jnp.broadcast_to(new_master.astype(BF16), new_ref.shape)


def ring(n, s):
    return [(i, (i + s) % n) for i in range(n)]


GATHER = ("zl", "y", "zh", "c")


def moved(on_z, shift):
    pairs = []
    for i in range(ZL * Y * ZH * C):
        zl, y, zh, c = i // (Y * ZH * C), i // (ZH * C) % Y, i // C % ZH, i % C
        if on_z(c):
            z = (zh * ZL + zl + shift(zl, True)) % (ZH * ZL)
            zl, zh = z % ZL, z // ZL
        else:
            y = (y + shift(y, False)) % Y
        pairs.append((i, ((zl * Y + y) * ZH + zh) * C + c))
    return pairs


def first_step(value, k):
    shift = lambda place, on_z: {1: -1, 2: 2 - 4 * (place % 2) if on_z else -2, 3: 1}[k]
    return lax.ppermute(value, GATHER, moved(lambda c: c == 1, shift))


def second_step(value, shift):
    return lax.ppermute(value, GATHER, moved(lambda c: c == 0, shift))


def mixed(value, first):
    groups = []
    for c in range(C):
        for i in range(X):
            lines = [((i, j) if (c == 0) == first else (j, i)) for j in range(Y)]
            groups.append([(y * X + x) * C + c for y, x in lines])
    return lax.all_to_all(value, ("y", "x", "c"), 0, 0, axis_index_groups=groups, tiled=True)


def shards(tokens, norm_gain, key_cotangent, secondary, master, moment_first, moment_second, signs):
    tok_rows, width = tokens.shape
    keys_w = key_cotangent.shape[1]
    c = lax.axis_index("c")
    gain = norm_gain.reshape(1, width)
    node_rows = secondary.shape[0]

    half = lax.dynamic_slice_in_dim(secondary, c * (node_rows // 2), node_rows // 2, 0)
    column = jnp.concatenate([half] + [first_step(half, k) for k in range(1, Y)], axis=0)

    part = width // X
    step = 64
    by_rows = lambda cols: pl.BlockSpec((step, cols), lambda i: (i, 0))
    send, inv = pl.pallas_call(
        norm_kernel,
        out_shape=(shape((X, tok_rows, part + keys_w), BF16), shape((tok_rows, 128), F32)),
        grid=(tok_rows // step,),
        in_specs=[by_rows(width), pl.BlockSpec((1, width), lambda i: (0, 0)), by_rows(keys_w)],
        out_specs=(pl.BlockSpec((X, step, part + keys_w), lambda i: (0, i, 0)), by_rows(128)),
        cost_estimate=pl.CostEstimate(flops=tok_rows * width * 6, bytes_accessed=5 << 20, transcendentals=0),
        compiler_params=pltpu.CompilerParams(vmem_limit_bytes=56 << 20),
    )(tokens, gain, key_cotangent)
    recv = mixed(send, True).reshape(X * tok_rows, part + keys_w)
    from_up = second_step(column, lambda place, on_z: -1)
    from_down = second_step(column, lambda place, on_z: 1)
    weights = []
    for block in (column, from_up, from_down):
        weights += [block, lax.ppermute(block, "c", ring(C, 1))]
    send = kernel_call(
        grad_kernel,
        shape((Y, part // Y, keys_w), BF16),
        0,
        1 << 20,
        1,
        40 << 20,
    )(recv)
    blocks = mixed(send, False)
    own, sib = kernel_call(
        sum_kernel,
        (shape((part // Y // C, keys_w), F32), shape((part // Y // C, keys_w), BF16)),
        0,
        1 << 20,
        1,
    )(blocks)
    from_up, from_down = weights[2], weights[4]
    rows = from_up.shape[0] // 2
    far = [
        second_step(from_up[:rows], lambda place, on_z: -1),
        second_step(from_down[rows:], lambda place, on_z: 1),
    ]
    sib, weights = lax.optimization_barrier((sib, weights))
    sib = lax.ppermute(sib, "c", ring(C, 1))
    summed = (own + sib.astype(F32)).astype(BF16)
    summed, far = lax.optimization_barrier((summed, far))
    for block in far:
        weights += [block, lax.ppermute(block, "c", ring(C, 1))]
    blocks = lax.all_to_all(summed.reshape(ZL * ZH, ROWS, keys_w), ("zl", "zh"), 0, 0, tiled=True)
    keys, mean = kernel_call(
        keys_kernel,
        (shape((tok_rows, keys_w), BF16), shape((tok_rows, 128), F32)),
        2 * tok_rows * width * keys_w,
        11 << 20,
        4 + len(weights),
        60 << 20,
    )(tokens, gain, key_cotangent, inv, *weights)
    blocks, keys, mean = lax.optimization_barrier((blocks, keys, mean))
    new_master, new_first, new_second, new_rows = kernel_call(
        functools.partial(adam_kernel, tok_rows * math.prod(SIZES)),
        (
            shape(master.shape, F32),
            shape(moment_first.shape, F32),
            shape(moment_second.shape, F32),
            shape((X * ZH, *master.shape), BF16),
        ),
        1 << 25,
        1 << 20,
        5,
        60 << 20,
    )(blocks, moment_first, moment_second, master, signs.reshape(1, -1))

    mine = lax.all_to_all(new_rows, ("x", "zh"), 0, 0, tiled=True)
    token_grad = kernel_call(
        token_grad_kernel,
        shape(tokens.shape, BF16),
        2 * tok_rows * width * keys_w,
        13 << 20,
        5 + len(weights),
        60 << 20,
    )(tokens, gain, key_cotangent, inv, mean, *weights)
    mine, token_grad = lax.optimization_barrier((mine, token_grad))
    other = lax.ppermute(mine, "c", ring(C, 1))
    even = jnp.where(c == 0, mine, other)
    odd = jnp.where(c == 0, other, mine)
    new_secondary = jnp.stack([even, odd], axis=1).reshape(node_rows, keys_w)
    return (keys, token_grad, new_master, new_first, new_second, new_secondary)


def solution(mesh):
    fine = Mesh(mesh.devices.reshape(SIZES), AXES)
    split = P(AXES, None)
    return jax.shard_map(
        shards,
        mesh=fine,
        in_specs=(split, P(), split, P(("zl", "y"), None), split, split, split, P()),
        out_specs=(split, split, split, split, split, P(("zl", "y"), None)),
        check_vma=False,
    )
```

```python
import functools
import math

import jax
import jax.numpy as jnp
from jax import lax
from jax.experimental import pallas as pl
from jax.experimental.pallas import tpu as pltpu
from jax.sharding import Mesh
from jax.sharding import PartitionSpec as P

PAIR_GAP = 16
norm_eps = 1e-05
adam_eps = 1e-08
beta_first = 0.9
beta_second = 0.95
adam_steps = 10
learn_rate = 0.002
weight_decay = 0.1

AXES = ("zl", "y", "x", "zh", "c")
SIZES = (4, 4, 4, 2, 2)
ZL, Y, X, ZH, C = SIZES
ROWS = 32
VMEM = pl.BlockSpec(memory_space=pltpu.VMEM)
HBM = pl.BlockSpec(memory_space=pltpu.HBM)
BF16 = jnp.bfloat16
F32 = jnp.float32


def shape(dims, kind):
    return jax.ShapeDtypeStruct(dims, kind)


def kernel_call(body, outs, flops, nbytes, in_specs, limit=24 << 20, out_specs=None, scratch=()):
    return pl.pallas_call(
        body,
        out_shape=outs,
        in_specs=[VMEM] * in_specs if isinstance(in_specs, int) else in_specs,
        out_specs=jax.tree.map(lambda _: VMEM, outs) if out_specs is None else out_specs,
        scratch_shapes=list(scratch),
        cost_estimate=pl.CostEstimate(flops=flops, bytes_accessed=nbytes, transcendentals=0),
        compiler_params=pltpu.CompilerParams(vmem_limit_bytes=limit),
    )


def norm_kernel(tok_ref, gain_ref, cot_ref, send_ref, inv_ref):
    c = lax.axis_index("c")
    rows, width = tok_ref.shape
    step = X * ZH * C * ROWS
    acc = jnp.zeros((rows, step), F32)
    for k in range(width // step):
        t = tok_ref[:, k * step : (k + 1) * step].astype(F32)
        acc = acc + t * t
    inv = lax.rsqrt(jnp.sum(acc, axis=-1, keepdims=True) / width + norm_eps)
    inv = jnp.broadcast_to(inv, inv_ref.shape)
    inv_ref[...] = inv
    part = ZH * C * ROWS
    stride_p, stride_q = jnp.where(c == 0, part, step), jnp.where(c == 0, step, part)
    for zl in range(ZL):
        for p in range(X):
            for q in range(Y):
                at = pl.multiple_of(zl * Y * step + p * stride_p + q * stride_q, part)
                cols = pl.ds(at, part)
                normed = tok_ref[:, cols].astype(F32) * inv
                to = (zl * Y + q) * part
                send_ref[p, :, to : to + part] = (normed * gain_ref[:, cols]).astype(BF16)
    for p in range(X):
        send_ref[p, :, ZL * Y * part :] = cot_ref[...]


def grad_kernel(recv_ref, send_ref, buf_ref, sem):
    part = ZH * C * ROWS
    cols = ZL * Y * part
    cot = recv_ref[:, cols:]
    copies = []
    for zl in range(ZL):
        block = recv_ref[:, zl * Y * part : (zl + 1) * Y * part]
        grad = lax.dot_general(block, cot, (((0,), (0,)), ((), ())), preferred_element_type=F32)
        grad = grad.astype(BF16)
        for q in range(Y):
            for zh in range(ZH):
                for c in range(C):
                    at = q * part + (zh * C + c) * ROWS
                    to = (c * ZH + zh) * ROWS
                    buf_ref[zl, q, to : to + ROWS, :] = grad[at : at + ROWS]
        rows = slice(zl * part, (zl + 1) * part)
        copy = pltpu.make_async_copy(buf_ref.at[zl], send_ref.at[:, rows, :], sem.at[zl])
        copy.start()
        copies.append(copy)
    for copy in copies:
        copy.wait()


def sum_kernel(recv_ref, own_ref, sib_ref):
    c = lax.axis_index("c")
    rows = ZH * ROWS
    for ref, core in ((sib_ref, 1 - c), (own_ref, c)):
        for zl in range(ZL):
            at = pl.multiple_of(zl * C * rows + core * rows, rows)
            part = recv_ref[:, pl.ds(at, rows), :].astype(F32)
            ref[zl * rows : (zl + 1) * rows, :] = jnp.sum(part, axis=0).astype(ref.dtype)


def halves_kernel(up_ref, down_ref, a_ref, b_ref, sem):
    rows = a_ref.shape[0]
    copies = (
        pltpu.make_async_copy(up_ref.at[0:rows, :], a_ref, sem.at[0]),
        pltpu.make_async_copy(down_ref.at[rows : 2 * rows, :], b_ref, sem.at[1]),
    )
    for copy in copies:
        copy.start()
    for copy in copies:
        copy.wait()


def places(width, refs, bufs, sem):
    c, zl, y = (lax.axis_index(name) for name in ("c", "zl", "y"))
    step = width // (ZL * Y)
    half = step // 2
    copies = [pltpu.make_async_copy(ref, buf, sem.at[i]) for i, (ref, buf) in enumerate(zip(refs, bufs))]
    for copy in copies:
        copy.start()
    for i, buf in enumerate(bufs):
        copies[i].wait()
        off = (0, 1, 3)[i // 2] if i < 6 else 2
        core = c if i % 2 == 0 else 1 - c
        for row in range(buf.shape[0] // half):
            k = row if i < 6 else row + 2 * ((i - 6) // 2)
            on_zl, on_y = jnp.where(core == 0, off, k), jnp.where(core == 0, k, off)
            node = lax.rem(zl + on_zl, ZL) * Y + lax.rem(y + on_y, Y)
            at = pl.multiple_of(node * step + core * half, half)
            yield pl.ds(at, half), buf[row * half : (row + 1) * half, :]


def widened(ref, cols):
    return jnp.concatenate([ref[...]] * (cols // ref.shape[1]), axis=1)


def keys_kernel(blocks, tok_ref, gain_ref, cot_ref, inv_ref, *refs):
    w_refs, (keys_ref, mean_ref), bufs, sem = refs[:blocks], refs[blocks : blocks + 2], refs[blocks + 2 : -1], refs[-1]
    width = tok_ref.shape[1]
    inv = widened(inv_ref, width // (ZL * Y * C))
    keys = jnp.zeros(keys_ref.shape, F32)
    for cols, weights in places(width, w_refs, bufs, sem):
        normed = tok_ref[:, cols].astype(F32) * inv
        hidden = (normed * gain_ref[:, cols]).astype(BF16)
        keys = keys + jnp.dot(hidden, weights, preferred_element_type=F32)
    keys_ref[...] = keys.astype(BF16)
    mean = jnp.sum(cot_ref[...].astype(F32) * keys, axis=-1, keepdims=True) / width
    mean_ref[...] = jnp.broadcast_to(mean, mean_ref.shape)


def token_grad_kernel(blocks, tok_ref, gain_ref, cot_ref, inv_ref, mean_ref, *refs):
    w_refs, tg_ref, bufs, sem = refs[:blocks], refs[blocks], refs[blocks + 1 : -1], refs[-1]
    width = tok_ref.shape[1]
    inv = widened(inv_ref, width // (ZL * Y * C))
    mean = widened(mean_ref, width // (ZL * Y * C))
    cot = cot_ref[...]
    for cols, weights in places(width, w_refs, bufs, sem):
        hidden_grad = lax.dot_general(cot, weights, (((1,), (1,)), ((), ())), preferred_element_type=F32)
        normed = tok_ref[:, cols].astype(F32) * inv
        tg_ref[:, cols] = (inv * (hidden_grad * gain_ref[:, cols] - normed * mean)).astype(BF16)


def hadamard(value, extent=128):
    rows, width = value.shape
    i = lax.broadcasted_iota(jnp.int32, (extent, extent), 0)
    j = lax.broadcasted_iota(jnp.int32, (extent, extent), 1)
    both = i & j
    both = both ^ (both >> 4)
    both = both ^ (both >> 2)
    both = both ^ (both >> 1)
    table = (1 - 2 * (both & 1)).astype(F32).astype(BF16)
    parts = []
    for k in range(width // extent):
        rest = value[:, k * extent : (k + 1) * extent]
        for _ in range(3):
            top = rest.astype(BF16)
            parts.append(top)
            rest = rest - top.astype(F32)
    out = jnp.dot(jnp.concatenate(parts, axis=0), table, preferred_element_type=F32)
    p = []
    for k in range(width // extent):
        at = 3 * k * rows
        p.append((out[at + 2 * rows : at + 3 * rows] + out[at + rows : at + 2 * rows]) + out[at : at + rows])
    s, t, u, v = p[0] + p[1], p[0] - p[1], p[2] + p[3], p[2] - p[3]
    return jnp.concatenate([s + u, t + v, s - u, t - v], axis=1)


def adam_kernel(tokens_all, recv_ref, first_ref, second_ref, master_ref, signs_ref, nm_ref, nf_ref, ns_ref, new_ref):
    total = jnp.sum(recv_ref[...].astype(F32), axis=0)
    half = total.shape[1]
    root = math.sqrt(2 * half)
    sign = (1 - 2 * signs_ref[...]).astype(F32)
    sign0, sign1 = sign[:, :half], sign[:, half:]
    gap = PAIR_GAP
    spun = hadamard(jnp.concatenate([total[:gap] * sign0, total[gap:] * sign1], axis=0)) * (1.0 / (root * tokens_all))
    q0, q1 = spun[:gap], spun[gap:]
    coded = jnp.concatenate([q0 + q1, q0 - q1], axis=1)
    new_first = beta_first * first_ref[...] + (1.0 - beta_first) * coded
    new_second = beta_second * second_ref[...] + (1.0 - beta_second) * coded * coded
    nf_ref[...] = new_first
    ns_ref[...] = new_second
    first_hat = new_first / (1.0 - beta_first**adam_steps)
    second_hat = new_second / (1.0 - beta_second**adam_steps)
    ratio = first_hat / (jnp.sqrt(second_hat) + adam_eps)
    lower, upper = ratio[:, :half], ratio[:, half:]
    back = hadamard(jnp.concatenate([lower + upper, lower - upper], axis=0)) / root
    update = jnp.concatenate([back[:gap] * sign0, back[gap:] * sign1], axis=0)
    master = master_ref[...]
    new_master = master - learn_rate * (update + weight_decay * master)
    nm_ref[...] = new_master
    new_ref[...] = jnp.broadcast_to(new_master.astype(BF16), new_ref.shape)


def ring(n, s):
    return [(i, (i + s) % n) for i in range(n)]


GATHER = ("zl", "y", "zh", "c")


def moved(on_z, shift):
    pairs = []
    for i in range(ZL * Y * ZH * C):
        zl, y, zh, c = i // (Y * ZH * C), i // (ZH * C) % Y, i // C % ZH, i % C
        if on_z(c):
            z = (zh * ZL + zl + shift(zl, True)) % (ZH * ZL)
            zl, zh = z % ZL, z // ZL
        else:
            y = (y + shift(y, False)) % Y
        pairs.append((i, ((zl * Y + y) * ZH + zh) * C + c))
    return pairs


def first_step(value, k):
    shift = lambda place, on_z: {1: -1, 2: 2 - 4 * (place % 2) if on_z else -2, 3: 1}[k]
    return lax.ppermute(value, GATHER, moved(lambda c: c == 1, shift))


def second_step(value, shift):
    return lax.ppermute(value, GATHER, moved(lambda c: c == 0, shift))


def mixed(value, first):
    groups = []
    for c in range(C):
        for i in range(X):
            lines = [((i, j) if (c == 0) == first else (j, i)) for j in range(Y)]
            groups.append([(y * X + x) * C + c for y, x in lines])
    return lax.all_to_all(value, ("y", "x", "c"), 0, 0, axis_index_groups=groups, tiled=True)


def shards(tokens, norm_gain, key_cotangent, secondary, master, moment_first, moment_second, signs):
    tok_rows, width = tokens.shape
    keys_w = key_cotangent.shape[1]
    c = lax.axis_index("c")
    gain = norm_gain.reshape(1, width)
    node_rows = secondary.shape[0]

    half = lax.dynamic_slice_in_dim(secondary, c * (node_rows // 2), node_rows // 2, 0)
    column = jnp.concatenate([half] + [first_step(half, k) for k in range(1, Y)], axis=0)

    part = width // X
    step = 64
    by_rows = lambda cols: pl.BlockSpec((step, cols), lambda i: (i, 0))
    send, inv = pl.pallas_call(
        norm_kernel,
        out_shape=(shape((X, tok_rows, part + keys_w), BF16), shape((tok_rows, 128), F32)),
        grid=(tok_rows // step,),
        in_specs=[by_rows(width), pl.BlockSpec((1, width), lambda i: (0, 0)), by_rows(keys_w)],
        out_specs=(pl.BlockSpec((X, step, part + keys_w), lambda i: (0, i, 0)), by_rows(128)),
        cost_estimate=pl.CostEstimate(flops=tok_rows * width * 6, bytes_accessed=5 << 20, transcendentals=0),
        compiler_params=pltpu.CompilerParams(vmem_limit_bytes=56 << 20),
    )(tokens, gain, key_cotangent)
    recv = mixed(send, True).reshape(X * tok_rows, part + keys_w)
    from_up = second_step(column, lambda place, on_z: -1)
    from_down = second_step(column, lambda place, on_z: 1)
    weights = []
    for block in (column, from_up, from_down):
        weights += [block, lax.ppermute(block, "c", ring(C, 1))]
    send = kernel_call(
        grad_kernel,
        pltpu.HBM((Y, part // Y, keys_w), BF16),
        0,
        1 << 20,
        1,
        40 << 20,
        HBM,
        (pltpu.VMEM((ZL, Y, ZH * C * ROWS, keys_w), BF16), pltpu.SemaphoreType.DMA((ZL,))),
    )(recv)
    blocks = mixed(send, False)
    own, sib = kernel_call(
        sum_kernel,
        (shape((part // Y // C, keys_w), F32), shape((part // Y // C, keys_w), BF16)),
        0,
        1 << 20,
        1,
    )(blocks)
    from_up, from_down = weights[2], weights[4]
    rows = from_up.shape[0] // 2
    far_a, far_b = kernel_call(
        halves_kernel,
        (shape((rows, keys_w), BF16),) * 2,
        0,
        1 << 20,
        [HBM, HBM],
        60 << 20,
        (HBM, HBM),
        (pltpu.SemaphoreType.DMA((2,)),),
    )(from_up, from_down)
    far = [
        second_step(far_a, lambda place, on_z: -1),
        second_step(far_b, lambda place, on_z: 1),
    ]
    sib, weights = lax.optimization_barrier((sib, weights))
    sib = lax.ppermute(sib, "c", ring(C, 1))
    summed = (own + sib.astype(F32)).astype(BF16)
    summed, far = lax.optimization_barrier((summed, far))
    for block in far:
        weights += [block, lax.ppermute(block, "c", ring(C, 1))]
    blocks = lax.all_to_all(summed.reshape(ZL * ZH, ROWS, keys_w), ("zl", "zh"), 0, 0, tiled=True)
    count = len(weights)
    scratch = [pltpu.VMEM(block.shape, BF16) for block in weights] + [pltpu.SemaphoreType.DMA((count,))]
    keys, mean = kernel_call(
        functools.partial(keys_kernel, count),
        (shape((tok_rows, keys_w), BF16), shape((tok_rows, 128), F32)),
        2 * tok_rows * width * keys_w,
        11 << 20,
        [VMEM] * 4 + [HBM] * count,
        60 << 20,
        scratch=scratch,
    )(tokens, gain, key_cotangent, inv, *weights)
    blocks, keys, mean = lax.optimization_barrier((blocks, keys, mean))
    new_master, new_first, new_second, new_rows = kernel_call(
        functools.partial(adam_kernel, tok_rows * math.prod(SIZES)),
        (
            shape(master.shape, F32),
            shape(moment_first.shape, F32),
            shape(moment_second.shape, F32),
            shape((X * ZH, *master.shape), BF16),
        ),
        1 << 25,
        1 << 20,
        5,
        60 << 20,
    )(blocks, moment_first, moment_second, master, signs.reshape(1, -1))

    mine = lax.all_to_all(new_rows, ("x", "zh"), 0, 0, tiled=True)
    token_grad = kernel_call(
        functools.partial(token_grad_kernel, count),
        shape(tokens.shape, BF16),
        2 * tok_rows * width * keys_w,
        13 << 20,
        [VMEM] * 5 + [HBM] * count,
        60 << 20,
        scratch=scratch,
    )(tokens, gain, key_cotangent, inv, mean, *weights)
    mine, token_grad = lax.optimization_barrier((mine, token_grad))
    other = lax.ppermute(mine, "c", ring(C, 1))
    even = jnp.where(c == 0, mine, other)
    odd = jnp.where(c == 0, other, mine)
    new_secondary = jnp.stack([even, odd], axis=1).reshape(node_rows, keys_w)
    return (keys, token_grad, new_master, new_first, new_second, new_secondary)


def solution(mesh):
    fine = Mesh(mesh.devices.reshape(SIZES), AXES)
    split = P(AXES, None)
    return jax.shard_map(
        shards,
        mesh=fine,
        in_specs=(split, P(), split, P(("zl", "y"), None), split, split, split, P()),
        out_specs=(split, split, split, split, split, P(("zl", "y"), None)),
        check_vma=False,
    )
```

```python
import functools
import math

import jax
import jax.numpy as jnp
from jax import lax
from jax.experimental import pallas as pl
from jax.experimental.pallas import tpu as pltpu
from jax.sharding import Mesh
from jax.sharding import PartitionSpec as P

PAIR_GAP = 16
norm_eps = 1e-05
adam_eps = 1e-08
beta_first = 0.9
beta_second = 0.95
adam_steps = 10
learn_rate = 0.002
weight_decay = 0.1

AXES = ("zl", "y", "x", "zh", "c")
SIZES = (4, 4, 4, 2, 2)
ZL, Y, X, ZH, C = SIZES
ROWS = 32
VMEM = pl.BlockSpec(memory_space=pltpu.VMEM)
HBM = pl.BlockSpec(memory_space=pltpu.HBM)
BF16 = jnp.bfloat16
F32 = jnp.float32


def shape(dims, kind):
    return jax.ShapeDtypeStruct(dims, kind)


def kernel_call(body, outs, flops, nbytes, in_specs, limit=24 << 20, out_specs=None, scratch=()):
    return pl.pallas_call(
        body,
        out_shape=outs,
        in_specs=[VMEM] * in_specs if isinstance(in_specs, int) else in_specs,
        out_specs=jax.tree.map(lambda _: VMEM, outs) if out_specs is None else out_specs,
        scratch_shapes=list(scratch),
        cost_estimate=pl.CostEstimate(flops=flops, bytes_accessed=nbytes, transcendentals=0),
        compiler_params=pltpu.CompilerParams(vmem_limit_bytes=limit),
    )


def norm_kernel(tok_ref, gain_ref, cot_ref, send_ref, inv_ref):
    c = lax.axis_index("c")
    rows, width = tok_ref.shape
    step = X * ZH * C * ROWS
    acc = jnp.zeros((rows, step), F32)
    for k in range(width // step):
        t = tok_ref[:, k * step : (k + 1) * step].astype(F32)
        acc = acc + t * t
    inv = lax.rsqrt(jnp.sum(acc, axis=-1, keepdims=True) / width + norm_eps)
    inv = jnp.broadcast_to(inv, inv_ref.shape)
    inv_ref[...] = inv
    part = ZH * C * ROWS
    stride_p, stride_q = jnp.where(c == 0, part, step), jnp.where(c == 0, step, part)
    for zl in range(ZL):
        for p in range(X):
            for q in range(Y):
                at = pl.multiple_of(zl * Y * step + p * stride_p + q * stride_q, part)
                cols = pl.ds(at, part)
                normed = tok_ref[:, cols].astype(F32) * inv
                to = (zl * Y + q) * part
                send_ref[p, :, to : to + part] = (normed * gain_ref[:, cols]).astype(BF16)
    for p in range(X):
        send_ref[p, :, ZL * Y * part :] = cot_ref[...]


def grad_kernel(recv_ref, send_ref, buf_ref, sem):
    part = ZH * C * ROWS
    cols = ZL * Y * part
    cot = recv_ref[:, cols:]
    copies = []
    for zl in range(ZL):
        block = recv_ref[:, zl * Y * part : (zl + 1) * Y * part]
        grad = lax.dot_general(block, cot, (((0,), (0,)), ((), ())), preferred_element_type=F32)
        grad = grad.astype(BF16)
        for q in range(Y):
            for zh in range(ZH):
                for c in range(C):
                    at = q * part + (zh * C + c) * ROWS
                    to = (c * ZH + zh) * ROWS
                    buf_ref[zl, q, to : to + ROWS, :] = grad[at : at + ROWS]
        rows = slice(zl * part, (zl + 1) * part)
        copy = pltpu.make_async_copy(buf_ref.at[zl], send_ref.at[:, rows, :], sem.at[zl])
        copy.start()
        copies.append(copy)
    for copy in copies:
        copy.wait()


def sum_kernel(recv_ref, own_ref, sib_ref):
    c = lax.axis_index("c")
    rows = ZH * ROWS
    for ref, core in ((sib_ref, 1 - c), (own_ref, c)):
        for zl in range(ZL):
            at = pl.multiple_of(zl * C * rows + core * rows, rows)
            part = recv_ref[:, pl.ds(at, rows), :].astype(F32)
            ref[zl * rows : (zl + 1) * rows, :] = jnp.sum(part, axis=0).astype(ref.dtype)


def halves_kernel(up_ref, down_ref, a_ref, b_ref, sem):
    rows = a_ref.shape[0]
    copies = (
        pltpu.make_async_copy(up_ref.at[0:rows, :], a_ref, sem.at[0]),
        pltpu.make_async_copy(down_ref.at[rows : 2 * rows, :], b_ref, sem.at[1]),
    )
    for copy in copies:
        copy.start()
    for copy in copies:
        copy.wait()


def places(width, refs, bufs, sem):
    c, zl, y = (lax.axis_index(name) for name in ("c", "zl", "y"))
    step = width // (ZL * Y)
    half = step // 2
    copies = [pltpu.make_async_copy(ref, buf, sem.at[i]) for i, (ref, buf) in enumerate(zip(refs, bufs))]
    for copy in copies:
        copy.start()
    for i, buf in enumerate(bufs):
        copies[i].wait()
        off = (0, 1, 3)[i // 2] if i < 6 else 2
        core = c if i % 2 == 0 else 1 - c
        for row in range(buf.shape[0] // half):
            k = row if i < 6 else row + 2 * ((i - 6) // 2)
            on_zl, on_y = jnp.where(core == 0, off, k), jnp.where(core == 0, k, off)
            node = lax.rem(zl + on_zl, ZL) * Y + lax.rem(y + on_y, Y)
            at = pl.multiple_of(node * step + core * half, half)
            yield pl.ds(at, half), buf[row * half : (row + 1) * half, :]


def widened(ref, cols):
    return jnp.concatenate([ref[...]] * (cols // ref.shape[1]), axis=1)


def keys_kernel(blocks, tok_ref, gain_ref, cot_ref, inv_ref, *refs):
    w_refs, (keys_ref, mean_ref), bufs, sem = refs[:blocks], refs[blocks : blocks + 2], refs[blocks + 2 : -1], refs[-1]
    width = tok_ref.shape[1]
    inv = widened(inv_ref, width // (ZL * Y * C))
    keys = jnp.zeros(keys_ref.shape, F32)
    for cols, weights in places(width, w_refs, bufs, sem):
        normed = tok_ref[:, cols].astype(F32) * inv
        hidden = (normed * gain_ref[:, cols]).astype(BF16)
        keys = keys + jnp.dot(hidden, weights, preferred_element_type=F32)
    keys_ref[...] = keys.astype(BF16)
    mean = jnp.sum(cot_ref[...].astype(F32) * keys, axis=-1, keepdims=True) / width
    mean_ref[...] = jnp.broadcast_to(mean, mean_ref.shape)


def token_grad_kernel(blocks, tok_ref, gain_ref, cot_ref, inv_ref, mean_ref, *refs):
    w_refs, tg_ref, bufs, sem = refs[:blocks], refs[blocks], refs[blocks + 1 : -1], refs[-1]
    width = tok_ref.shape[1]
    inv = widened(inv_ref, width // (ZL * Y * C))
    mean = widened(mean_ref, width // (ZL * Y * C))
    cot = cot_ref[...]
    for cols, weights in places(width, w_refs, bufs, sem):
        hidden_grad = lax.dot_general(cot, weights, (((1,), (1,)), ((), ())), preferred_element_type=F32)
        normed = tok_ref[:, cols].astype(F32) * inv
        tg_ref[:, cols] = (inv * (hidden_grad * gain_ref[:, cols] - normed * mean)).astype(BF16)


def hadamard(value, extent=128):
    rows, width = value.shape
    i = lax.broadcasted_iota(jnp.int32, (extent, extent), 0)
    j = lax.broadcasted_iota(jnp.int32, (extent, extent), 1)
    both = i & j
    both = both ^ (both >> 4)
    both = both ^ (both >> 2)
    both = both ^ (both >> 1)
    table = (1 - 2 * (both & 1)).astype(F32).astype(BF16)
    parts = []
    for k in range(width // extent):
        rest = value[:, k * extent : (k + 1) * extent]
        for _ in range(3):
            top = rest.astype(BF16)
            parts.append(top)
            rest = rest - top.astype(F32)
    out = jnp.dot(jnp.concatenate(parts, axis=0), table, preferred_element_type=F32)
    p = []
    for k in range(width // extent):
        at = 3 * k * rows
        p.append((out[at + 2 * rows : at + 3 * rows] + out[at + rows : at + 2 * rows]) + out[at : at + rows])
    s, t, u, v = p[0] + p[1], p[0] - p[1], p[2] + p[3], p[2] - p[3]
    return jnp.concatenate([s + u, t + v, s - u, t - v], axis=1)


def adam_kernel(tokens_all, recv_ref, first_ref, second_ref, master_ref, signs_ref, nm_ref, nf_ref, ns_ref, new_ref):
    total = jnp.sum(recv_ref[...].astype(F32), axis=0)
    half = total.shape[1]
    root = math.sqrt(2 * half)
    sign = (1 - 2 * signs_ref[...]).astype(F32)
    sign0, sign1 = sign[:, :half], sign[:, half:]
    gap = PAIR_GAP
    spun = hadamard(jnp.concatenate([total[:gap] * sign0, total[gap:] * sign1], axis=0)) * (1.0 / (root * tokens_all))
    q0, q1 = spun[:gap], spun[gap:]
    coded = jnp.concatenate([q0 + q1, q0 - q1], axis=1)
    new_first = beta_first * first_ref[...] + (1.0 - beta_first) * coded
    new_second = beta_second * second_ref[...] + (1.0 - beta_second) * coded * coded
    nf_ref[...] = new_first
    ns_ref[...] = new_second
    first_hat = new_first / (1.0 - beta_first**adam_steps)
    second_hat = new_second / (1.0 - beta_second**adam_steps)
    ratio = first_hat / (jnp.sqrt(second_hat) + adam_eps)
    lower, upper = ratio[:, :half], ratio[:, half:]
    back = hadamard(jnp.concatenate([lower + upper, lower - upper], axis=0)) / root
    update = jnp.concatenate([back[:gap] * sign0, back[gap:] * sign1], axis=0)
    master = master_ref[...]
    new_master = master - learn_rate * (update + weight_decay * master)
    nm_ref[...] = new_master
    new_ref[...] = jnp.broadcast_to(new_master.astype(BF16), new_ref.shape)


def ring(n, s):
    return [(i, (i + s) % n) for i in range(n)]


GATHER = ("zl", "y", "zh", "c")


def moved(on_z, shift):
    pairs = []
    for i in range(ZL * Y * ZH * C):
        zl, y, zh, c = i // (Y * ZH * C), i // (ZH * C) % Y, i // C % ZH, i % C
        if on_z(c):
            z = (zh * ZL + zl + shift(zl, True)) % (ZH * ZL)
            zl, zh = z % ZL, z // ZL
        else:
            y = (y + shift(y, False)) % Y
        pairs.append((i, ((zl * Y + y) * ZH + zh) * C + c))
    return pairs


def first_step(value, k):
    shift = lambda place, on_z: {1: -1, 2: 2 - 4 * (place % 2) if on_z else -2, 3: 1}[k]
    return lax.ppermute(value, GATHER, moved(lambda c: c == 1, shift))


def second_step(value, shift):
    return lax.ppermute(value, GATHER, moved(lambda c: c == 0, shift))


def mixed(value, first):
    groups = []
    for c in range(C):
        for i in range(X):
            lines = [((i, j) if (c == 0) == first else (j, i)) for j in range(Y)]
            groups.append([(y * X + x) * C + c for y, x in lines])
    return lax.all_to_all(value, ("y", "x", "c"), 0, 0, axis_index_groups=groups, tiled=True)


def shards(tokens, norm_gain, key_cotangent, secondary, master, moment_first, moment_second, signs):
    tok_rows, width = tokens.shape
    keys_w = key_cotangent.shape[1]
    c = lax.axis_index("c")
    gain = norm_gain.reshape(1, width)
    node_rows = secondary.shape[0]

    half = lax.dynamic_slice_in_dim(secondary, c * (node_rows // 2), node_rows // 2, 0)
    column = jnp.concatenate([half] + [first_step(half, k) for k in range(1, Y)], axis=0)

    part = width // X
    step = 64
    by_rows = lambda cols: pl.BlockSpec((step, cols), lambda i: (i, 0))
    send, inv = pl.pallas_call(
        norm_kernel,
        out_shape=(shape((X, tok_rows, part + keys_w), BF16), shape((tok_rows, 128), F32)),
        grid=(tok_rows // step,),
        in_specs=[by_rows(width), pl.BlockSpec((1, width), lambda i: (0, 0)), by_rows(keys_w)],
        out_specs=(pl.BlockSpec((X, step, part + keys_w), lambda i: (0, i, 0)), by_rows(128)),
        cost_estimate=pl.CostEstimate(flops=tok_rows * width * 6, bytes_accessed=5 << 20, transcendentals=0),
        compiler_params=pltpu.CompilerParams(vmem_limit_bytes=56 << 20),
    )(tokens, gain, key_cotangent)
    recv = mixed(send, True).reshape(X * tok_rows, part + keys_w)
    from_up = second_step(column, lambda place, on_z: -1)
    from_down = second_step(column, lambda place, on_z: 1)
    weights = []
    for block in (column, from_up, from_down):
        weights += [block, lax.ppermute(block, "c", ring(C, 1))]
    send = kernel_call(
        grad_kernel,
        pltpu.HBM((Y, part // Y, keys_w), BF16),
        0,
        1 << 20,
        1,
        40 << 20,
        HBM,
        (pltpu.VMEM((ZL, Y, ZH * C * ROWS, keys_w), BF16), pltpu.SemaphoreType.DMA((ZL,))),
    )(recv)
    blocks = mixed(send, False)
    own, sib = kernel_call(
        sum_kernel,
        (shape((part // Y // C, keys_w), F32), shape((part // Y // C, keys_w), BF16)),
        0,
        1 << 20,
        1,
    )(blocks)
    from_up, from_down = weights[2], weights[4]
    rows = from_up.shape[0] // 2
    far_a, far_b = kernel_call(
        halves_kernel,
        (pltpu.VMEM((rows, keys_w), BF16),) * 2,
        0,
        1 << 20,
        [HBM, HBM],
        24 << 20,
        scratch=(pltpu.SemaphoreType.DMA((2,)),),
    )(from_up, from_down)
    far = [
        second_step(far_a, lambda place, on_z: -1),
        second_step(far_b, lambda place, on_z: 1),
    ]
    sib, weights = lax.optimization_barrier((sib, weights))
    sib = lax.ppermute(sib, "c", ring(C, 1))
    summed = (own + sib.astype(F32)).astype(BF16)
    summed, far = lax.optimization_barrier((summed, far))
    for block in far:
        weights += [block, lax.ppermute(block, "c", ring(C, 1))]
    blocks = lax.all_to_all(summed.reshape(ZL * ZH, ROWS, keys_w), ("zl", "zh"), 0, 0, tiled=True)
    count = len(weights)
    scratch = [pltpu.VMEM(block.shape, BF16) for block in weights] + [pltpu.SemaphoreType.DMA((count,))]
    keys, mean = kernel_call(
        functools.partial(keys_kernel, count),
        (shape((tok_rows, keys_w), BF16), shape((tok_rows, 128), F32)),
        2 * tok_rows * width * keys_w,
        11 << 20,
        [VMEM] * 4 + [HBM] * count,
        60 << 20,
        scratch=scratch,
    )(tokens, gain, key_cotangent, inv, *weights)
    blocks, keys, mean = lax.optimization_barrier((blocks, keys, mean))
    new_master, new_first, new_second, new_rows = kernel_call(
        functools.partial(adam_kernel, tok_rows * math.prod(SIZES)),
        (
            shape(master.shape, F32),
            shape(moment_first.shape, F32),
            shape(moment_second.shape, F32),
            shape((X * ZH, *master.shape), BF16),
        ),
        1 << 25,
        1 << 20,
        5,
        60 << 20,
    )(blocks, moment_first, moment_second, master, signs.reshape(1, -1))

    mine = lax.all_to_all(new_rows, ("x", "zh"), 0, 0, tiled=True)
    token_grad = kernel_call(
        functools.partial(token_grad_kernel, count),
        shape(tokens.shape, BF16),
        2 * tok_rows * width * keys_w,
        13 << 20,
        [VMEM] * 5 + [HBM] * count,
        60 << 20,
        scratch=scratch,
    )(tokens, gain, key_cotangent, inv, mean, *weights)
    mine, token_grad = lax.optimization_barrier((mine, token_grad))
    other = lax.ppermute(mine, "c", ring(C, 1))
    even = jnp.where(c == 0, mine, other)
    odd = jnp.where(c == 0, other, mine)
    new_secondary = jnp.stack([even, odd], axis=1).reshape(node_rows, keys_w)
    return (keys, token_grad, new_master, new_first, new_second, new_secondary)


def solution(mesh):
    fine = Mesh(mesh.devices.reshape(SIZES), AXES)
    split = P(AXES, None)
    return jax.shard_map(
        shards,
        mesh=fine,
        in_specs=(split, P(), split, P(("zl", "y"), None), split, split, split, P()),
        out_specs=(split, split, split, split, split, P(("zl", "y"), None)),
        check_vma=False,
    )
```

```python
import functools
import math

import jax
import jax.numpy as jnp
from jax import lax
from jax.experimental import pallas as pl
from jax.experimental.pallas import tpu as pltpu
from jax.sharding import Mesh
from jax.sharding import PartitionSpec as P

PAIR_GAP = 16
norm_eps = 1e-05
adam_eps = 1e-08
beta_first = 0.9
beta_second = 0.95
adam_steps = 10
learn_rate = 0.002
weight_decay = 0.1

AXES = ("zl", "y", "x", "zh", "c")
SIZES = (4, 4, 4, 2, 2)
ZL, Y, X, ZH, C = SIZES
ROWS = 32
VMEM = pl.BlockSpec(memory_space=pltpu.VMEM)
HBM = pl.BlockSpec(memory_space=pltpu.HBM)
BF16 = jnp.bfloat16
F32 = jnp.float32


def shape(dims, kind):
    return jax.ShapeDtypeStruct(dims, kind)


def in_hbm(*values):
    return [pltpu.with_memory_space_constraint(value, pltpu.HBM) for value in values]


def in_vmem(*values):
    return [pltpu.with_memory_space_constraint(value, pltpu.VMEM) for value in values]


def kernel_call(body, outs, flops, nbytes, in_specs, limit=24 << 20, out_specs=None, scratch=()):
    return pl.pallas_call(
        body,
        out_shape=outs,
        in_specs=[VMEM] * in_specs if isinstance(in_specs, int) else in_specs,
        out_specs=jax.tree.map(lambda _: VMEM, outs) if out_specs is None else out_specs,
        scratch_shapes=list(scratch),
        cost_estimate=pl.CostEstimate(flops=flops, bytes_accessed=nbytes, transcendentals=0),
        compiler_params=pltpu.CompilerParams(vmem_limit_bytes=limit),
    )


def norm_kernel(tok_ref, gain_ref, cot_ref, send_ref, inv_ref):
    c = lax.axis_index("c")
    rows, width = tok_ref.shape
    step = X * ZH * C * ROWS
    acc = jnp.zeros((rows, step), F32)
    for k in range(width // step):
        t = tok_ref[:, k * step : (k + 1) * step].astype(F32)
        acc = acc + t * t
    inv = lax.rsqrt(jnp.sum(acc, axis=-1, keepdims=True) / width + norm_eps)
    inv = jnp.broadcast_to(inv, inv_ref.shape)
    inv_ref[...] = inv
    part = ZH * C * ROWS
    stride_p, stride_q = jnp.where(c == 0, part, step), jnp.where(c == 0, step, part)
    for zl in range(ZL):
        for p in range(X):
            for q in range(Y):
                at = pl.multiple_of(zl * Y * step + p * stride_p + q * stride_q, part)
                cols = pl.ds(at, part)
                normed = tok_ref[:, cols].astype(F32) * inv
                to = (zl * Y + q) * part
                send_ref[p, :, to : to + part] = (normed * gain_ref[:, cols]).astype(BF16)
    for p in range(X):
        send_ref[p, :, ZL * Y * part :] = cot_ref[...]


def grad_kernel(recv_ref, send_ref, buf_ref, sem):
    part = ZH * C * ROWS
    cols = ZL * Y * part
    cot = recv_ref[:, cols:]
    copies = []
    for zl in range(ZL):
        block = recv_ref[:, zl * Y * part : (zl + 1) * Y * part]
        grad = lax.dot_general(block, cot, (((0,), (0,)), ((), ())), preferred_element_type=F32)
        grad = grad.astype(BF16)
        for q in range(Y):
            for zh in range(ZH):
                for c in range(C):
                    at = q * part + (zh * C + c) * ROWS
                    to = (c * ZH + zh) * ROWS
                    buf_ref[zl, q, to : to + ROWS, :] = grad[at : at + ROWS]
        rows = slice(zl * part, (zl + 1) * part)
        copy = pltpu.make_async_copy(buf_ref.at[zl], send_ref.at[:, rows, :], sem.at[zl])
        copy.start()
        copies.append(copy)
    for copy in copies:
        copy.wait()


def sum_kernel(recv_ref, own_ref, sib_ref):
    c = lax.axis_index("c")
    rows = ZH * ROWS
    for ref, core in ((sib_ref, 1 - c), (own_ref, c)):
        for zl in range(ZL):
            at = pl.multiple_of(zl * C * rows + core * rows, rows)
            part = recv_ref[:, pl.ds(at, rows), :].astype(F32)
            ref[zl * rows : (zl + 1) * rows, :] = jnp.sum(part, axis=0).astype(ref.dtype)


def halves_kernel(up_ref, down_ref, a_ref, b_ref, sem):
    rows = a_ref.shape[0]
    copies = (
        pltpu.make_async_copy(up_ref.at[0:rows, :], a_ref, sem.at[0]),
        pltpu.make_async_copy(down_ref.at[rows : 2 * rows, :], b_ref, sem.at[1]),
    )
    for copy in copies:
        copy.start()
    for copy in copies:
        copy.wait()


def places(width, refs):
    c, zl, y = (lax.axis_index(name) for name in ("c", "zl", "y"))
    step = width // (ZL * Y)
    half = step // 2
    for i, ref in enumerate(refs):
        off = (0, 1, 3)[i // 2] if i < 6 else 2
        core = c if i % 2 == 0 else 1 - c
        for row in range(ref.shape[0] // half):
            k = row if i < 6 else row + 2 * ((i - 6) // 2)
            on_zl, on_y = jnp.where(core == 0, off, k), jnp.where(core == 0, k, off)
            node = lax.rem(zl + on_zl, ZL) * Y + lax.rem(y + on_y, Y)
            at = pl.multiple_of(node * step + core * half, half)
            yield pl.ds(at, half), ref[row * half : (row + 1) * half, :]


def widened(ref, cols):
    return jnp.concatenate([ref[...]] * (cols // ref.shape[1]), axis=1)


def keys_kernel(tok_ref, gain_ref, cot_ref, inv_ref, *refs):
    w_refs, (keys_ref, mean_ref) = refs[:-2], refs[-2:]
    width = tok_ref.shape[1]
    inv = widened(inv_ref, width // (ZL * Y * C))
    keys = jnp.zeros(keys_ref.shape, F32)
    for cols, weights in places(width, w_refs):
        normed = tok_ref[:, cols].astype(F32) * inv
        hidden = (normed * gain_ref[:, cols]).astype(BF16)
        keys = keys + jnp.dot(hidden, weights, preferred_element_type=F32)
    keys_ref[...] = keys.astype(BF16)
    mean = jnp.sum(cot_ref[...].astype(F32) * keys, axis=-1, keepdims=True) / width
    mean_ref[...] = jnp.broadcast_to(mean, mean_ref.shape)


def token_grad_kernel(tok_ref, gain_ref, cot_ref, inv_ref, mean_ref, *refs):
    w_refs, tg_ref = refs[:-1], refs[-1]
    width = tok_ref.shape[1]
    inv = widened(inv_ref, width // (ZL * Y * C))
    mean = widened(mean_ref, width // (ZL * Y * C))
    cot = cot_ref[...]
    for cols, weights in places(width, w_refs):
        hidden_grad = lax.dot_general(cot, weights, (((1,), (1,)), ((), ())), preferred_element_type=F32)
        normed = tok_ref[:, cols].astype(F32) * inv
        tg_ref[:, cols] = (inv * (hidden_grad * gain_ref[:, cols] - normed * mean)).astype(BF16)


def hadamard(value, extent=128):
    rows, width = value.shape
    i = lax.broadcasted_iota(jnp.int32, (extent, extent), 0)
    j = lax.broadcasted_iota(jnp.int32, (extent, extent), 1)
    both = i & j
    both = both ^ (both >> 4)
    both = both ^ (both >> 2)
    both = both ^ (both >> 1)
    table = (1 - 2 * (both & 1)).astype(F32).astype(BF16)
    parts = []
    for k in range(width // extent):
        rest = value[:, k * extent : (k + 1) * extent]
        for _ in range(3):
            top = rest.astype(BF16)
            parts.append(top)
            rest = rest - top.astype(F32)
    out = jnp.dot(jnp.concatenate(parts, axis=0), table, preferred_element_type=F32)
    p = []
    for k in range(width // extent):
        at = 3 * k * rows
        p.append((out[at + 2 * rows : at + 3 * rows] + out[at + rows : at + 2 * rows]) + out[at : at + rows])
    s, t, u, v = p[0] + p[1], p[0] - p[1], p[2] + p[3], p[2] - p[3]
    return jnp.concatenate([s + u, t + v, s - u, t - v], axis=1)


def adam_kernel(tokens_all, recv_ref, first_ref, second_ref, master_ref, signs_ref, nm_ref, nf_ref, ns_ref, new_ref):
    total = jnp.sum(recv_ref[...].astype(F32), axis=0)
    half = total.shape[1]
    root = math.sqrt(2 * half)
    sign = (1 - 2 * signs_ref[...]).astype(F32)
    sign0, sign1 = sign[:, :half], sign[:, half:]
    gap = PAIR_GAP
    spun = hadamard(jnp.concatenate([total[:gap] * sign0, total[gap:] * sign1], axis=0)) * (1.0 / (root * tokens_all))
    q0, q1 = spun[:gap], spun[gap:]
    coded = jnp.concatenate([q0 + q1, q0 - q1], axis=1)
    new_first = beta_first * first_ref[...] + (1.0 - beta_first) * coded
    new_second = beta_second * second_ref[...] + (1.0 - beta_second) * coded * coded
    nf_ref[...] = new_first
    ns_ref[...] = new_second
    first_hat = new_first / (1.0 - beta_first**adam_steps)
    second_hat = new_second / (1.0 - beta_second**adam_steps)
    ratio = first_hat / (jnp.sqrt(second_hat) + adam_eps)
    lower, upper = ratio[:, :half], ratio[:, half:]
    back = hadamard(jnp.concatenate([lower + upper, lower - upper], axis=0)) / root
    update = jnp.concatenate([back[:gap] * sign0, back[gap:] * sign1], axis=0)
    master = master_ref[...]
    new_master = master - learn_rate * (update + weight_decay * master)
    nm_ref[...] = new_master
    new_ref[...] = jnp.broadcast_to(new_master.astype(BF16), new_ref.shape)


def ring(n, s):
    return [(i, (i + s) % n) for i in range(n)]


GATHER = ("zl", "y", "zh", "c")


def moved(on_z, shift):
    pairs = []
    for i in range(ZL * Y * ZH * C):
        zl, y, zh, c = i // (Y * ZH * C), i // (ZH * C) % Y, i // C % ZH, i % C
        if on_z(c):
            z = (zh * ZL + zl + shift(zl, True)) % (ZH * ZL)
            zl, zh = z % ZL, z // ZL
        else:
            y = (y + shift(y, False)) % Y
        pairs.append((i, ((zl * Y + y) * ZH + zh) * C + c))
    return pairs


def first_step(value, k):
    shift = lambda place, on_z: {1: -1, 2: 2 - 4 * (place % 2) if on_z else -2, 3: 1}[k]
    return lax.ppermute(value, GATHER, moved(lambda c: c == 1, shift))


def second_step(value, shift):
    return lax.ppermute(value, GATHER, moved(lambda c: c == 0, shift))


def mixed(value, first):
    groups = []
    for c in range(C):
        for i in range(X):
            lines = [((i, j) if (c == 0) == first else (j, i)) for j in range(Y)]
            groups.append([(y * X + x) * C + c for y, x in lines])
    return lax.all_to_all(value, ("y", "x", "c"), 0, 0, axis_index_groups=groups, tiled=True)


def shards(tokens, norm_gain, key_cotangent, secondary, master, moment_first, moment_second, signs):
    tok_rows, width = tokens.shape
    keys_w = key_cotangent.shape[1]
    c = lax.axis_index("c")
    gain = norm_gain.reshape(1, width)
    node_rows = secondary.shape[0]

    half = lax.dynamic_slice_in_dim(secondary, c * (node_rows // 2), node_rows // 2, 0)
    column = jnp.concatenate([half] + [first_step(half, k) for k in range(1, Y)], axis=0)

    part = width // X
    step = 64
    by_rows = lambda cols: pl.BlockSpec((step, cols), lambda i: (i, 0))
    send, inv = pl.pallas_call(
        norm_kernel,
        out_shape=(pltpu.HBM((X, tok_rows, part + keys_w), BF16), pltpu.HBM((tok_rows, 128), F32)),
        grid=(tok_rows // step,),
        in_specs=[by_rows(width), pl.BlockSpec((1, width), lambda i: (0, 0)), by_rows(keys_w)],
        out_specs=(pl.BlockSpec((X, step, part + keys_w), lambda i: (0, i, 0)), by_rows(128)),
        cost_estimate=pl.CostEstimate(flops=tok_rows * width * 6, bytes_accessed=5 << 20, transcendentals=0),
        compiler_params=pltpu.CompilerParams(vmem_limit_bytes=24 << 20),
    )(*in_hbm(tokens, gain, key_cotangent))
    recv = mixed(send, True).reshape(X * tok_rows, part + keys_w)
    from_up = second_step(column, lambda place, on_z: -1)
    from_down = second_step(column, lambda place, on_z: 1)
    weights = []
    for block in (column, from_up, from_down):
        weights += [block, lax.ppermute(block, "c", ring(C, 1))]
    send = kernel_call(
        grad_kernel,
        pltpu.HBM((Y, part // Y, keys_w), BF16),
        0,
        1 << 20,
        1,
        24 << 20,
        HBM,
        (pltpu.VMEM((ZL, Y, ZH * C * ROWS, keys_w), BF16), pltpu.SemaphoreType.DMA((ZL,))),
    )(recv)
    blocks = mixed(send, False)
    own, sib = kernel_call(
        sum_kernel,
        (shape((part // Y // C, keys_w), F32), shape((part // Y // C, keys_w), BF16)),
        0,
        1 << 20,
        1,
    )(blocks)
    from_up, from_down = weights[2], weights[4]
    rows = from_up.shape[0] // 2
    far_a, far_b = kernel_call(
        halves_kernel,
        (pltpu.VMEM((rows, keys_w), BF16),) * 2,
        0,
        1 << 20,
        [HBM, HBM],
        24 << 20,
        scratch=(pltpu.SemaphoreType.DMA((2,)),),
    )(from_up, from_down)
    far = [
        second_step(far_a, lambda place, on_z: -1),
        second_step(far_b, lambda place, on_z: 1),
    ]
    sib, weights = lax.optimization_barrier((sib, weights))
    sib = lax.ppermute(sib, "c", ring(C, 1))
    summed = (own + sib.astype(F32)).astype(BF16)
    summed, far = lax.optimization_barrier((summed, far))
    for block in far:
        weights += [block, lax.ppermute(block, "c", ring(C, 1))]
    blocks = lax.all_to_all(summed.reshape(ZL * ZH, ROWS, keys_w), ("zl", "zh"), 0, 0, tiled=True)
    keys, mean = kernel_call(
        keys_kernel,
        (pltpu.HBM((tok_rows, keys_w), BF16), pltpu.HBM((tok_rows, 128), F32)),
        2 * tok_rows * width * keys_w,
        3 << 20,
        4 + len(weights),
    )(*in_hbm(tokens, gain, key_cotangent, inv), *in_vmem(*weights))
    blocks, keys, mean = lax.optimization_barrier((blocks, keys, mean))
    new_master, new_first, new_second, new_rows = kernel_call(
        functools.partial(adam_kernel, tok_rows * math.prod(SIZES)),
        (
            pltpu.HBM(master.shape, F32),
            pltpu.HBM(moment_first.shape, F32),
            pltpu.HBM(moment_second.shape, F32),
            pltpu.HBM((X * ZH, *master.shape), BF16),
        ),
        1 << 25,
        1 << 20,
        5,
    )(blocks, *in_hbm(moment_first, moment_second, master, signs.reshape(1, -1)))

    mine = lax.all_to_all(new_rows, ("x", "zh"), 0, 0, tiled=True)
    token_grad = kernel_call(
        token_grad_kernel,
        pltpu.HBM(tokens.shape, BF16),
        2 * tok_rows * width * keys_w,
        5 << 20,
        5 + len(weights),
    )(*in_hbm(tokens, gain, key_cotangent, inv, mean), *in_vmem(*weights))
    mine, token_grad = lax.optimization_barrier((mine, token_grad))
    other = lax.ppermute(mine, "c", ring(C, 1))
    even = jnp.where(c == 0, mine, other)
    odd = jnp.where(c == 0, other, mine)
    new_secondary = jnp.stack([even, odd], axis=1).reshape(node_rows, keys_w)
    return (keys, token_grad, new_master, new_first, new_second, new_secondary)


def solution(mesh):
    fine = Mesh(mesh.devices.reshape(SIZES), AXES)
    split = P(AXES, None)
    return jax.shard_map(
        shards,
        mesh=fine,
        in_specs=(split, P(), split, P(("zl", "y"), None), split, split, split, P()),
        out_specs=(split, split, split, split, split, P(("zl", "y"), None)),
        check_vma=False,
    )
```

```python
import functools
import math

import jax
import jax.numpy as jnp
from jax import lax
from jax.experimental import pallas as pl
from jax.experimental.pallas import tpu as pltpu
from jax.sharding import Mesh
from jax.sharding import PartitionSpec as P

PAIR_GAP = 16
norm_eps = 1e-05
adam_eps = 1e-08
beta_first = 0.9
beta_second = 0.95
adam_steps = 10
learn_rate = 0.002
weight_decay = 0.1

AXES = ("zl", "y", "x", "zh", "c")
SIZES = (4, 4, 4, 2, 2)
ZL, Y, X, ZH, C = SIZES
ROWS = 32
VMEM = pl.BlockSpec(memory_space=pltpu.VMEM)
HBM = pl.BlockSpec(memory_space=pltpu.HBM)
BF16 = jnp.bfloat16
F32 = jnp.float32


def shape(dims, kind):
    return jax.ShapeDtypeStruct(dims, kind)


def in_hbm(*values):
    return [pltpu.with_memory_space_constraint(value, pltpu.HBM) for value in values]


def in_vmem(*values):
    return [pltpu.with_memory_space_constraint(value, pltpu.VMEM) for value in values]


def kernel_call(body, outs, flops, nbytes, in_specs, limit=24 << 20, out_specs=None, scratch=()):
    return pl.pallas_call(
        body,
        out_shape=outs,
        in_specs=[VMEM] * in_specs if isinstance(in_specs, int) else in_specs,
        out_specs=jax.tree.map(lambda _: VMEM, outs) if out_specs is None else out_specs,
        scratch_shapes=list(scratch),
        cost_estimate=pl.CostEstimate(flops=flops, bytes_accessed=nbytes, transcendentals=0),
        compiler_params=pltpu.CompilerParams(vmem_limit_bytes=limit),
    )


def norm_kernel(tok_ref, gain_ref, cot_ref, send_ref, inv_ref):
    c = lax.axis_index("c")
    rows, width = tok_ref.shape
    step = X * ZH * C * ROWS
    acc = jnp.zeros((rows, step), F32)
    for k in range(width // step):
        t = tok_ref[:, k * step : (k + 1) * step].astype(F32)
        acc = acc + t * t
    inv = lax.rsqrt(jnp.sum(acc, axis=-1, keepdims=True) / width + norm_eps)
    inv = jnp.broadcast_to(inv, inv_ref.shape)
    inv_ref[...] = inv
    part = ZH * C * ROWS
    stride_p, stride_q = jnp.where(c == 0, part, step), jnp.where(c == 0, step, part)
    for zl in range(ZL):
        for p in range(X):
            for q in range(Y):
                at = pl.multiple_of(zl * Y * step + p * stride_p + q * stride_q, part)
                cols = pl.ds(at, part)
                normed = tok_ref[:, cols].astype(F32) * inv
                to = (zl * Y + q) * part
                send_ref[p, :, to : to + part] = (normed * gain_ref[:, cols]).astype(BF16)
    for p in range(X):
        send_ref[p, :, ZL * Y * part :] = cot_ref[...]


def grad_kernel(recv_ref, send_ref, buf_ref, sem):
    part = ZH * C * ROWS
    cols = ZL * Y * part
    cot = recv_ref[:, cols:]
    copies = []
    for zl in range(ZL):
        block = recv_ref[:, zl * Y * part : (zl + 1) * Y * part]
        grad = lax.dot_general(block, cot, (((0,), (0,)), ((), ())), preferred_element_type=F32)
        grad = grad.astype(BF16)
        for q in range(Y):
            for zh in range(ZH):
                for c in range(C):
                    at = q * part + (zh * C + c) * ROWS
                    to = (c * ZH + zh) * ROWS
                    buf_ref[zl, q, to : to + ROWS, :] = grad[at : at + ROWS]
        rows = slice(zl * part, (zl + 1) * part)
        copy = pltpu.make_async_copy(buf_ref.at[zl], send_ref.at[:, rows, :], sem.at[zl])
        copy.start()
        copies.append(copy)
    for copy in copies:
        copy.wait()


def sum_kernel(recv_ref, own_ref, sib_ref):
    c = lax.axis_index("c")
    rows = ZH * ROWS
    for ref, core in ((sib_ref, 1 - c), (own_ref, c)):
        for zl in range(ZL):
            at = pl.multiple_of(zl * C * rows + core * rows, rows)
            part = recv_ref[:, pl.ds(at, rows), :].astype(F32)
            ref[zl * rows : (zl + 1) * rows, :] = jnp.sum(part, axis=0).astype(ref.dtype)


def halves_kernel(up_ref, down_ref, a_ref, b_ref, sem):
    rows = a_ref.shape[0]
    copies = (
        pltpu.make_async_copy(up_ref.at[0:rows, :], a_ref, sem.at[0]),
        pltpu.make_async_copy(down_ref.at[rows : 2 * rows, :], b_ref, sem.at[1]),
    )
    for copy in copies:
        copy.start()
    for copy in copies:
        copy.wait()


def places(width, refs):
    c, zl, y = (lax.axis_index(name) for name in ("c", "zl", "y"))
    step = width // (ZL * Y)
    half = step // 2
    for i, ref in enumerate(refs):
        off = (0, 1, 3)[i // 2] if i < 6 else 2
        core = c if i % 2 == 0 else 1 - c
        for row in range(ref.shape[0] // half):
            k = row if i < 6 else row + 2 * ((i - 6) // 2)
            on_zl, on_y = jnp.where(core == 0, off, k), jnp.where(core == 0, k, off)
            node = lax.rem(zl + on_zl, ZL) * Y + lax.rem(y + on_y, Y)
            at = pl.multiple_of(node * step + core * half, half)
            yield pl.ds(at, half), ref[row * half : (row + 1) * half, :]


def widened(ref, cols):
    return jnp.concatenate([ref[...]] * (cols // ref.shape[1]), axis=1)


def keys_kernel(tok_ref, gain_ref, cot_ref, inv_ref, *refs):
    w_refs, (keys_ref, mean_ref) = refs[:-2], refs[-2:]
    width = tok_ref.shape[1]
    inv = widened(inv_ref, width // (ZL * Y * C))
    keys = jnp.zeros(keys_ref.shape, F32)
    for cols, weights in places(width, w_refs):
        normed = tok_ref[:, cols].astype(F32) * inv
        hidden = (normed * gain_ref[:, cols]).astype(BF16)
        keys = keys + jnp.dot(hidden, weights, preferred_element_type=F32)
    keys_ref[...] = keys.astype(BF16)
    mean = jnp.sum(cot_ref[...].astype(F32) * keys, axis=-1, keepdims=True) / width
    mean_ref[...] = jnp.broadcast_to(mean, mean_ref.shape)


def token_grad_kernel(tok_ref, gain_ref, cot_ref, inv_ref, mean_ref, *refs):
    w_refs, tg_ref = refs[:-1], refs[-1]
    width = tok_ref.shape[1]
    inv = widened(inv_ref, width // (ZL * Y * C))
    mean = widened(mean_ref, width // (ZL * Y * C))
    cot = cot_ref[...]
    for cols, weights in places(width, w_refs):
        hidden_grad = lax.dot_general(cot, weights, (((1,), (1,)), ((), ())), preferred_element_type=F32)
        normed = tok_ref[:, cols].astype(F32) * inv
        tg_ref[:, cols] = (inv * (hidden_grad * gain_ref[:, cols] - normed * mean)).astype(BF16)


def hadamard(value, extent=128):
    rows, width = value.shape
    i = lax.broadcasted_iota(jnp.int32, (extent, extent), 0)
    j = lax.broadcasted_iota(jnp.int32, (extent, extent), 1)
    both = i & j
    both = both ^ (both >> 4)
    both = both ^ (both >> 2)
    both = both ^ (both >> 1)
    table = (1 - 2 * (both & 1)).astype(F32).astype(BF16)
    parts = []
    for k in range(width // extent):
        rest = value[:, k * extent : (k + 1) * extent]
        for _ in range(3):
            top = rest.astype(BF16)
            parts.append(top)
            rest = rest - top.astype(F32)
    out = jnp.dot(jnp.concatenate(parts, axis=0), table, preferred_element_type=F32)
    p = []
    for k in range(width // extent):
        at = 3 * k * rows
        p.append((out[at + 2 * rows : at + 3 * rows] + out[at + rows : at + 2 * rows]) + out[at : at + rows])
    s, t, u, v = p[0] + p[1], p[0] - p[1], p[2] + p[3], p[2] - p[3]
    return jnp.concatenate([s + u, t + v, s - u, t - v], axis=1)


def adam_kernel(tokens_all, recv_ref, first_ref, second_ref, master_ref, signs_ref, nm_ref, nf_ref, ns_ref, new_ref):
    total = jnp.sum(recv_ref[...].astype(F32), axis=0)
    half = total.shape[1]
    root = math.sqrt(2 * half)
    sign = (1 - 2 * signs_ref[...]).astype(F32)
    sign0, sign1 = sign[:, :half], sign[:, half:]
    gap = PAIR_GAP
    spun = hadamard(jnp.concatenate([total[:gap] * sign0, total[gap:] * sign1], axis=0)) * (1.0 / (root * tokens_all))
    q0, q1 = spun[:gap], spun[gap:]
    coded = jnp.concatenate([q0 + q1, q0 - q1], axis=1)
    new_first = beta_first * first_ref[...] + (1.0 - beta_first) * coded
    new_second = beta_second * second_ref[...] + (1.0 - beta_second) * coded * coded
    nf_ref[...] = new_first
    ns_ref[...] = new_second
    first_hat = new_first / (1.0 - beta_first**adam_steps)
    second_hat = new_second / (1.0 - beta_second**adam_steps)
    ratio = first_hat / (jnp.sqrt(second_hat) + adam_eps)
    lower, upper = ratio[:, :half], ratio[:, half:]
    back = hadamard(jnp.concatenate([lower + upper, lower - upper], axis=0)) / root
    update = jnp.concatenate([back[:gap] * sign0, back[gap:] * sign1], axis=0)
    master = master_ref[...]
    new_master = master - learn_rate * (update + weight_decay * master)
    nm_ref[...] = new_master
    new_ref[...] = jnp.broadcast_to(new_master.astype(BF16), new_ref.shape)


def ring(n, s):
    return [(i, (i + s) % n) for i in range(n)]


GATHER = ("zl", "y", "zh", "c")


def moved(on_z, shift):
    pairs = []
    for i in range(ZL * Y * ZH * C):
        zl, y, zh, c = i // (Y * ZH * C), i // (ZH * C) % Y, i // C % ZH, i % C
        if on_z(c):
            z = (zh * ZL + zl + shift(zl, True)) % (ZH * ZL)
            zl, zh = z % ZL, z // ZL
        else:
            y = (y + shift(y, False)) % Y
        pairs.append((i, ((zl * Y + y) * ZH + zh) * C + c))
    return pairs


def first_step(value, shift):
    return lax.ppermute(value, GATHER, moved(lambda c: c == 1, shift))


def second_step(value, shift):
    return lax.ppermute(value, GATHER, moved(lambda c: c == 0, shift))


def mixed(value, first):
    groups = []
    for c in range(C):
        for i in range(X):
            lines = [((i, j) if (c == 0) == first else (j, i)) for j in range(Y)]
            groups.append([(y * X + x) * C + c for y, x in lines])
    return lax.all_to_all(value, ("y", "x", "c"), 0, 0, axis_index_groups=groups, tiled=True)


def shards(tokens, norm_gain, key_cotangent, secondary, master, moment_first, moment_second, signs):
    tok_rows, width = tokens.shape
    keys_w = key_cotangent.shape[1]
    c = lax.axis_index("c")
    gain = norm_gain.reshape(1, width)
    node_rows = secondary.shape[0]

    half = lax.dynamic_slice_in_dim(secondary, c * (node_rows // 2), node_rows // 2, 0)
    up = first_step(half, lambda place, on_z: -1)
    down = first_step(half, lambda place, on_z: 1)
    odd = jnp.where(c == 0, lax.axis_index("y"), lax.axis_index("zl")) % 2 == 1
    far = first_step(jnp.where(odd, up, down), lambda place, on_z: 1 - 2 * (place % 2))
    column = jnp.concatenate([half, up, far, down], axis=0)

    part = width // X
    step = 64
    by_rows = lambda cols: pl.BlockSpec((step, cols), lambda i: (i, 0))
    send, inv = pl.pallas_call(
        norm_kernel,
        out_shape=(pltpu.HBM((X, tok_rows, part + keys_w), BF16), pltpu.HBM((tok_rows, 128), F32)),
        grid=(tok_rows // step,),
        in_specs=[by_rows(width), pl.BlockSpec((1, width), lambda i: (0, 0)), by_rows(keys_w)],
        out_specs=(pl.BlockSpec((X, step, part + keys_w), lambda i: (0, i, 0)), by_rows(128)),
        cost_estimate=pl.CostEstimate(flops=tok_rows * width * 6, bytes_accessed=5 << 20, transcendentals=0),
        compiler_params=pltpu.CompilerParams(vmem_limit_bytes=24 << 20),
    )(*in_hbm(tokens, gain, key_cotangent))
    recv = mixed(send, True).reshape(X * tok_rows, part + keys_w)
    from_up = second_step(column, lambda place, on_z: -1)
    from_down = second_step(column, lambda place, on_z: 1)
    weights = []
    for block in (column, from_up, from_down):
        weights += [block, lax.ppermute(block, "c", ring(C, 1))]
    send = kernel_call(
        grad_kernel,
        pltpu.HBM((Y, part // Y, keys_w), BF16),
        0,
        1 << 20,
        1,
        24 << 20,
        HBM,
        (pltpu.VMEM((ZL, Y, ZH * C * ROWS, keys_w), BF16), pltpu.SemaphoreType.DMA((ZL,))),
    )(recv)
    blocks = mixed(send, False)
    own, sib = kernel_call(
        sum_kernel,
        (shape((part // Y // C, keys_w), F32), shape((part // Y // C, keys_w), BF16)),
        0,
        1 << 20,
        1,
    )(blocks)
    from_up, from_down = weights[2], weights[4]
    rows = from_up.shape[0] // 2
    far_a, far_b = kernel_call(
        halves_kernel,
        (pltpu.VMEM((rows, keys_w), BF16),) * 2,
        0,
        1 << 20,
        [HBM, HBM],
        24 << 20,
        scratch=(pltpu.SemaphoreType.DMA((2,)),),
    )(from_up, from_down)
    far = [
        second_step(far_a, lambda place, on_z: -1),
        second_step(far_b, lambda place, on_z: 1),
    ]
    sib, weights = lax.optimization_barrier((sib, weights))
    sib = lax.ppermute(sib, "c", ring(C, 1))
    summed = (own + sib.astype(F32)).astype(BF16)
    summed, far = lax.optimization_barrier((summed, far))
    for block in far:
        weights += [block, lax.ppermute(block, "c", ring(C, 1))]
    blocks = lax.all_to_all(summed.reshape(ZL * ZH, ROWS, keys_w), ("zl", "zh"), 0, 0, tiled=True)
    keys, mean = kernel_call(
        keys_kernel,
        (pltpu.HBM((tok_rows, keys_w), BF16), pltpu.HBM((tok_rows, 128), F32)),
        2 * tok_rows * width * keys_w,
        3 << 20,
        4 + len(weights),
    )(*in_hbm(tokens, gain, key_cotangent, inv), *in_vmem(*weights))
    blocks, keys, mean = lax.optimization_barrier((blocks, keys, mean))
    new_master, new_first, new_second, new_rows = kernel_call(
        functools.partial(adam_kernel, tok_rows * math.prod(SIZES)),
        (
            pltpu.HBM(master.shape, F32),
            pltpu.HBM(moment_first.shape, F32),
            pltpu.HBM(moment_second.shape, F32),
            pltpu.HBM((X * ZH, *master.shape), BF16),
        ),
        1 << 25,
        1 << 20,
        5,
    )(blocks, *in_hbm(moment_first, moment_second, master, signs.reshape(1, -1)))

    mine = lax.all_to_all(new_rows, ("x", "zh"), 0, 0, tiled=True)
    token_grad = kernel_call(
        token_grad_kernel,
        pltpu.HBM(tokens.shape, BF16),
        2 * tok_rows * width * keys_w,
        5 << 20,
        5 + len(weights),
    )(*in_hbm(tokens, gain, key_cotangent, inv, mean), *in_vmem(*weights))
    mine, token_grad = lax.optimization_barrier((mine, token_grad))
    other = lax.ppermute(mine, "c", ring(C, 1))
    even = jnp.where(c == 0, mine, other)
    odd = jnp.where(c == 0, other, mine)
    new_secondary = jnp.stack([even, odd], axis=1).reshape(node_rows, keys_w)
    return (keys, token_grad, new_master, new_first, new_second, new_secondary)


def solution(mesh):
    fine = Mesh(mesh.devices.reshape(SIZES), AXES)
    split = P(AXES, None)
    return jax.shard_map(
        shards,
        mesh=fine,
        in_specs=(split, P(), split, P(("zl", "y"), None), split, split, split, P()),
        out_specs=(split, split, split, split, split, P(("zl", "y"), None)),
        check_vma=False,
    )
```

```python
import functools
import math

import jax
import jax.numpy as jnp
from jax import lax
from jax.experimental import pallas as pl
from jax.experimental.pallas import tpu as pltpu
from jax.sharding import Mesh
from jax.sharding import PartitionSpec as P

PAIR_GAP = 16
norm_eps = 1e-05
adam_eps = 1e-08
beta_first = 0.9
beta_second = 0.95
adam_steps = 10
learn_rate = 0.002
weight_decay = 0.1

AXES = ("zl", "y", "x", "zh", "c")
SIZES = (4, 4, 4, 2, 2)
ZL, Y, X, ZH, C = SIZES
ROWS = 32
VMEM = pl.BlockSpec(memory_space=pltpu.VMEM)
HBM = pl.BlockSpec(memory_space=pltpu.HBM)
BF16 = jnp.bfloat16
F32 = jnp.float32


def shape(dims, kind):
    return jax.ShapeDtypeStruct(dims, kind)


def in_hbm(*values):
    return [pltpu.with_memory_space_constraint(value, pltpu.HBM) for value in values]


def in_vmem(*values):
    return [pltpu.with_memory_space_constraint(value, pltpu.VMEM) for value in values]


def kernel_call(body, outs, flops, nbytes, in_specs, limit=24 << 20, out_specs=None, scratch=()):
    return pl.pallas_call(
        body,
        out_shape=outs,
        in_specs=[VMEM] * in_specs if isinstance(in_specs, int) else in_specs,
        out_specs=jax.tree.map(lambda _: VMEM, outs) if out_specs is None else out_specs,
        scratch_shapes=list(scratch),
        cost_estimate=pl.CostEstimate(flops=flops, bytes_accessed=nbytes, transcendentals=0),
        compiler_params=pltpu.CompilerParams(vmem_limit_bytes=limit),
    )


def norm_kernel(tok_ref, gain_ref, cot_ref, send_ref, inv_ref):
    c = lax.axis_index("c")
    rows, width = tok_ref.shape
    step = X * ZH * C * ROWS
    acc = jnp.zeros((rows, step), F32)
    for k in range(width // step):
        t = tok_ref[:, k * step : (k + 1) * step].astype(F32)
        acc = acc + t * t
    inv = lax.rsqrt(jnp.sum(acc, axis=-1, keepdims=True) / width + norm_eps)
    inv = jnp.broadcast_to(inv, inv_ref.shape)
    inv_ref[...] = inv
    part = ZH * C * ROWS
    stride_p, stride_q = jnp.where(c == 0, part, step), jnp.where(c == 0, step, part)
    for zl in range(ZL):
        for p in range(X):
            for q in range(Y):
                at = pl.multiple_of(zl * Y * step + p * stride_p + q * stride_q, part)
                cols = pl.ds(at, part)
                normed = tok_ref[:, cols].astype(F32) * inv
                to = (zl * Y + q) * part
                send_ref[p, :, to : to + part] = (normed * gain_ref[:, cols]).astype(BF16)
    for p in range(X):
        send_ref[p, :, ZL * Y * part :] = cot_ref[...]


def grad_kernel(recv_ref, send_ref, buf_ref, sem):
    part = ZH * C * ROWS
    cols = ZL * Y * part
    cot = recv_ref[:, cols:]
    copies = []
    for zl in range(ZL):
        block = recv_ref[:, zl * Y * part : (zl + 1) * Y * part]
        grad = lax.dot_general(block, cot, (((0,), (0,)), ((), ())), preferred_element_type=F32)
        grad = grad.astype(BF16)
        for q in range(Y):
            for zh in range(ZH):
                for c in range(C):
                    at = q * part + (zh * C + c) * ROWS
                    to = (c * ZH + zh) * ROWS
                    buf_ref[zl, q, to : to + ROWS, :] = grad[at : at + ROWS]
        rows = slice(zl * part, (zl + 1) * part)
        copy = pltpu.make_async_copy(buf_ref.at[zl], send_ref.at[:, rows, :], sem.at[zl])
        copy.start()
        copies.append(copy)
    for copy in copies:
        copy.wait()


def sum_kernel(recv_ref, own_ref, sib_ref):
    c = lax.axis_index("c")
    rows = ZH * ROWS
    for ref, core in ((sib_ref, 1 - c), (own_ref, c)):
        for zl in range(ZL):
            at = pl.multiple_of(zl * C * rows + core * rows, rows)
            part = recv_ref[:, pl.ds(at, rows), :].astype(F32)
            ref[zl * rows : (zl + 1) * rows, :] = jnp.sum(part, axis=0).astype(ref.dtype)


def halves_kernel(up_ref, down_ref, a_ref, b_ref, sem):
    rows = a_ref.shape[0]
    copies = (
        pltpu.make_async_copy(up_ref.at[0:rows, :], a_ref, sem.at[0]),
        pltpu.make_async_copy(down_ref.at[rows : 2 * rows, :], b_ref, sem.at[1]),
    )
    for copy in copies:
        copy.start()
    for copy in copies:
        copy.wait()


def places(width, refs):
    c, zl, y = (lax.axis_index(name) for name in ("c", "zl", "y"))
    step = width // (ZL * Y)
    half = step // 2
    for i, ref in enumerate(refs):
        off = (0, 1, 3)[i // 2] if i < 6 else 2
        core = c if i % 2 == 0 else 1 - c
        for row in range(ref.shape[0] // half):
            k = row if i < 6 else row + 2 * ((i - 6) // 2)
            on_zl, on_y = jnp.where(core == 0, k, off), jnp.where(core == 0, off, k)
            node = lax.rem(zl + on_zl, ZL) * Y + lax.rem(y + on_y, Y)
            at = pl.multiple_of(node * step + core * half, half)
            yield pl.ds(at, half), ref[row * half : (row + 1) * half, :]


def widened(ref, cols):
    return jnp.concatenate([ref[...]] * (cols // ref.shape[1]), axis=1)


def keys_kernel(tok_ref, gain_ref, cot_ref, inv_ref, *refs):
    w_refs, (keys_ref, mean_ref) = refs[:-2], refs[-2:]
    width = tok_ref.shape[1]
    inv = widened(inv_ref, width // (ZL * Y * C))
    keys = jnp.zeros(keys_ref.shape, F32)
    for cols, weights in places(width, w_refs):
        normed = tok_ref[:, cols].astype(F32) * inv
        hidden = (normed * gain_ref[:, cols]).astype(BF16)
        keys = keys + jnp.dot(hidden, weights, preferred_element_type=F32)
    keys_ref[...] = keys.astype(BF16)
    mean = jnp.sum(cot_ref[...].astype(F32) * keys, axis=-1, keepdims=True) / width
    mean_ref[...] = jnp.broadcast_to(mean, mean_ref.shape)


def token_grad_kernel(tok_ref, gain_ref, cot_ref, inv_ref, mean_ref, *refs):
    w_refs, tg_ref = refs[:-1], refs[-1]
    width = tok_ref.shape[1]
    inv = widened(inv_ref, width // (ZL * Y * C))
    mean = widened(mean_ref, width // (ZL * Y * C))
    cot = cot_ref[...]
    for cols, weights in places(width, w_refs):
        hidden_grad = lax.dot_general(cot, weights, (((1,), (1,)), ((), ())), preferred_element_type=F32)
        normed = tok_ref[:, cols].astype(F32) * inv
        tg_ref[:, cols] = (inv * (hidden_grad * gain_ref[:, cols] - normed * mean)).astype(BF16)


def hadamard(value, extent=128):
    rows, width = value.shape
    i = lax.broadcasted_iota(jnp.int32, (extent, extent), 0)
    j = lax.broadcasted_iota(jnp.int32, (extent, extent), 1)
    both = i & j
    both = both ^ (both >> 4)
    both = both ^ (both >> 2)
    both = both ^ (both >> 1)
    table = (1 - 2 * (both & 1)).astype(F32).astype(BF16)
    parts = []
    for k in range(width // extent):
        rest = value[:, k * extent : (k + 1) * extent]
        for _ in range(3):
            top = rest.astype(BF16)
            parts.append(top)
            rest = rest - top.astype(F32)
    out = jnp.dot(jnp.concatenate(parts, axis=0), table, preferred_element_type=F32)
    p = []
    for k in range(width // extent):
        at = 3 * k * rows
        p.append((out[at + 2 * rows : at + 3 * rows] + out[at + rows : at + 2 * rows]) + out[at : at + rows])
    s, t, u, v = p[0] + p[1], p[0] - p[1], p[2] + p[3], p[2] - p[3]
    return jnp.concatenate([s + u, t + v, s - u, t - v], axis=1)


def adam_kernel(tokens_all, recv_ref, first_ref, second_ref, master_ref, signs_ref, nm_ref, nf_ref, ns_ref, new_ref):
    total = jnp.sum(recv_ref[...].astype(F32), axis=0)
    half = total.shape[1]
    root = math.sqrt(2 * half)
    sign = (1 - 2 * signs_ref[...]).astype(F32)
    sign0, sign1 = sign[:, :half], sign[:, half:]
    gap = PAIR_GAP
    spun = hadamard(jnp.concatenate([total[:gap] * sign0, total[gap:] * sign1], axis=0)) * (1.0 / (root * tokens_all))
    q0, q1 = spun[:gap], spun[gap:]
    coded = jnp.concatenate([q0 + q1, q0 - q1], axis=1)
    new_first = beta_first * first_ref[...] + (1.0 - beta_first) * coded
    new_second = beta_second * second_ref[...] + (1.0 - beta_second) * coded * coded
    nf_ref[...] = new_first
    ns_ref[...] = new_second
    first_hat = new_first / (1.0 - beta_first**adam_steps)
    second_hat = new_second / (1.0 - beta_second**adam_steps)
    ratio = first_hat / (jnp.sqrt(second_hat) + adam_eps)
    lower, upper = ratio[:, :half], ratio[:, half:]
    back = hadamard(jnp.concatenate([lower + upper, lower - upper], axis=0)) / root
    update = jnp.concatenate([back[:gap] * sign0, back[gap:] * sign1], axis=0)
    master = master_ref[...]
    new_master = master - learn_rate * (update + weight_decay * master)
    nm_ref[...] = new_master
    new_ref[...] = jnp.broadcast_to(new_master.astype(BF16), new_ref.shape)


def ring(n, s):
    return [(i, (i + s) % n) for i in range(n)]


GATHER = ("zl", "y", "zh", "c")


def moved(on_z, shift):
    pairs = []
    for i in range(ZL * Y * ZH * C):
        zl, y, zh, c = i // (Y * ZH * C), i // (ZH * C) % Y, i // C % ZH, i % C
        if on_z(c):
            z = (zh * ZL + zl + shift(zl, True)) % (ZH * ZL)
            zl, zh = z % ZL, z // ZL
        else:
            y = (y + shift(y, False)) % Y
        pairs.append((i, ((zl * Y + y) * ZH + zh) * C + c))
    return pairs


def first_step(value, k):
    shift = lambda place, on_z: {1: -1, 2: 2 - 4 * (place % 2) if on_z else -2, 3: 1}[k]
    return lax.ppermute(value, GATHER, moved(lambda c: c == 0, shift))


def second_step(value, shift):
    return lax.ppermute(value, GATHER, moved(lambda c: c == 1, shift))


def mixed(value, first):
    groups = []
    for c in range(C):
        for i in range(X):
            lines = [((i, j) if (c == 0) == first else (j, i)) for j in range(Y)]
            groups.append([(y * X + x) * C + c for y, x in lines])
    return lax.all_to_all(value, ("y", "x", "c"), 0, 0, axis_index_groups=groups, tiled=True)


def shards(tokens, norm_gain, key_cotangent, secondary, master, moment_first, moment_second, signs):
    tok_rows, width = tokens.shape
    keys_w = key_cotangent.shape[1]
    c = lax.axis_index("c")
    gain = norm_gain.reshape(1, width)
    node_rows = secondary.shape[0]

    half = lax.dynamic_slice_in_dim(secondary, c * (node_rows // 2), node_rows // 2, 0)
    column = jnp.concatenate([half] + [first_step(half, k) for k in range(1, Y)], axis=0)

    part = width // X
    step = 64
    by_rows = lambda cols: pl.BlockSpec((step, cols), lambda i: (i, 0))
    send, inv = pl.pallas_call(
        norm_kernel,
        out_shape=(pltpu.HBM((X, tok_rows, part + keys_w), BF16), pltpu.HBM((tok_rows, 128), F32)),
        grid=(tok_rows // step,),
        in_specs=[by_rows(width), pl.BlockSpec((1, width), lambda i: (0, 0)), by_rows(keys_w)],
        out_specs=(pl.BlockSpec((X, step, part + keys_w), lambda i: (0, i, 0)), by_rows(128)),
        cost_estimate=pl.CostEstimate(flops=tok_rows * width * 6, bytes_accessed=5 << 20, transcendentals=0),
        compiler_params=pltpu.CompilerParams(vmem_limit_bytes=24 << 20),
    )(*in_hbm(tokens, gain, key_cotangent))
    recv = mixed(send, True).reshape(X * tok_rows, part + keys_w)
    from_up = second_step(column, lambda place, on_z: -1)
    from_down = second_step(column, lambda place, on_z: 1)
    weights = []
    for block in (column, from_up, from_down):
        weights += [block, lax.ppermute(block, "c", ring(C, 1))]
    send = kernel_call(
        grad_kernel,
        pltpu.HBM((Y, part // Y, keys_w), BF16),
        0,
        1 << 20,
        1,
        24 << 20,
        HBM,
        (pltpu.VMEM((ZL, Y, ZH * C * ROWS, keys_w), BF16), pltpu.SemaphoreType.DMA((ZL,))),
    )(recv)
    blocks = mixed(send, False)
    own, sib = kernel_call(
        sum_kernel,
        (shape((part // Y // C, keys_w), F32), shape((part // Y // C, keys_w), BF16)),
        0,
        1 << 20,
        1,
    )(blocks)
    from_up, from_down = weights[2], weights[4]
    rows = from_up.shape[0] // 2
    far_a, far_b = kernel_call(
        halves_kernel,
        (pltpu.VMEM((rows, keys_w), BF16),) * 2,
        0,
        1 << 20,
        [HBM, HBM],
        24 << 20,
        scratch=(pltpu.SemaphoreType.DMA((2,)),),
    )(from_up, from_down)
    far = [
        second_step(far_a, lambda place, on_z: -1),
        second_step(far_b, lambda place, on_z: 1),
    ]
    sib, weights = lax.optimization_barrier((sib, weights))
    sib = lax.ppermute(sib, "c", ring(C, 1))
    summed = (own + sib.astype(F32)).astype(BF16)
    summed, far = lax.optimization_barrier((summed, far))
    for block in far:
        weights += [block, lax.ppermute(block, "c", ring(C, 1))]
    blocks = lax.all_to_all(summed.reshape(ZL * ZH, ROWS, keys_w), ("zl", "zh"), 0, 0, tiled=True)
    keys, mean = kernel_call(
        keys_kernel,
        (pltpu.HBM((tok_rows, keys_w), BF16), pltpu.HBM((tok_rows, 128), F32)),
        2 * tok_rows * width * keys_w,
        3 << 20,
        4 + len(weights),
    )(*in_hbm(tokens, gain, key_cotangent, inv), *in_vmem(*weights))
    blocks, keys, mean = lax.optimization_barrier((blocks, keys, mean))
    new_master, new_first, new_second, new_rows = kernel_call(
        functools.partial(adam_kernel, tok_rows * math.prod(SIZES)),
        (
            pltpu.HBM(master.shape, F32),
            pltpu.HBM(moment_first.shape, F32),
            pltpu.HBM(moment_second.shape, F32),
            pltpu.HBM((X * ZH, *master.shape), BF16),
        ),
        1 << 25,
        1 << 20,
        5,
    )(blocks, *in_hbm(moment_first, moment_second, master, signs.reshape(1, -1)))

    mine = lax.all_to_all(new_rows, ("x", "zh"), 0, 0, tiled=True)
    token_grad = kernel_call(
        token_grad_kernel,
        pltpu.HBM(tokens.shape, BF16),
        2 * tok_rows * width * keys_w,
        5 << 20,
        5 + len(weights),
    )(*in_hbm(tokens, gain, key_cotangent, inv, mean), *in_vmem(*weights))
    mine, token_grad = lax.optimization_barrier((mine, token_grad))
    other = lax.ppermute(mine, "c", ring(C, 1))
    even = jnp.where(c == 0, mine, other)
    odd = jnp.where(c == 0, other, mine)
    new_secondary = jnp.stack([even, odd], axis=1).reshape(node_rows, keys_w)
    return (keys, token_grad, new_master, new_first, new_second, new_secondary)


def solution(mesh):
    fine = Mesh(mesh.devices.reshape(SIZES), AXES)
    split = P(AXES, None)
    return jax.shard_map(
        shards,
        mesh=fine,
        in_specs=(split, P(), split, P(("zl", "y"), None), split, split, split, P()),
        out_specs=(split, split, split, split, split, P(("zl", "y"), None)),
        check_vma=False,
    )
```

```python
import functools
import math

import jax
import jax.numpy as jnp
from jax import lax
from jax.experimental import pallas as pl
from jax.experimental.pallas import tpu as pltpu
from jax.sharding import Mesh
from jax.sharding import PartitionSpec as P

PAIR_GAP = 16
norm_eps = 1e-05
adam_eps = 1e-08
beta_first = 0.9
beta_second = 0.95
adam_steps = 10
learn_rate = 0.002
weight_decay = 0.1

AXES = ("zl", "y", "x", "zh", "c")
SIZES = (4, 4, 4, 2, 2)
ZL, Y, X, ZH, C = SIZES
ROWS = 32
VMEM = pl.BlockSpec(memory_space=pltpu.VMEM)
HBM = pl.BlockSpec(memory_space=pltpu.HBM)
BF16 = jnp.bfloat16
F32 = jnp.float32


def shape(dims, kind):
    return jax.ShapeDtypeStruct(dims, kind)


def in_hbm(*values):
    return [pltpu.with_memory_space_constraint(value, pltpu.HBM) for value in values]


def in_vmem(*values):
    return [pltpu.with_memory_space_constraint(value, pltpu.VMEM) for value in values]


def kernel_call(body, outs, flops, nbytes, in_specs, limit=24 << 20, out_specs=None, scratch=()):
    return pl.pallas_call(
        body,
        out_shape=outs,
        in_specs=[VMEM] * in_specs if isinstance(in_specs, int) else in_specs,
        out_specs=jax.tree.map(lambda _: VMEM, outs) if out_specs is None else out_specs,
        scratch_shapes=list(scratch),
        cost_estimate=pl.CostEstimate(flops=flops, bytes_accessed=nbytes, transcendentals=0),
        compiler_params=pltpu.CompilerParams(vmem_limit_bytes=limit),
    )


def norm_kernel(tok_ref, gain_ref, cot_ref, send_ref, inv_ref):
    c = lax.axis_index("c")
    rows, width = tok_ref.shape
    step = X * ZH * C * ROWS
    acc = jnp.zeros((rows, step), F32)
    for k in range(width // step):
        t = tok_ref[:, k * step : (k + 1) * step].astype(F32)
        acc = acc + t * t
    inv = lax.rsqrt(jnp.sum(acc, axis=-1, keepdims=True) / width + norm_eps)
    inv = jnp.broadcast_to(inv, inv_ref.shape)
    inv_ref[...] = inv
    part = ZH * C * ROWS
    stride_p, stride_q = jnp.where(c == 0, part, step), jnp.where(c == 0, step, part)
    for zl in range(ZL):
        for p in range(X):
            for q in range(Y):
                at = pl.multiple_of(zl * Y * step + p * stride_p + q * stride_q, part)
                cols = pl.ds(at, part)
                normed = tok_ref[:, cols].astype(F32) * inv
                to = (zl * Y + q) * part
                send_ref[p, :, to : to + part] = (normed * gain_ref[:, cols]).astype(BF16)
    for p in range(X):
        send_ref[p, :, ZL * Y * part :] = cot_ref[...]


def grad_kernel(recv_ref, send_ref, buf_ref, sem):
    part = ZH * C * ROWS
    cols = ZL * Y * part
    cot = recv_ref[:, cols:]
    copies = []
    for zl in range(ZL):
        block = recv_ref[:, zl * Y * part : (zl + 1) * Y * part]
        grad = lax.dot_general(block, cot, (((0,), (0,)), ((), ())), preferred_element_type=F32)
        grad = grad.astype(BF16)
        for q in range(Y):
            for zh in range(ZH):
                for c in range(C):
                    at = q * part + (zh * C + c) * ROWS
                    to = (c * ZH + zh) * ROWS
                    buf_ref[zl, q, to : to + ROWS, :] = grad[at : at + ROWS]
        rows = slice(zl * part, (zl + 1) * part)
        copy = pltpu.make_async_copy(buf_ref.at[zl], send_ref.at[:, rows, :], sem.at[zl])
        copy.start()
        copies.append(copy)
    for copy in copies:
        copy.wait()


def sum_kernel(recv_ref, own_ref, sib_ref):
    c = lax.axis_index("c")
    rows = ZH * ROWS
    for ref, core in ((sib_ref, 1 - c), (own_ref, c)):
        for zl in range(ZL):
            at = pl.multiple_of(zl * C * rows + core * rows, rows)
            part = recv_ref[:, pl.ds(at, rows), :].astype(F32)
            ref[zl * rows : (zl + 1) * rows, :] = jnp.sum(part, axis=0).astype(ref.dtype)


def halves_kernel(up_ref, down_ref, a_ref, b_ref, sem):
    rows = a_ref.shape[0]
    copies = (
        pltpu.make_async_copy(up_ref.at[0:rows, :], a_ref, sem.at[0]),
        pltpu.make_async_copy(down_ref.at[rows : 2 * rows, :], b_ref, sem.at[1]),
    )
    for copy in copies:
        copy.start()
    for copy in copies:
        copy.wait()


def places(width, refs):
    c, zl, y = (lax.axis_index(name) for name in ("c", "zl", "y"))
    step = width // (ZL * Y)
    half = step // 2
    for i, ref in enumerate(refs):
        off = (0, 1, 3)[i // 2] if i < 6 else 2
        core = c if i % 2 == 0 else 1 - c
        for row in range(ref.shape[0] // half):
            k = row if i < 6 else row + 2 * ((i - 6) // 2)
            on_zl, on_y = jnp.where(core == 0, off, k), jnp.where(core == 0, k, off)
            node = lax.rem(zl + on_zl, ZL) * Y + lax.rem(y + on_y, Y)
            at = pl.multiple_of(node * step + core * half, half)
            yield pl.ds(at, half), ref[row * half : (row + 1) * half, :]


def widened(ref, cols):
    return jnp.concatenate([ref[...]] * (cols // ref.shape[1]), axis=1)


def keys_kernel(tok_ref, gain_ref, cot_ref, inv_ref, *refs):
    w_refs, (keys_ref, mean_ref) = refs[:-2], refs[-2:]
    width = tok_ref.shape[1]
    inv = widened(inv_ref, width // (ZL * Y * C))
    keys = jnp.zeros(keys_ref.shape, F32)
    for cols, weights in places(width, w_refs):
        normed = tok_ref[:, cols].astype(F32) * inv
        hidden = (normed * gain_ref[:, cols]).astype(BF16)
        keys = keys + jnp.dot(hidden, weights, preferred_element_type=F32)
    keys_ref[...] = keys.astype(BF16)
    mean = jnp.sum(cot_ref[...].astype(F32) * keys, axis=-1, keepdims=True) / width
    mean_ref[...] = jnp.broadcast_to(mean, mean_ref.shape)


def token_grad_kernel(tok_ref, gain_ref, cot_ref, inv_ref, mean_ref, *refs):
    w_refs, tg_ref = refs[:-1], refs[-1]
    width = tok_ref.shape[1]
    inv = widened(inv_ref, width // (ZL * Y * C))
    mean = widened(mean_ref, width // (ZL * Y * C))
    cot = cot_ref[...]
    for cols, weights in places(width, w_refs):
        hidden_grad = lax.dot_general(cot, weights, (((1,), (1,)), ((), ())), preferred_element_type=F32)
        normed = tok_ref[:, cols].astype(F32) * inv
        tg_ref[:, cols] = (inv * (hidden_grad * gain_ref[:, cols] - normed * mean)).astype(BF16)


def hadamard(value, extent=128):
    rows, width = value.shape
    i = lax.broadcasted_iota(jnp.int32, (extent, extent), 0)
    j = lax.broadcasted_iota(jnp.int32, (extent, extent), 1)
    both = i & j
    both = both ^ (both >> 4)
    both = both ^ (both >> 2)
    both = both ^ (both >> 1)
    table = (1 - 2 * (both & 1)).astype(F32).astype(BF16)
    parts = []
    for k in range(width // extent):
        rest = value[:, k * extent : (k + 1) * extent]
        for _ in range(3):
            top = rest.astype(BF16)
            parts.append(top)
            rest = rest - top.astype(F32)
    out = jnp.dot(jnp.concatenate(parts, axis=0), table, preferred_element_type=F32)
    p = []
    for k in range(width // extent):
        at = 3 * k * rows
        p.append((out[at + 2 * rows : at + 3 * rows] + out[at + rows : at + 2 * rows]) + out[at : at + rows])
    s, t, u, v = p[0] + p[1], p[0] - p[1], p[2] + p[3], p[2] - p[3]
    return jnp.concatenate([s + u, t + v, s - u, t - v], axis=1)


def adam_kernel(tokens_all, recv_ref, first_ref, second_ref, master_ref, signs_ref, nm_ref, nf_ref, ns_ref, new_ref):
    total = jnp.sum(recv_ref[...].astype(F32), axis=0)
    half = total.shape[1]
    root = math.sqrt(2 * half)
    sign = (1 - 2 * signs_ref[...]).astype(F32)
    sign0, sign1 = sign[:, :half], sign[:, half:]
    gap = PAIR_GAP
    spun = hadamard(jnp.concatenate([total[:gap] * sign0, total[gap:] * sign1], axis=0)) * (1.0 / (root * tokens_all))
    q0, q1 = spun[:gap], spun[gap:]
    coded = jnp.concatenate([q0 + q1, q0 - q1], axis=1)
    new_first = beta_first * first_ref[...] + (1.0 - beta_first) * coded
    new_second = beta_second * second_ref[...] + (1.0 - beta_second) * coded * coded
    nf_ref[...] = new_first
    ns_ref[...] = new_second
    first_hat = new_first / (1.0 - beta_first**adam_steps)
    second_hat = new_second / (1.0 - beta_second**adam_steps)
    ratio = first_hat / (jnp.sqrt(second_hat) + adam_eps)
    lower, upper = ratio[:, :half], ratio[:, half:]
    back = hadamard(jnp.concatenate([lower + upper, lower - upper], axis=0)) / root
    update = jnp.concatenate([back[:gap] * sign0, back[gap:] * sign1], axis=0)
    master = master_ref[...]
    new_master = master - learn_rate * (update + weight_decay * master)
    nm_ref[...] = new_master
    new_ref[...] = jnp.broadcast_to(new_master.astype(BF16), new_ref.shape)


def ring(n, s):
    return [(i, (i + s) % n) for i in range(n)]


GATHER = ("zl", "y", "zh", "c")


def moved(on_z, shift):
    pairs = []
    for i in range(ZL * Y * ZH * C):
        zl, y, zh, c = i // (Y * ZH * C), i // (ZH * C) % Y, i // C % ZH, i % C
        if on_z(c):
            z = (zh * ZL + zl + shift(zl, True)) % (ZH * ZL)
            zl, zh = z % ZL, z // ZL
        else:
            y = (y + shift(y, False)) % Y
        pairs.append((i, ((zl * Y + y) * ZH + zh) * C + c))
    return pairs


def first_step(value, k):
    shift = lambda place, on_z: {1: -1, 2: 2 - 4 * (place % 2) if on_z else -2, 3: 1}[k]
    return lax.ppermute(value, GATHER, moved(lambda c: c == 1, shift))


def second_step(value, shift):
    return lax.ppermute(value, GATHER, moved(lambda c: c == 0, shift))


def mixed(value, first):
    groups = []
    for c in range(C):
        for i in range(X):
            lines = [((i, j) if (c == 0) == first else (j, i)) for j in range(Y)]
            groups.append([(y * X + x) * C + c for y, x in lines])
    return lax.all_to_all(value, ("y", "x", "c"), 0, 0, axis_index_groups=groups, tiled=True)


def shards(tokens, norm_gain, key_cotangent, secondary, master, moment_first, moment_second, signs):
    tok_rows, width = tokens.shape
    keys_w = key_cotangent.shape[1]
    c = lax.axis_index("c")
    gain = norm_gain.reshape(1, width)
    node_rows = secondary.shape[0]

    half = lax.dynamic_slice_in_dim(secondary, c * (node_rows // 2), node_rows // 2, 0)
    column = jnp.concatenate([half] + [first_step(half, k) for k in range(1, Y)], axis=0)

    part = width // X
    step = 64
    by_rows = lambda cols: pl.BlockSpec((step, cols), lambda i: (i, 0))
    send, inv = pl.pallas_call(
        norm_kernel,
        out_shape=(pltpu.HBM((X, tok_rows, part + keys_w), BF16), pltpu.HBM((tok_rows, 128), F32)),
        grid=(tok_rows // step,),
        in_specs=[by_rows(width), pl.BlockSpec((1, width), lambda i: (0, 0)), by_rows(keys_w)],
        out_specs=(pl.BlockSpec((X, step, part + keys_w), lambda i: (0, i, 0)), by_rows(128)),
        cost_estimate=pl.CostEstimate(flops=tok_rows * width * 6, bytes_accessed=5 << 20, transcendentals=0),
        compiler_params=pltpu.CompilerParams(vmem_limit_bytes=24 << 20),
    )(*in_hbm(tokens, gain, key_cotangent))
    recv = mixed(send, True).reshape(X * tok_rows, part + keys_w)
    from_up = second_step(column, lambda place, on_z: -1)
    from_down = second_step(column, lambda place, on_z: 1)
    send = kernel_call(
        grad_kernel,
        pltpu.HBM((Y, part // Y, keys_w), BF16),
        0,
        1 << 20,
        1,
        24 << 20,
        HBM,
        (pltpu.VMEM((ZL, Y, ZH * C * ROWS, keys_w), BF16), pltpu.SemaphoreType.DMA((ZL,))),
    )(recv)
    blocks = mixed(send, False)
    own, sib = kernel_call(
        sum_kernel,
        (shape((part // Y // C, keys_w), F32), shape((part // Y // C, keys_w), BF16)),
        0,
        1 << 20,
        1,
    )(blocks)
    rows = from_up.shape[0] // 2
    far_a, far_b = kernel_call(
        halves_kernel,
        (pltpu.VMEM((rows, keys_w), BF16),) * 2,
        0,
        1 << 20,
        [HBM, HBM],
        24 << 20,
        scratch=(pltpu.SemaphoreType.DMA((2,)),),
    )(from_up, from_down)
    far = [
        second_step(far_a, lambda place, on_z: -1),
        second_step(far_b, lambda place, on_z: 1),
    ]
    column, from_up, from_down, far_a, far_b = lax.optimization_barrier((column, from_up, from_down, far_a, far_b))
    weights = []
    for block in (column, from_up, from_down):
        weights += [block, lax.ppermute(block, "c", ring(C, 1))]
    sib, far = lax.optimization_barrier((sib, far))
    sib = lax.ppermute(sib, "c", ring(C, 1))
    summed = (own + sib.astype(F32)).astype(BF16)
    summed, weights = lax.optimization_barrier((summed, weights))
    for block in far:
        weights += [block, lax.ppermute(block, "c", ring(C, 1))]
    blocks = lax.all_to_all(summed.reshape(ZL * ZH, ROWS, keys_w), ("zl", "zh"), 0, 0, tiled=True)
    keys, mean = kernel_call(
        keys_kernel,
        (pltpu.HBM((tok_rows, keys_w), BF16), pltpu.HBM((tok_rows, 128), F32)),
        2 * tok_rows * width * keys_w,
        3 << 20,
        4 + len(weights),
    )(*in_hbm(tokens, gain, key_cotangent, inv), *in_vmem(*weights))
    blocks, keys, mean = lax.optimization_barrier((blocks, keys, mean))
    new_master, new_first, new_second, new_rows = kernel_call(
        functools.partial(adam_kernel, tok_rows * math.prod(SIZES)),
        (
            pltpu.HBM(master.shape, F32),
            pltpu.HBM(moment_first.shape, F32),
            pltpu.HBM(moment_second.shape, F32),
            pltpu.HBM((X * ZH, *master.shape), BF16),
        ),
        1 << 25,
        1 << 20,
        5,
    )(blocks, *in_hbm(moment_first, moment_second, master, signs.reshape(1, -1)))

    mine = lax.all_to_all(new_rows, ("x", "zh"), 0, 0, tiled=True)
    token_grad = kernel_call(
        token_grad_kernel,
        pltpu.HBM(tokens.shape, BF16),
        2 * tok_rows * width * keys_w,
        5 << 20,
        5 + len(weights),
    )(*in_hbm(tokens, gain, key_cotangent, inv, mean), *in_vmem(*weights))
    mine, token_grad = lax.optimization_barrier((mine, token_grad))
    other = lax.ppermute(mine, "c", ring(C, 1))
    even = jnp.where(c == 0, mine, other)
    odd = jnp.where(c == 0, other, mine)
    new_secondary = jnp.stack([even, odd], axis=1).reshape(node_rows, keys_w)
    return (keys, token_grad, new_master, new_first, new_second, new_secondary)


def solution(mesh):
    fine = Mesh(mesh.devices.reshape(SIZES), AXES)
    split = P(AXES, None)
    return jax.shard_map(
        shards,
        mesh=fine,
        in_specs=(split, P(), split, P(("zl", "y"), None), split, split, split, P()),
        out_specs=(split, split, split, split, split, P(("zl", "y"), None)),
        check_vma=False,
    )
```
